32 devices in a mesh: dp: 2 (over x), seq: 4 (over z), tensor: 4 (over y, core).
Axes of the slice: x: 2, y: 2, z: 4, core: 2. Of those that a mesh axis runs over, the one named last changes fastest.
Arguments:
- tokens: bfloat16 [2, 4, 32, 196, 768], P(None, 'dp', 'seq', 'tensor'), may hold values from -6 to 6
- out_grad: bfloat16 [2, 4, 32, 196, 768], P(None, 'dp', 'seq', 'tensor'), may hold values from -6 to 6
- slot_window: int32 [2, 4, 32], P(None, 'dp', 'seq'), may hold values from 0 to 31, each once within a row
- first_gain: float32 [768], replicated, may hold values from 0.5 to 1.5
- first_shift: float32 [768], replicated, may hold values from -0.3 to 0.3
- triple_weight: bfloat16 [768, 2304], P('tensor'), may hold values from -0.21875 to 0.21875
- triple_bias: float32 [2304], replicated, may hold values from -0.3 to 0.3
- height_table: float32 [27, 64], replicated, may hold values from -0.2 to 0.2
- width_table: float32 [27, 64], replicated, may hold values from -0.2 to 0.2
- output_weight: bfloat16 [768, 768], P('tensor'), may hold values from -1.25 to 1.25
- output_bias: float32 [768], replicated, may hold values from -0.3 to 0.3
- second_gain: float32 [768], replicated, may hold values from 0.5 to 1.5
- second_shift: float32 [768], replicated, may hold values from -0.3 to 0.3
- expand_weight: bfloat16 [768, 3072], P('tensor'), may hold values from -0.21875 to 0.21875
- expand_bias: float32 [3072], replicated, may hold values from -0.3 to 0.3
- shrink_weight: bfloat16 [3072, 768], P('tensor'), may hold values from -0.109375 to 0.109375
- shrink_bias: float32 [768], replicated, may hold values from -0.3 to 0.3
Outputs:
- result: bfloat16 [2, 4, 32, 196, 768], P(None, 'dp', 'seq', 'tensor')
- tokens_gradient: bfloat16 [2, 4, 32, 196, 768], P(None, 'dp', 'seq', 'tensor')
- first_gain_gradient: float32 [768], replicated
- first_shift_gradient: float32 [768], replicated
- triple_weight_gradient: float32 [768, 2304], P('tensor')
- triple_bias_gradient: float32 [2304], replicated
- height_table_gradient: float32 [27, 64], replicated
- width_table_gradient: float32 [27, 64], replicated
- output_weight_gradient: float32 [768, 768], P('tensor')
- output_bias_gradient: float32 [768], replicated
- second_gain_gradient: float32 [768], replicated
- second_shift_gradient: float32 [768], replicated
- expand_weight_gradient: float32 [768, 3072], P('tensor')
- expand_bias_gradient: float32 [3072], replicated
- shrink_weight_gradient: float32 [3072, 768], P('tensor')
- shrink_bias_gradient: float32 [768], replicated
The draws below stay inside these ranges and needn't reach their ends.
Inputs may be any that keep to these rules, and one draw needn't show every extreme that they name: For each micro-batch and image, slot_window is a permutation of 0 to 31; a value w below 25 names the window in row w // 5 and column w % 5 of the grid padded to 70 tokens a side, larger values mark empty slots.
All inputs are finite; a program needn't handle non-finite values.
Results may differ from the reference program's by a relative error of at most 0.015.
Values may be sent and summed in bfloat16 or wider, within the bound.
No kernel may reach another device: no remote copies, remote signals or barrier semaphores. Data moves between devices by JAX's collectives and lax.ppermute only.
A program may use at most 320 MiB of HBM per device.

```python
from functools import partial
import jax
import jax.numpy as jnp
import numpy as np
from jax import lax

D = 768
HEADS = 12
HD = 64
FF = 3072
WIN = 14
GRID = 64
SLOTS = 32
MICRO = 2
WGRID = 5
WROWS = 196
REL = 27
IMAGES = 4


def level_of(stream_key, dims, shards, least, high):
    level, own = 1.0, jax.random.fold_in(stream_key, 6)
    for dim, shards_of in shards:
        steps = jnp.exp(jax.random.uniform(jax.random.fold_in(own, dim), (shards_of,), jnp.float32, least / len(shards), high / len(shards)))
        level = level * jnp.repeat(steps, dims[dim] // shards_of).reshape([-1 if axis == dim else 1 for axis in range(len(dims))])
    return level


def noise(stream_key, shape, width, most, split=(), held_as=jnp.bfloat16):
    level = level_of(stream_key, shape, split, -0.22, 0.18) if split else 1.0
    values = jax.random.normal(stream_key, shape, jnp.float32) * width * level
    return jnp.minimum(jnp.maximum(values, -most), most).astype(held_as)


def setup_inputs(seed: int = 0) -> dict:
    streams_of = jax.random.split(jax.random.key(seed), 18)
    tokens = noise(streams_of[0], (MICRO, IMAGES, SLOTS, WROWS, D), 1.0, 6.0, ((1, 2), (2, 4), (3, 4)))
    out_grad = noise(streams_of[1], (MICRO, IMAGES, SLOTS, WROWS, D), 1.0, 6.0, ((1, 2), (2, 4), (3, 4)))
    slot_window = jax.vmap(lambda own: jax.random.permutation(own, SLOTS))(jax.random.split(streams_of[2], MICRO * IMAGES)).reshape((MICRO, IMAGES, SLOTS)).astype(jnp.int32)
    first_gain = jnp.clip(1.0 + 0.1 * jax.random.normal(streams_of[3], (D,), jnp.float32), 0.5, 1.5)
    first_shift = jnp.clip(jax.random.uniform(streams_of[4], (D,), jnp.float32, -0.3, 0.3), -0.3, 0.3)
    triple_weight = noise(streams_of[5], (D, 3 * D), D ** -0.5, 0.21875, ((0, 4),))
    triple_bias = jnp.clip(jax.random.uniform(streams_of[6], (3 * D,), jnp.float32, -0.3, 0.3), -0.3, 0.3)
    height_table = jnp.clip(jax.random.uniform(streams_of[7], (REL, HD), jnp.float32, -0.2, 0.2), -0.2, 0.2)
    width_table = jnp.clip(jax.random.uniform(streams_of[8], (REL, HD), jnp.float32, -0.2, 0.2), -0.2, 0.2)
    output_weight = noise(streams_of[9], (D, D), (D // 32) ** -0.5, 1.25, ((0, 4),))
    output_bias = jnp.clip(jax.random.uniform(streams_of[10], (D,), jnp.float32, -0.3, 0.3), -0.3, 0.3)
    second_gain = jnp.clip(1.0 + 0.1 * jax.random.normal(streams_of[11], (D,), jnp.float32), 0.5, 1.5)
    second_shift = jnp.clip(jax.random.uniform(streams_of[12], (D,), jnp.float32, -0.3, 0.3), -0.3, 0.3)
    expand_weight = noise(streams_of[13], (D, FF), D ** -0.5, 0.21875, ((0, 4),))
    expand_bias = jnp.clip(jax.random.uniform(streams_of[14], (FF,), jnp.float32, -0.3, 0.3), -0.3, 0.3)
    shrink_weight = noise(streams_of[15], (FF, D), FF ** -0.5, 0.109375, ((0, 4),))
    shrink_bias = jnp.clip(jax.random.uniform(streams_of[16], (D,), jnp.float32, -0.3, 0.3), -0.3, 0.3)
    return {"tokens": tokens, "out_grad": out_grad, "slot_window": slot_window, "first_gain": first_gain, "first_shift": first_shift, "triple_weight": triple_weight, "triple_bias": triple_bias, "height_table": height_table, "width_table": width_table, "output_weight": output_weight, "output_bias": output_bias, "second_gain": second_gain, "second_shift": second_shift, "expand_weight": expand_weight, "expand_bias": expand_bias, "shrink_weight": shrink_weight, "shrink_bias": shrink_bias}


EPSILON = 1e-06
MASKED_SCORE = -1000000000.0
PRECISE = lax.Precision.HIGHEST

@jax.custom_vjp
def low(v):
    return lax.optimization_barrier(v.astype(jnp.bfloat16)).astype(jnp.float32)

@jax.custom_vjp
def low_back(v):
    return v

def low_keep(v):
    return (low(v), None)

def low_pass(kept, grad):
    return (grad,)

def back_keep(v):
    return (v, None)

def back_low(kept, grad):
    return (low(grad),)
low.defvjp(low_keep, low_pass)
low_back.defvjp(back_keep, back_low)

def layer_norm(values, gain, shift):
    centre = lax.optimization_barrier(jnp.mean(values, axis=-1, keepdims=True))
    spread = values - centre
    variance = lax.optimization_barrier(jnp.mean(spread * spread, axis=-1, keepdims=True))
    return spread * lax.rsqrt(variance + EPSILON) * gain + shift

def smooth_gate(values):
    return 0.5 * values * (1.0 + jax.scipy.special.erf(values * 0.7071067811865476))

def window_valid(slot_window, window, grid, across):
    position = jnp.arange(window * window, dtype=jnp.int32)
    window_id = slot_window[..., None]
    inside = (window_id < across * across) & (window_id // across * window + position // window < grid) & (window_id % across * window + position % window < grid)
    return jnp.where(inside, 1.0, 0.0).astype(jnp.float32)

def offset_table(window):
    first_index = np.arange(window)[:, None, None]
    second = np.arange(window)[None, :, None]
    offset = np.arange(2 * window - 1)[None, None, :]
    return jnp.asarray((first_index - second + window - 1 == offset).astype(np.float32))

def slot_attention(packed, height_full, width_full):
    slot_triple, slot_valid = packed
    query_rows = slot_triple[:, 0]
    key_rows = slot_triple[:, 1]
    value_rows = slot_triple[:, 2]
    raw_scores = jnp.einsum('qhc,khc->hqk', query_rows, key_rows, precision=PRECISE) * HD ** (-0.5)
    grid_query = query_rows.reshape(WIN, WIN, HEADS, HD)
    along_height = jnp.einsum('ijhc,ikc->hijk', grid_query, height_full, precision=PRECISE)
    along_width = jnp.einsum('ijhc,jlc->hijl', grid_query, width_full, precision=PRECISE)
    scores = raw_scores.reshape(HEADS, WIN, WIN, WIN, WIN) + along_height[..., :, None] + along_width[..., None, :]
    scores = low_back(scores.reshape(HEADS, WROWS, WROWS))
    masked = jnp.where(slot_valid[None, None, :] > 0, scores, MASKED_SCORE)
    maxima = lax.optimization_barrier(jnp.max(masked, axis=-1, keepdims=True))
    exponent = jnp.exp(masked - maxima)
    soft_weights = exponent / lax.optimization_barrier(jnp.sum(exponent, axis=-1, keepdims=True))
    mixed_rows = jnp.einsum('hqk,khc->qhc', low(soft_weights), value_rows, precision=PRECISE)
    return mixed_rows * slot_valid[:, None, None]

def image_forward(image, valid, params):
    first_gain, first_shift, triple_weight, triple_bias, height_table, width_table, output_weight, output_bias, second_gain, second_shift, expand_weight, expand_bias, shrink_weight, shrink_bias = params
    offsets = offset_table(WIN)
    height_full = jnp.einsum('ikr,rc->ikc', offsets, height_table, precision=PRECISE)
    width_full = jnp.einsum('ikr,rc->ikc', offsets, width_table, precision=PRECISE)
    row_values = image.reshape(SLOTS * WROWS, D)
    normed = low(layer_norm(row_values, first_gain, first_shift))
    triple = low_back(low(jnp.dot(normed, triple_weight, precision=PRECISE) + triple_bias))
    triple = triple.reshape(SLOTS, WROWS, 3, HEADS, HD)
    attend = jax.checkpoint(partial(slot_attention, height_full=height_full, width_full=width_full))
    mixed = lax.map(attend, (triple, valid))
    attended = low_back(low(mixed.reshape(SLOTS * WROWS, D)))
    branch = low_back(jnp.dot(attended, output_weight, precision=PRECISE) + output_bias)
    middle = row_values + branch
    normed2 = low(layer_norm(middle, second_gain, second_shift))
    hidden = low_back(jnp.dot(normed2, expand_weight, precision=PRECISE) + expand_bias)
    active = low(smooth_gate(hidden))
    return middle + low_back(jnp.dot(active, shrink_weight, precision=PRECISE) + shrink_bias)

def reference(tokens, out_grad, slot_window, first_gain, first_shift, triple_weight, triple_bias, height_table, width_table, output_weight, output_bias, second_gain, second_shift, expand_weight, expand_bias, shrink_weight, shrink_bias):
    params = tuple((item.astype(jnp.float32) for item in (first_gain, first_shift, triple_weight, triple_bias, height_table, width_table, output_weight, output_bias, second_gain, second_shift, expand_weight, expand_bias, shrink_weight, shrink_bias)))
    valid_all = window_valid(slot_window, WIN, GRID, WGRID).reshape(MICRO * IMAGES, SLOTS, WROWS)
    images_in = tokens.astype(jnp.float32).reshape(MICRO * IMAGES, SLOTS, WROWS, D)
    cotangents = out_grad.astype(jnp.float32).reshape(MICRO * IMAGES, SLOTS * WROWS, D)

    def one_image(totals, packed):
        image, cotangent, valid = packed

        def forward(image_in, params_in):
            return image_forward(image_in, valid, params_in)
        output_rows, pullback = jax.vjp(forward, image, params)
        image_grad, param_grads = pullback(cotangent * valid.reshape(SLOTS * WROWS, 1))
        totals = tuple((left + right for left, right in zip(totals, param_grads)))
        return (totals, (output_rows.astype(jnp.bfloat16), image_grad.astype(jnp.bfloat16)))
    start = tuple((jnp.zeros_like(item) for item in params))
    totals, (outputs, image_grads) = lax.scan(one_image, start, (images_in, cotangents, valid_all))
    result = outputs.reshape(MICRO, IMAGES, SLOTS, WROWS, D)
    tokens_gradient = image_grads.reshape(MICRO, IMAGES, SLOTS, WROWS, D)
    return (result, tokens_gradient, totals[0], totals[1], totals[2], totals[3], totals[4], totals[5], totals[6], totals[7], totals[8], totals[9], totals[10], totals[11], totals[12], totals[13])
```

```python
import functools

import jax
import jax.numpy as jnp
import numpy as np
from jax import lax
from jax.experimental import pallas as pl
from jax.experimental.pallas import tpu as pltpu
from jax.sharding import PartitionSpec as P

HEADS = 12
HD = 64
WIN = 14
GRID = 64
WGRID = 5
WROWS = WIN * WIN
ROWS = 200
QUAD = 4
LANES = 128
SEG = 32
EPSILON = 1e-06
PENALTY = -1e9

F32 = jnp.float32
BF16 = jnp.bfloat16
VMEM_LIMIT = 58 * 1024 * 1024


def dot(left, right):
    return lax.dot_general(left, right, (((1,), (0,)), ((), ())), preferred_element_type=F32)


def dot_t(left, right):
    return lax.dot_general(left, right, (((1,), (1,)), ((), ())), preferred_element_type=F32)


def dot_rows(left, right):
    return lax.dot_general(left, right, (((0,), (0,)), ((), ())), preferred_element_type=F32)


def key_selectors(mirrored):
    out = np.zeros((QUAD, ROWS, LANES), np.float32)
    for head in range(QUAD):
        for key in range(WROWS):
            high, wide = key // WIN, key % WIN
            if mirrored:
                high, wide = WIN - 1 - high, WIN - 1 - wide
            out[head, key, SEG * head + high] = 1.0
            out[head, key, SEG * head + 16 + wide] = 1.0
    return jnp.asarray(out, BF16)


def block_diagonal(table):
    padded = jnp.pad(table.T, ((0, 0), (0, SEG - table.shape[0])))
    rows = []
    for head in range(QUAD):
        rows.append(jnp.pad(padded, ((0, 0), (SEG * head, LANES - SEG * (head + 1)))))
    return jnp.concatenate(rows, axis=0)


def forward_tables(height_table, width_table):
    high = jnp.roll(block_diagonal(height_table[::-1]), 1 - WIN, axis=1)
    wide = jnp.roll(block_diagonal(width_table[::-1]), 17 - WIN, axis=1)
    return jnp.concatenate([high, wide], axis=1).astype(BF16)


def backward_tables(height_table, width_table):
    high = block_diagonal(height_table)
    wide = jnp.roll(block_diagonal(width_table), 16, axis=1)
    return jnp.concatenate([high, wide], axis=1).astype(BF16)


def table_gradients(summed, count):
    high = summed[:, :LANES]
    wide = jnp.roll(summed[:, LANES:], -16, axis=1)
    out = []
    for part in (high, wide):
        total = 0.0
        for head in range(QUAD):
            total = total + part[HD * head : HD * (head + 1), SEG * head : SEG * head + count]
        out.append(total.T)
    return out


def valid_rows(high_limit, wide_limit):
    row = lax.broadcasted_iota(jnp.int32, (ROWS, 1), 0)
    high = (row * 4682) >> 16
    wide = row - high * WIN
    return (high < high_limit) & (wide < wide_limit) & (row < WROWS)


def roll_rows(values, by_width):
    sub = lax.broadcasted_iota(jnp.int32, (8, LANES), 0)
    pieces = []
    for start in range(0, ROWS, 8):
        piece = values[start : start + 8]
        first = start // WIN
        crossing = (first + 1) * WIN - start
        shifts = (first, first + 1)
        if by_width:
            one = pltpu.roll(piece, start - first * WIN, 1, stride=1, stride_axis=0)
        else:
            one = pltpu.roll(piece, first, 1) if first else piece
        if crossing < 8:
            if by_width:
                two = pltpu.roll(piece, LANES - crossing, 1)
                two = pltpu.roll(two, 0, 1, stride=1, stride_axis=0)
            else:
                two = pltpu.roll(piece, shifts[1], 1)
            one = jnp.where(sub < crossing, one, two)
        pieces.append(one)
    return jnp.concatenate(pieces, axis=0)


def normalize(values):
    centre = jnp.mean(values, axis=-1, keepdims=True)
    spread = values - centre
    variance = jnp.mean(spread * spread, axis=-1, keepdims=True)
    scale = lax.rsqrt(variance + EPSILON)
    return spread * scale, scale


def normalize_back(unit, scale, grad, gain):
    scaled = grad * gain
    mean_grad = jnp.mean(scaled, axis=-1, keepdims=True)
    mean_both = jnp.mean(scaled * unit, axis=-1, keepdims=True)
    return (scaled - mean_grad - unit * mean_both) * scale


def load_shards(shards, order_ref, target, sems, columns=None):
    copies = []
    for index, shard in enumerate(shards):
        source = shard if columns is None else shard.at[:, columns]
        height = shard.shape[0]
        start = pl.multiple_of(order_ref[index] * height, 16)
        copies.append(
            pltpu.make_async_copy(source, target.at[pl.ds(start, height), :], sems.at[index])
        )
    for copy in copies:
        copy.start()
    for copy in copies:
        copy.wait()


def gather_quarters(block, target, slabs, fill_tail):
    parts, rows = block.shape[0], block.shape[2]
    for slab in range(slabs):
        for part in range(parts):
            target[slab, part * rows : (part + 1) * rows, :] = block[part, slab].astype(F32)
        if fill_tail:
            target[slab, parts * rows :, :] = jnp.zeros(
                (ROWS - parts * rows, target.shape[2]), F32
            )


def attend_kernel(
    slabs,
    lims,
    order,
    tokens,
    gain,
    shift,
    bias,
    tables,
    selectors,
    w0,
    w1,
    w2,
    w3,
    *rest,
):
    rows_out, normed_out, triple_out, probs_out, attended_out, full, weight, masked_keys, sems = (
        rest[-9:]
    )
    step = pl.program_id(0)

    @pl.when(step == 0)
    def _():
        load_shards((w0, w1, w2, w3), order, weight, sems)

    width = full.shape[2]
    gather_quarters(tokens, full, slabs, True)
    rows = full[...].reshape(slabs * ROWS, width)
    unit, _ = normalize(rows)
    normed = (unit * gain[...] + shift[...]).astype(BF16)
    rows_out[...] = rows.astype(BF16).reshape(slabs, ROWS, width)
    normed_out[...] = normed.reshape(slabs, ROWS, width)
    for part in range(3):
        columns = slice(part * width, (part + 1) * width)
        triple = dot(normed, weight[:, columns]) + bias[:, columns]
        triple_out[:, :, columns] = triple.astype(BF16).reshape(slabs, ROWS, width)

    lane = lax.broadcasted_iota(jnp.int32, (ROWS, LANES), 1)
    within = lane & (SEG - 1)
    upper = lane >= HD
    quads = HEADS // QUAD
    for slab in range(slabs):
        which = step * slabs + slab
        allowed = valid_rows(lims[which, 0], lims[which, 1])
        penalty = jnp.where((lane == WIN) & jnp.logical_not(allowed), PENALTY, 0.0).astype(BF16)
        for head in range(QUAD):
            masked_keys[slab, head] = selectors[head] + penalty

    def one_quad(index, carry):
        slab = index // quads
        quad = index - slab * quads
        which = step * slabs + slab
        allowed = valid_rows(lims[which, 0], lims[which, 1])
        base = pl.multiple_of(quad * QUAD * HD, LANES)
        queries = triple_out[slab, :, pl.ds(base, QUAD * HD)]
        keys = triple_out[slab, :, pl.ds(pl.multiple_of(base + width, LANES), QUAD * HD)]
        values = triple_out[slab, :, pl.ds(pl.multiple_of(base + 2 * width, LANES), QUAD * HD)]
        terms = dot(queries, tables[...])
        high = roll_rows(terms[:, :LANES], False)
        wide = roll_rows(terms[:, LANES:], True)
        constant = jnp.where(lane == WIN, 1.0, 0.0)
        relative = jnp.where(
            within < WIN, high, jnp.where((within >= 16) & (within < 16 + WIN), wide, constant)
        ).astype(BF16)
        queries = queries * jnp.asarray(HD**-0.5, BF16)
        outs = []
        for pair in range(QUAD // 2):
            columns = slice(pair * LANES, (pair + 1) * LANES)
            left = jnp.concatenate([queries[:, columns], relative], axis=1)
            total = None
            for side in range(2):
                head = 2 * pair + side
                mine = upper if side else jnp.logical_not(upper)
                zero = jnp.zeros((ROWS, LANES), BF16)
                right = jnp.concatenate(
                    [jnp.where(mine, keys[:, columns], zero), masked_keys[slab, head]], axis=1
                )
                scores = dot_t(left, right)
                maxima = jnp.max(scores, axis=-1, keepdims=True)
                exponent = jnp.exp(scores - maxima)
                summed = jnp.sum(exponent, axis=-1, keepdims=True)
                probs = (exponent * (1.0 / summed)).astype(BF16)
                probs_out[slab, quad * QUAD + head] = probs
                part = dot(probs, jnp.where(mine, values[:, columns], zero))
                total = part if total is None else total + part
            outs.append(total)
        mixed = jnp.concatenate(outs, axis=1)
        mixed = jnp.where(allowed, mixed, 0.0)
        attended_out[slab, :, pl.ds(base, QUAD * HD)] = mixed.astype(BF16)
        return carry

    lax.fori_loop(0, slabs * quads, one_quad, 0)


def attend(micro, slabs_all, lims, order, tokens, gain, shift, bias, tables, selectors, shards, kept):
    parts, slabs_here, rows_dev, width = tokens.shape
    slabs = 2 if slabs_here % 2 == 0 else 1
    steps = slabs_here // slabs
    here = micro * steps
    triple_width = shards[0].shape[1]
    block3 = lambda columns: pl.BlockSpec((slabs, ROWS, columns), lambda i, *_: (i + here, 0, 0))
    whole = lambda *shape: pl.BlockSpec(shape, lambda i, *_: (0,) * len(shape))
    anywhere = pl.BlockSpec(memory_space=pl.ANY)
    out_shape = (
        jax.ShapeDtypeStruct((slabs_all, ROWS, width), BF16),
        jax.ShapeDtypeStruct((slabs_all, ROWS, width), BF16),
        jax.ShapeDtypeStruct((slabs_all, ROWS, triple_width), BF16),
        jax.ShapeDtypeStruct((slabs_all, HEADS, ROWS, ROWS), BF16),
        jax.ShapeDtypeStruct((slabs_all, ROWS, width), BF16),
    )
    in_specs = [
        pl.BlockSpec((parts, slabs, rows_dev, width), lambda i, *_: (0, i, 0, 0)),
        whole(1, width),
        whole(1, width),
        whole(1, triple_width),
        whole(2 * LANES, 2 * LANES),
        whole(QUAD, ROWS, LANES),
    ] + [anywhere] * 4
    aliases = {}
    if kept is not None:
        aliases = {2 + len(in_specs) + n: n for n in range(len(kept))}
        in_specs = in_specs + [anywhere] * len(kept)
    rows = slabs_here * ROWS
    flops = 2 * rows * width * triple_width + slabs_here * HEADS * 2 * 2 * ROWS * ROWS * 256
    return pl.pallas_call(
        functools.partial(attend_kernel, slabs),
        out_shape=out_shape,
        grid_spec=pltpu.PrefetchScalarGridSpec(
            num_scalar_prefetch=2,
            grid=(steps,),
            in_specs=in_specs,
            out_specs=(
                block3(width),
                block3(width),
                block3(triple_width),
                pl.BlockSpec((slabs, HEADS, ROWS, ROWS), lambda i, *_: (i + here, 0, 0, 0)),
                block3(width),
            ),
            scratch_shapes=[
                pltpu.VMEM((slabs, ROWS, width), F32),
                pltpu.VMEM((width, triple_width), BF16),
                pltpu.VMEM((slabs, QUAD, ROWS, LANES), BF16),
                pltpu.SemaphoreType.DMA((4,)),
            ],
        ),
        input_output_aliases=aliases,
        compiler_params=pltpu.CompilerParams(vmem_limit_bytes=VMEM_LIMIT),
        cost_estimate=pl.CostEstimate(
            flops=flops,
            bytes_accessed=rows * (width * 8 + triple_width * 2 + HEADS * 512) + width * 4608,
            transcendentals=slabs_here * HEADS * ROWS * ROWS,
        ),
        name="attend",
    )(lims, order, tokens, gain, shift, bias, tables, selectors, *shards, *(kept or ()))


def project_kernel(
    slabs, lims, order, attended, rows_in, grads, bias, gain, shift, w0, w1, w2, w3,
    middle_out, normed_out, branch_out, shrink_bias_out, full, weight, sems,
):
    step = pl.program_id(0)

    @pl.when(step == 0)
    def _():
        load_shards((w0, w1, w2, w3), order, weight, sems)
        shrink_bias_out[...] = jnp.zeros_like(shrink_bias_out)

    width = full.shape[2]
    count = slabs * ROWS
    middle = (
        rows_in[...].reshape(count, width).astype(F32)
        + dot(attended[...].reshape(count, width), weight[...])
        + bias[...]
    )
    unit, _ = normalize(middle)
    middle_out[...] = middle.reshape(slabs, ROWS, width)
    normed_out[...] = (unit * gain[...] + shift[...]).astype(BF16).reshape(slabs, ROWS, width)
    gather_quarters(grads.at[0], full, slabs, True)
    for slab in range(slabs):
        which = step * slabs + slab
        allowed = valid_rows(lims[which, 0], lims[which, 1])
        branch = jnp.where(allowed, full[slab], 0.0)
        branch_out[slab] = branch.astype(BF16)
        shrink_bias_out[...] += jnp.sum(branch, axis=0, keepdims=True)


def project(lims, order, attended, rows_in, grads, bias, gain, shift, shards):
    slabs_all, _, width = attended.shape
    micros, parts, slabs_here, rows_dev, _ = grads.shape
    slabs = 2 if slabs_here % 2 == 0 else 1
    per = slabs_here // slabs
    block = pl.BlockSpec((slabs, ROWS, width), lambda i, *_: (i, 0, 0))
    vector = pl.BlockSpec((1, width), lambda i, *_: (0, 0))
    anywhere = pl.BlockSpec(memory_space=pl.ANY)
    rows = slabs_all * ROWS
    return pl.pallas_call(
        functools.partial(project_kernel, slabs),
        out_shape=(
            jax.ShapeDtypeStruct((slabs_all, ROWS, width), F32),
            jax.ShapeDtypeStruct((slabs_all, ROWS, width), BF16),
            jax.ShapeDtypeStruct((slabs_all, ROWS, width), BF16),
            jax.ShapeDtypeStruct((1, width), F32),
        ),
        grid_spec=pltpu.PrefetchScalarGridSpec(
            num_scalar_prefetch=2,
            grid=(micros * per,),
            in_specs=[
                block,
                block,
                pl.BlockSpec(
                    (1, parts, slabs, rows_dev, width), lambda i, *_: (i // per, 0, i % per, 0, 0)
                ),
                vector,
                vector,
                vector,
            ]
            + [anywhere] * 4,
            out_specs=(block, block, block, vector),
            scratch_shapes=[
                pltpu.VMEM((slabs, ROWS, width), F32),
                pltpu.VMEM((width, width), BF16),
                pltpu.SemaphoreType.DMA((4,)),
            ],
        ),
        compiler_params=pltpu.CompilerParams(vmem_limit_bytes=VMEM_LIMIT),
        cost_estimate=pl.CostEstimate(
            flops=2 * rows * width * width, bytes_accessed=rows * width * 14, transcendentals=0
        ),
        name="project",
    )(lims, order, attended, rows_in, grads, bias, gain, shift, *shards)


def gate_both(hidden):
    half = 0.5 * (1.0 + lax.erf(hidden * 0.7071067811865476))
    density = jnp.exp(hidden * hidden * -0.5) * 0.3989422804014327
    return hidden * half, half + hidden * density


def feed_kernel(
    relative, first, tile, lims, order, normed, branch, bias, shrink, e0, e1, e2, e3, *rest,
):
    if not first:
        out_in, grad_in = rest[:2]
    (out_acc, grad_acc, expand_grad, shrink_grad, bias_grad, expand, acc_e, acc_s, sems) = rest[-9:]
    step = pl.program_id(0)
    last = pl.num_programs(0) - 1
    chunk = shrink.shape[0]
    width = shrink.shape[1]

    @pl.when(step == 0)
    def _():
        start = pl.multiple_of(order[relative] * chunk, LANES)
        load_shards((e0, e1, e2, e3), order, expand, sems, pl.ds(start, chunk))
        acc_e[...] = jnp.zeros_like(acc_e)
        acc_s[...] = jnp.zeros_like(acc_s)
        bias_grad[...] = jnp.zeros_like(bias_grad)

    rows = normed[...]
    grads = branch[...]
    total_out = None
    total_grad = None
    for start in range(0, chunk, tile):
        columns = slice(start, start + tile)
        hidden = dot(rows, expand[:, columns]) + bias[0, :, columns]
        active, slope = gate_both(hidden)
        active = active.astype(BF16)
        part = dot(active, shrink[columns, :])
        total_out = part if total_out is None else total_out + part
        back = (dot_t(grads, shrink[columns, :]) * slope).astype(BF16)
        acc_s[columns, :] += dot_rows(active, grads)
        acc_e[:, columns] += dot_rows(rows, back)
        bias_grad[:, columns] += jnp.sum(back.astype(F32), axis=0, keepdims=True)
        part = dot_t(back, expand[:, columns])
        total_grad = part if total_grad is None else total_grad + part
    if first:
        out_acc[...] = total_out
        grad_acc[...] = total_grad
    else:
        out_acc[...] = out_in[...] + total_out
        grad_acc[...] = grad_in[...] + total_grad

    @pl.when(step == last)
    def _():
        shrink_grad[...] = acc_s[...].astype(BF16)
        parts, height = expand_grad.shape[0], expand_grad.shape[1]
        for part in range(parts):
            start = pl.multiple_of(order[part] * height, 16)
            expand_grad[part] = acc_e[pl.ds(start, height), :].astype(BF16)


def feed(relative, lims, order, normed, branch, bias, shrink, shards, kept):
    rows, width = normed.shape
    chunk = shrink.shape[0]
    parts = len(shards)
    height = shards[0].shape[0]
    block_rows = 2 * ROWS
    block = pl.BlockSpec((block_rows, width), lambda i, *_: (i, 0))
    anywhere = pl.BlockSpec(memory_space=pl.ANY)
    in_specs = [
        block,
        block,
        pl.BlockSpec((1, 1, chunk), lambda i, lims, order: (order[relative], 0, 0)),
        pl.BlockSpec((chunk, width), lambda i, *_: (0, 0)),
    ] + [anywhere] * parts
    aliases = {}
    if kept is not None:
        aliases = {2 + len(in_specs) + n: n for n in range(2)}
        in_specs = in_specs + [block, block]
    else:
        kept = ()
    return pl.pallas_call(
        functools.partial(feed_kernel, relative, not kept, 256),
        out_shape=(
            jax.ShapeDtypeStruct((rows, width), F32),
            jax.ShapeDtypeStruct((rows, width), F32),
            jax.ShapeDtypeStruct((parts, height, chunk), BF16),
            jax.ShapeDtypeStruct((chunk, width), BF16),
            jax.ShapeDtypeStruct((1, chunk), F32),
        ),
        grid_spec=pltpu.PrefetchScalarGridSpec(
            num_scalar_prefetch=2,
            grid=(rows // block_rows,),
            in_specs=in_specs,
            out_specs=(
                block,
                block,
                pl.BlockSpec((parts, height, chunk), lambda i, *_: (0, 0, 0)),
                pl.BlockSpec((chunk, width), lambda i, *_: (0, 0)),
                pl.BlockSpec((1, chunk), lambda i, *_: (0, 0)),
            ),
            scratch_shapes=[
                pltpu.VMEM((width, chunk), BF16),
                pltpu.VMEM((width, chunk), F32),
                pltpu.VMEM((chunk, width), F32),
                pltpu.SemaphoreType.DMA((parts,)),
            ],
        ),
        input_output_aliases=aliases,
        compiler_params=pltpu.CompilerParams(vmem_limit_bytes=VMEM_LIMIT),
        cost_estimate=pl.CostEstimate(
            flops=12 * rows * width * chunk,
            bytes_accessed=rows * width * 20 + width * chunk * 8,
            transcendentals=2 * rows * chunk,
        ),
        name="feed",
    )(lims, order, normed, branch, bias, shrink, *shards, *kept)


def middle_kernel(
    slabs, lims, order, middle, out_acc, grad_acc, branch, attended, bias, gain, w0, w1, w2, w3,
    result_out, d_middle_out, d_attended_out, weight_grad, output_bias_grad, gain_grad, shift_grad,
    full, weight, acc, sems,
):
    step = pl.program_id(0)
    last = pl.num_programs(0) - 1

    @pl.when(step == 0)
    def _():
        load_shards((w0, w1, w2, w3), order, weight, sems)
        acc[...] = jnp.zeros_like(acc)
        output_bias_grad[...] = jnp.zeros_like(output_bias_grad)
        gain_grad[...] = jnp.zeros_like(gain_grad)
        shift_grad[...] = jnp.zeros_like(shift_grad)

    width = full.shape[2]
    count = slabs * ROWS
    rows = middle[...].reshape(count, width)
    full[...] = (rows + out_acc[...] + bias[...]).reshape(slabs, ROWS, width)
    parts, rows_dev = result_out.shape[1], result_out.shape[3]
    for slab in range(slabs):
        for part in range(parts):
            result_out[0, part, slab] = full[
                slab, part * rows_dev : (part + 1) * rows_dev, :
            ].astype(BF16)
    unit, scale = normalize(rows)
    grad = grad_acc[...]
    gain_grad[...] += jnp.sum(grad * unit, axis=0, keepdims=True)
    shift_grad[...] += jnp.sum(grad, axis=0, keepdims=True)
    d_middle = branch[...].reshape(count, width).astype(F32) + normalize_back(
        unit, scale, grad, gain[...]
    )
    d_middle_out[...] = d_middle.reshape(slabs, ROWS, width)
    d_output = d_middle.astype(BF16)
    output_bias_grad[...] += jnp.sum(d_output.astype(F32), axis=0, keepdims=True)
    acc[...] += dot_rows(attended[...].reshape(count, width), d_output)
    d_attended = dot_t(d_output, weight[...]).astype(BF16)
    d_attended_out[...] = d_attended.reshape(slabs, ROWS, width)
    for slab in range(slabs):
        which = step * slabs + slab
        allowed = valid_rows(lims[which, 0], lims[which, 1])
        mine = d_attended_out[slab]
        d_attended_out[slab] = jnp.where(allowed, mine, jnp.zeros_like(mine))

    @pl.when(step == last)
    def _():
        height = weight_grad.shape[1]
        for part in range(weight_grad.shape[0]):
            start = pl.multiple_of(order[part] * height, 16)
            weight_grad[part] = acc[pl.ds(start, height), :].astype(BF16)


def middle_back(micros, parts, lims, order, middle, out_acc, grad_acc, branch, attended, bias, gain, shards):
    slabs_all, _, width = attended.shape
    slabs_here = slabs_all // micros
    rows_dev = WROWS // parts
    slabs = 2 if slabs_here % 2 == 0 else 1
    per = slabs_here // slabs
    height = shards[0].shape[0]
    block = pl.BlockSpec((slabs, ROWS, width), lambda i, *_: (i, 0, 0))
    flat = pl.BlockSpec((slabs * ROWS, width), lambda i, *_: (i, 0))
    vector = pl.BlockSpec((1, width), lambda i, *_: (0, 0))
    anywhere = pl.BlockSpec(memory_space=pl.ANY)
    rows = slabs_all * ROWS
    vec = jax.ShapeDtypeStruct((1, width), F32)
    return pl.pallas_call(
        functools.partial(middle_kernel, slabs),
        out_shape=(
            jax.ShapeDtypeStruct((micros, parts, slabs_here, rows_dev, width), BF16),
            jax.ShapeDtypeStruct((slabs_all, ROWS, width), F32),
            jax.ShapeDtypeStruct((slabs_all, ROWS, width), BF16),
            jax.ShapeDtypeStruct((len(shards), height, width), BF16),
            vec,
            vec,
            vec,
        ),
        grid_spec=pltpu.PrefetchScalarGridSpec(
            num_scalar_prefetch=2,
            grid=(micros * per,),
            in_specs=[block, flat, flat, block, block, vector, vector] + [anywhere] * len(shards),
            out_specs=(
                pl.BlockSpec(
                    (1, parts, slabs, rows_dev, width), lambda i, *_: (i // per, 0, i % per, 0, 0)
                ),
                block,
                block,
                pl.BlockSpec((len(shards), height, width), lambda i, *_: (0, 0, 0)),
                vector,
                vector,
                vector,
            ),
            scratch_shapes=[
                pltpu.VMEM((slabs, ROWS, width), F32),
                pltpu.VMEM((width, width), BF16),
                pltpu.VMEM((width, width), F32),
                pltpu.SemaphoreType.DMA((len(shards),)),
            ],
        ),
        compiler_params=pltpu.CompilerParams(vmem_limit_bytes=VMEM_LIMIT),
        cost_estimate=pl.CostEstimate(
            flops=4 * rows * width * width, bytes_accessed=rows * width * 24, transcendentals=0
        ),
        name="middle",
    )(lims, order, middle, out_acc, grad_acc, branch, attended, bias, gain, *shards)


def attend_back_kernel(
    slabs, order, normed, queries_in, keys_in, values_in, probs_in, d_mixed_in, mixed_in,
    tables, selectors, sums,
    d_queries, d_keys, d_values, weight_grad, bias_grad, table_grad, grads, acc,
):
    step = pl.program_id(0)
    last = pl.num_programs(0) - 1
    wide4 = QUAD * HD

    @pl.when(step == 0)
    def _():
        acc[...] = jnp.zeros_like(acc)
        bias_grad[...] = jnp.zeros_like(bias_grad)
        table_grad[...] = jnp.zeros_like(table_grad)

    lane = lax.broadcasted_iota(jnp.int32, (ROWS, LANES), 1)
    within = lane & (SEG - 1)
    upper = lane >= HD
    zero = jnp.zeros((ROWS, LANES), BF16)

    def one_slab(slab, carry):
        queries, keys, values = queries_in[slab], keys_in[slab], values_in[slab]
        d_mixed = d_mixed_in[slab]
        product = d_mixed.astype(F32) * mixed_in[slab].astype(F32)
        product_high = product.astype(BF16)
        product_low = (product - product_high.astype(F32)).astype(BF16)
        inner = dot(product_high, sums[...]) + dot(product_low, sums[...])
        inner_high = inner.astype(BF16)
        inner_low = (inner - inner_high.astype(F32)).astype(BF16)
        inner = jnp.where((lane & 1) == 0, inner_high, inner_low)
        d_relative = None
        dq, dk, dv = [], [], []
        for pair in range(QUAD // 2):
            columns = slice(pair * LANES, (pair + 1) * LANES)
            left = jnp.concatenate([d_mixed[:, columns], inner], axis=1)
            dq_pair = dk_pair = dv_pair = None
            for side in range(2):
                head = 2 * pair + side
                mine = upper if side else jnp.logical_not(upper)
                minus = jnp.where((lane == 2 * head) | (lane == 2 * head + 1), -1.0, 0.0)
                right = jnp.concatenate(
                    [jnp.where(mine, values[:, columns], zero), minus.astype(BF16)], axis=1
                )
                d_probs = dot_t(left, right)
                probs = probs_in[slab, head]
                d_scores = (probs.astype(F32) * d_probs).astype(BF16)
                back = dot(
                    d_scores,
                    jnp.concatenate(
                        [jnp.where(mine, keys[:, columns], zero), selectors[head]], axis=1
                    ),
                )
                part_k = dot_rows(d_scores, jnp.where(mine, queries[:, columns], zero))
                part_v = dot_rows(probs, jnp.where(mine, d_mixed[:, columns], zero))
                if dq_pair is None:
                    dq_pair, dk_pair, dv_pair = back[:, :LANES], part_k, part_v
                else:
                    dq_pair = dq_pair + back[:, :LANES]
                    dk_pair = dk_pair + part_k
                    dv_pair = dv_pair + part_v
                d_relative = back[:, LANES:] if d_relative is None else d_relative + back[:, LANES:]
            dq.append(dq_pair)
            dk.append(dk_pair)
            dv.append(dv_pair)
        high = roll_rows(jnp.where(within < WIN, d_relative, 0.0), False)
        wide = roll_rows(
            jnp.where((within >= 16) & (within < 16 + WIN), d_relative, 0.0), True
        )
        d_terms = jnp.concatenate([high, wide], axis=1).astype(BF16)
        scale = HD**-0.5
        dq = jnp.concatenate(dq, axis=1) * scale + dot_t(d_terms, tables[...])
        table_grad[...] += dot_rows(queries, d_terms)
        dq = dq.astype(BF16)
        dk = (jnp.concatenate(dk, axis=1) * scale).astype(BF16)
        dv = jnp.concatenate(dv, axis=1).astype(BF16)
        d_queries[slab] = dq
        d_keys[slab] = dk
        d_values[slab] = dv
        grads[slab] = jnp.concatenate([dq, dk, dv], axis=1)
        return carry

    lax.fori_loop(0, slabs, one_slab, 0)
    width = normed.shape[2]
    both = grads[...].reshape(slabs * ROWS, 3 * wide4)
    bias_grad[...] += jnp.sum(both.astype(F32), axis=0, keepdims=True)
    acc[...] += dot_rows(normed[...].reshape(slabs * ROWS, width), both)

    @pl.when(step == last)
    def _():
        height = weight_grad.shape[1]
        for part in range(weight_grad.shape[0]):
            start = pl.multiple_of(order[part] * height, 16)
            weight_grad[part] = acc[pl.ds(start, height), :].astype(BF16)


def attend_back(quad, parts, order, normed, triple, probs, d_mixed, mixed, tables, selectors, sums):
    slabs_all, _, width = normed.shape
    slabs = 2 if slabs_all % 2 == 0 else 1
    wide4 = QUAD * HD
    quads = HEADS // QUAD
    column = lambda where: pl.BlockSpec((slabs, ROWS, wide4), lambda i, *_: (i, 0, where))
    whole = lambda *shape: pl.BlockSpec(shape, lambda i, *_: (0,) * len(shape))
    narrow = jax.ShapeDtypeStruct((slabs_all, ROWS, wide4), BF16)
    out_block = pl.BlockSpec((slabs, ROWS, wide4), lambda i, *_: (i, 0, 0))
    rows = slabs_all * ROWS
    return pl.pallas_call(
        functools.partial(attend_back_kernel, slabs),
        out_shape=(
            narrow,
            narrow,
            narrow,
            jax.ShapeDtypeStruct((parts, width // parts, 3 * wide4), BF16),
            jax.ShapeDtypeStruct((1, 3 * wide4), F32),
            jax.ShapeDtypeStruct((wide4, 2 * LANES), F32),
        ),
        grid_spec=pltpu.PrefetchScalarGridSpec(
            num_scalar_prefetch=1,
            grid=(slabs_all // slabs,),
            in_specs=[
                pl.BlockSpec((slabs, ROWS, width), lambda i, *_: (i, 0, 0)),
                column(quad),
                column(quads + quad),
                column(2 * quads + quad),
                pl.BlockSpec((slabs, QUAD, ROWS, ROWS), lambda i, *_: (i, quad, 0, 0)),
                column(quad),
                column(quad),
                whole(wide4, 2 * LANES),
                whole(QUAD, ROWS, LANES),
                whole(wide4, LANES),
            ],
            out_specs=(
                out_block,
                out_block,
                out_block,
                whole(parts, width // parts, 3 * wide4),
                whole(1, 3 * wide4),
                whole(wide4, 2 * LANES),
            ),
            scratch_shapes=[
                pltpu.VMEM((slabs, ROWS, 3 * wide4), BF16),
                pltpu.VMEM((width, 3 * wide4), F32),
            ],
        ),
        compiler_params=pltpu.CompilerParams(vmem_limit_bytes=VMEM_LIMIT),
        cost_estimate=pl.CostEstimate(
            flops=2 * rows * width * 3 * wide4 + slabs_all * QUAD * 2 * 4 * ROWS * ROWS * 256,
            bytes_accessed=rows * (width * 2 + wide4 * 16 + QUAD * 512),
            transcendentals=0,
        ),
        name="attend_back",
    )(order, normed, triple, triple, triple, probs, d_mixed, mixed, tables, selectors, sums)


def first_kernel(slabs, order, rows_in, d_middle, gain, *rest):
    grads, (w0, w1, w2, w3) = rest[:9], rest[9:13]
    out, gain_grad, shift_grad, full, weight, sems = rest[13:]
    step = pl.program_id(0)

    @pl.when(step == 0)
    def _():
        load_shards((w0, w1, w2, w3), order, weight, sems)
        gain_grad[...] = jnp.zeros_like(gain_grad)
        shift_grad[...] = jnp.zeros_like(shift_grad)

    width = full.shape[2]
    count = slabs * ROWS
    total = None
    wide4 = QUAD * HD
    for index, grad in enumerate(grads):
        part = dot_t(
            grad[...].reshape(count, wide4), weight[:, index * wide4 : (index + 1) * wide4]
        )
        total = part if total is None else total + part
    unit, scale = normalize(rows_in[...].reshape(count, width).astype(F32))
    gain_grad[...] += jnp.sum(total * unit, axis=0, keepdims=True)
    shift_grad[...] += jnp.sum(total, axis=0, keepdims=True)
    back = normalize_back(unit, scale, total, gain[...])
    full[...] = d_middle[...] + back.reshape(slabs, ROWS, width)
    parts, rows_dev = out.shape[0], out.shape[2]
    for slab in range(slabs):
        for part in range(parts):
            out[part, slab] = full[slab, part * rows_dev : (part + 1) * rows_dev, :].astype(BF16)


def first_back(micro, micros, parts, order, rows_in, d_middle, gain, grads, shards):
    slabs_all, _, width = rows_in.shape
    slabs_here = slabs_all // micros
    slabs = 2 if slabs_here % 2 == 0 else 1
    steps = slabs_here // slabs
    here = micro * steps
    rows_dev = WROWS // parts
    wide4 = QUAD * HD
    block = pl.BlockSpec((slabs, ROWS, width), lambda i, *_: (i + here, 0, 0))
    narrow = pl.BlockSpec((slabs, ROWS, wide4), lambda i, *_: (i + here, 0, 0))
    vector = pl.BlockSpec((1, width), lambda i, *_: (0, 0))
    anywhere = pl.BlockSpec(memory_space=pl.ANY)
    rows = slabs_here * ROWS
    return pl.pallas_call(
        functools.partial(first_kernel, slabs),
        out_shape=(
            jax.ShapeDtypeStruct((parts, slabs_here, rows_dev, width), BF16),
            jax.ShapeDtypeStruct((1, width), F32),
            jax.ShapeDtypeStruct((1, width), F32),
        ),
        grid_spec=pltpu.PrefetchScalarGridSpec(
            num_scalar_prefetch=1,
            grid=(steps,),
            in_specs=[block, block, vector] + [narrow] * len(grads) + [anywhere] * len(shards),
            out_specs=(
                pl.BlockSpec((parts, slabs, rows_dev, width), lambda i, *_: (0, i, 0, 0)),
                vector,
                vector,
            ),
            scratch_shapes=[
                pltpu.VMEM((slabs, ROWS, width), F32),
                pltpu.VMEM((width, 3 * width), BF16),
                pltpu.SemaphoreType.DMA((len(shards),)),
            ],
        ),
        compiler_params=pltpu.CompilerParams(vmem_limit_bytes=VMEM_LIMIT),
        cost_estimate=pl.CostEstimate(
            flops=6 * rows * width * width, bytes_accessed=rows * width * 14, transcendentals=0
        ),
        name="first_back",
    )(order, rows_in, d_middle, gain, *grads, *shards)


def exchange(values, bit):
    count = lax.axis_size("tensor")
    return lax.ppermute(values, "tensor", [(n, n ^ bit) for n in range(count)])


def gather_shards(shard):
    far = exchange(shard, 2)
    near = exchange(shard, 1)
    return (shard, near, far, exchange(far, 1))


def swap_windows(values, axis):
    return lax.all_to_all(values, "tensor", split_axis=axis, concat_axis=axis, tiled=True)


def reduce_group(pieces):
    mine = lax.axis_index("tensor")
    out = []
    for piece in pieces:
        ordered = jnp.take(piece, jnp.arange(piece.shape[0]) ^ mine, axis=0)
        share = lax.psum_scatter(ordered, "tensor", scatter_dimension=0, tiled=True)
        share = share.reshape(piece.shape[1:])
        part = lax.psum_scatter(share, ("dp", "seq"), scatter_dimension=0, tiled=True)
        out.append(lax.all_gather(part, ("dp", "seq"), axis=0, tiled=True))
    return out


def local(
    tokens,
    out_grad,
    slot_window,
    first_gain,
    first_shift,
    triple_weight,
    triple_bias,
    height_table,
    width_table,
    output_weight,
    output_bias,
    second_gain,
    second_shift,
    expand_weight,
    expand_bias,
    shrink_weight,
    shrink_bias,
):
    micros, images, slots, rows_dev, width = tokens.shape
    parts = lax.axis_size("tensor")
    mine = lax.axis_index("tensor")
    slabs_here = images * slots // parts
    slabs_all = micros * slabs_here
    rows = slabs_all * ROWS
    order = mine ^ jnp.arange(parts, dtype=jnp.int32)
    vector = lambda item: item.reshape(1, -1)

    windows = slot_window.reshape(micros, parts, slabs_here)
    windows = lax.dynamic_index_in_dim(windows, mine, axis=1, keepdims=False).reshape(-1)
    limits = jnp.stack([GRID - windows // WGRID * WIN, GRID - windows % WGRID * WIN], axis=1)
    limits = jnp.where((windows < WGRID * WGRID)[:, None], limits, 0).astype(jnp.int32)

    rows_in = [
        swap_windows(tokens[m].reshape(parts, slabs_here, rows_dev, width), 0)
        for m in range(micros)
    ]
    triple_shards = gather_shards(triple_weight)
    output_shards = gather_shards(output_weight)
    expand_shards = gather_shards(expand_weight)
    shrink_shards = gather_shards(shrink_weight)
    grads_in = swap_windows(out_grad.reshape(micros, parts, slabs_here, rows_dev, width), 1)

    ahead = forward_tables(height_table, width_table)
    behind = backward_tables(height_table, width_table)
    selectors = key_selectors(False)
    mirrored = key_selectors(True)
    sums = np.zeros((QUAD * HD, LANES), np.float32)
    for head in range(QUAD):
        sums[head * HD : (head + 1) * HD, 2 * head : 2 * head + 2] = 1.0
    sums = jnp.asarray(sums, BF16)

    kept = None
    for m in range(micros):
        kept = attend(
            m, slabs_all, limits[m * slabs_here : (m + 1) * slabs_here], order, rows_in[m],
            vector(first_gain), vector(first_shift), vector(triple_bias), ahead, selectors,
            triple_shards, kept,
        )
    full_rows, normed, triple, probs, attended = kept

    middle, normed2, branch, shrink_bias_grad = project(
        limits, order, attended, full_rows, grads_in, vector(output_bias), vector(second_gain),
        vector(second_shift), output_shards,
    )
    flat_normed2 = normed2.reshape(rows, width)
    flat_branch = branch.reshape(rows, width)
    bias_chunks = expand_bias.reshape(parts, 1, -1)
    sums_kept = None
    expand_grads, shrink_grads, expand_bias_grads = [], [], []
    for relative in range(parts):
        out_acc, grad_acc, expand_grad, shrink_grad, bias_grad = feed(
            relative, limits, order, flat_normed2, flat_branch, bias_chunks,
            shrink_shards[relative], expand_shards, sums_kept,
        )
        sums_kept = (out_acc, grad_acc)
        expand_grads.append(expand_grad)
        shrink_grads.append(shrink_grad)
        expand_bias_grads.append(bias_grad)

    result, d_middle, d_attended, output_grad, output_bias_grad, gain2_grad, shift2_grad = (
        middle_back(
            micros, parts, limits, order, middle, out_acc, grad_acc, branch, attended,
            vector(shrink_bias), vector(second_gain), output_shards,
        )
    )
    result = swap_windows(result, 1).reshape(tokens.shape)

    expand_grads = jnp.take(jnp.stack(expand_grads), order, axis=0)
    expand_grads = jnp.moveaxis(expand_grads, 0, 2).reshape(parts, width // parts, -1)
    shrink_grads = jnp.stack(shrink_grads)

    quad_grads, triple_grads, triple_bias_grads, table_sum = [], [], [], 0.0
    for quad in range(HEADS // QUAD):
        dq, dk, dv, weight_grad, bias_grad, table_grad = attend_back(
            quad, parts, order, normed, triple, probs, d_attended, attended, behind, mirrored, sums
        )
        quad_grads.append((dq, dk, dv))
        triple_grads.append(weight_grad)
        triple_bias_grads.append(bias_grad)
        table_sum = table_sum + table_grad
    wide4 = QUAD * HD
    grads9 = [quad_grads[quad][part] for part in range(3) for quad in range(HEADS // QUAD)]
    by_part = lambda items: jnp.concatenate(
        [
            item[..., part * wide4 : (part + 1) * wide4]
            for part in range(3)
            for item in items
        ],
        axis=-1,
    )
    triple_grads = by_part(triple_grads)
    triple_bias_grad = by_part(triple_bias_grads)

    token_grads, gain1_grad, shift1_grad = [], 0.0, 0.0
    for m in range(micros):
        token_grad, gain_grad, shift_grad = first_back(
            m, micros, parts, order, full_rows, d_middle, vector(first_gain), grads9, triple_shards
        )
        token_grads.append(swap_windows(token_grad, 0))
        gain1_grad = gain1_grad + gain_grad
        shift1_grad = shift1_grad + shift_grad
    tokens_gradient = jnp.stack(token_grads).reshape(tokens.shape)

    shrink_gradient, expand_gradient, output_gradient, triple_gradient = (
        item.astype(F32)
        for item in reduce_group((shrink_grads, expand_grads, output_grad, triple_grads))
    )
    expand_bias_grad = jnp.take(
        jnp.stack(expand_bias_grads).reshape(parts, -1), order, axis=0
    ).reshape(1, -1)
    height_grad, width_grad = table_gradients(table_sum, height_table.shape[0])
    small = [
        gain1_grad, shift1_grad, triple_bias_grad, height_grad, width_grad, output_bias_grad,
        gain2_grad, shift2_grad, expand_bias_grad, shrink_bias_grad,
    ]
    packed = jnp.concatenate([item.reshape(-1) for item in small])
    packed = lax.psum(packed, ("dp", "seq", "tensor"))
    outs, start = [], 0
    for item, like in zip(
        small,
        (
            first_gain, first_shift, triple_bias, height_table, width_table, output_bias,
            second_gain, second_shift, expand_bias, shrink_bias,
        ),
    ):
        outs.append(packed[start : start + item.size].reshape(like.shape))
        start += item.size
    return (
        result,
        tokens_gradient,
        outs[0],
        outs[1],
        triple_gradient,
        outs[2],
        outs[3],
        outs[4],
        output_gradient,
        outs[5],
        outs[6],
        outs[7],
        expand_gradient,
        outs[8],
        shrink_gradient,
        outs[9],
    )


def solution(mesh):
    split = P(None, "dp", "seq", "tensor", None)
    rows = P("tensor", None)
    return jax.shard_map(
        local,
        mesh=mesh,
        in_specs=(
            split, split, P(None, "dp", "seq"), P(), P(), rows, P(), P(), P(), rows, P(), P(), P(),
            rows, P(), rows, P(),
        ),
        out_specs=(
            split, split, P(), P(), rows, P(), P(), P(), rows, P(), P(), P(), rows, P(), rows, P(),
        ),
        check_vma=False,
    )
```

```python
import functools

import jax
import jax.numpy as jnp
import numpy as np
from jax import lax
from jax.experimental import pallas as pl
from jax.experimental.pallas import tpu as pltpu
from jax.sharding import PartitionSpec as P

HEADS = 12
HD = 64
WIN = 14
GRID = 64
WGRID = 5
WROWS = WIN * WIN
ROWS = 200
QUAD = 4
LANES = 128
REL = 2 * WIN - 1
SEG = 32
EPSILON = 1e-06
PENALTY = -1e9

F32 = jnp.float32
BF16 = jnp.bfloat16
FIRST_GAIN, FIRST_SHIFT, OUTPUT_BIAS, SECOND_GAIN, SECOND_SHIFT, SHRINK_BIAS = range(6)
TRIPLE_BIAS, EXPAND_BIAS, TABLES = 6, 9, 13
VMEM_LIMIT = 58 * 1024 * 1024


def dot(left, right):
    return lax.dot_general(left, right, (((1,), (0,)), ((), ())), preferred_element_type=F32)


def dot_t(left, right):
    return lax.dot_general(left, right, (((1,), (1,)), ((), ())), preferred_element_type=F32)


def dot_rows(left, right):
    return lax.dot_general(left, right, (((0,), (0,)), ((), ())), preferred_element_type=F32)


def key_selectors(mirrored):
    out = np.zeros((QUAD, ROWS, LANES), np.float32)
    for head in range(QUAD):
        for key in range(WROWS):
            high, wide = key // WIN, key % WIN
            if mirrored:
                high, wide = WIN - 1 - high, WIN - 1 - wide
            out[head, key, SEG * head + high] = 1.0
            out[head, key, SEG * head + 16 + wide] = 1.0
    return jnp.asarray(out, BF16)


def table_places(mirrored):
    out = np.zeros((2, REL, 2 * LANES), np.float32)
    for head in range(QUAD):
        for row in range(REL):
            if mirrored:
                out[0, row, SEG * head + row] = 1.0
                out[1, row, LANES + (SEG * head + 16 + row) % LANES] = 1.0
            else:
                out[0, REL - 1 - row, (SEG * head + row - 13) % LANES] = 1.0
                out[1, REL - 1 - row, LANES + (SEG * head + row + 3) % LANES] = 1.0
    return jnp.asarray(out, BF16)


def head_blocks(mirrored):
    out = np.zeros((QUAD * HD, 2 * LANES), np.float32)
    for head in range(QUAD):
        rows = slice(head * HD, (head + 1) * HD)
        for row in range(REL):
            if mirrored:
                out[rows, SEG * head + row] = 1.0
                out[rows, LANES + (SEG * head + 16 + row) % LANES] = 1.0
            else:
                out[rows, (SEG * head + row - 13) % LANES] = 1.0
                out[rows, LANES + (SEG * head + row + 3) % LANES] = 1.0
    return jnp.asarray(out, BF16)


def valid_rows(window):
    high_place = (window * 13) >> 6
    wide_place = window - high_place * WGRID
    inside = window < WGRID * WGRID
    row = lax.broadcasted_iota(jnp.int32, (ROWS, 1), 0)
    high = (row * 4682) >> 16
    wide = row - high * WIN
    high_limit = jnp.where(inside, GRID - high_place * WIN, 0)
    return (high < high_limit) & (wide < GRID - wide_place * WIN) & (row < WROWS)


def build_tables(height, width, places, blocks):
    both = dot_rows(height[...].astype(BF16), places[0]) + dot_rows(
        width[...].astype(BF16), places[1]
    )
    both = both.astype(BF16)
    return jnp.concatenate([both] * QUAD, axis=0) * blocks[...]


def roll_rows(values, by_width):
    sub = lax.broadcasted_iota(jnp.int32, (8, LANES), 0)
    pieces = []
    for start in range(0, ROWS, 8):
        piece = values[start : start + 8]
        first = start // WIN
        crossing = (first + 1) * WIN - start
        shifts = (first, first + 1)
        if by_width:
            one = pltpu.roll(piece, start - first * WIN, 1, stride=1, stride_axis=0)
        else:
            one = pltpu.roll(piece, first, 1) if first else piece
        if crossing < 8:
            if by_width:
                two = pltpu.roll(piece, LANES - crossing, 1)
                two = pltpu.roll(two, 0, 1, stride=1, stride_axis=0)
            else:
                two = pltpu.roll(piece, shifts[1], 1)
            one = jnp.where(sub < crossing, one, two)
        pieces.append(one)
    return jnp.concatenate(pieces, axis=0)


def normalize(values):
    centre = jnp.mean(values, axis=-1, keepdims=True)
    spread = values - centre
    variance = jnp.mean(spread * spread, axis=-1, keepdims=True)
    scale = lax.rsqrt(variance + EPSILON)
    return spread * scale, scale


def normalize_back(unit, scale, grad, gain):
    scaled = grad * gain
    mean_grad = jnp.mean(scaled, axis=-1, keepdims=True)
    mean_both = jnp.mean(scaled * unit, axis=-1, keepdims=True)
    return (scaled - mean_grad - unit * mean_both) * scale


def weight_places(meta, pieces):
    own, near, far0, far1, cross0, cross1 = pieces
    mine, bit = meta[0], meta[1]
    return [
        (own, 0, 2 * mine),
        (own, 1, 2 * mine + 1),
        (near, 0, 2 * (mine ^ 1)),
        (near, 1, 2 * (mine ^ 1) + 1),
        (far0, None, 2 * (mine ^ 2) + bit),
        (far1, None, 2 * (mine ^ 2) + 1 - bit),
        (cross0, None, 2 * (mine ^ 3) + bit),
        (cross1, None, 2 * (mine ^ 3) + 1 - bit),
    ]


def start_copies(pairs, sems):
    copies = []
    for number, (source, target) in enumerate(pairs):
        copies.append(pltpu.make_async_copy(source, target, sems.at[number]))
    for copy in copies:
        copy.start()
    return copies


def wait_all(copies):
    for copy in copies:
        copy.wait()


def load_rows(meta, pieces, target, sems, first=0):
    height = target.shape[0] // 8
    pairs = []
    for source, half, place in weight_places(meta, pieces):
        source = source if half is None else source.at[half]
        start = pl.multiple_of(place * height, 16)
        pairs.append(
            (source.at[pl.ds(first, height), :], target.at[pl.ds(start, height), :])
        )
    return start_copies(pairs, sems)


def gather_quarters(first, block, staged, target, base, slabs):
    parts, rows, slots, width = block.shape
    lanes = width // LANES

    @pl.when(first)
    def _():
        for part in range(parts):
            values = block[part].astype(F32).reshape(rows * slots, width)
            for piece in range(lanes):
                staged[part * lanes + piece] = values[:, piece * LANES : (piece + 1) * LANES]
        target[:, parts * rows :, :] = jnp.zeros((slabs, ROWS - parts * rows, width), F32)

    for slab in range(slabs):
        for part in range(parts):
            for piece in range(lanes):
                target[
                    slab, part * rows : (part + 1) * rows, piece * LANES : (piece + 1) * LANES
                ] = staged[part * lanes + piece, pl.ds(base + slab, rows, stride=slots), :]


def scatter_quarters(last, full, staged, block, base, slabs):
    parts, rows, slots, width = block.shape
    lanes = width // LANES
    for slab in range(slabs):
        for part in range(parts):
            for piece in range(lanes):
                staged[part * lanes + piece, pl.ds(base + slab, rows, stride=slots), :] = full[
                    slab, part * rows : (part + 1) * rows, piece * LANES : (piece + 1) * LANES
                ]

    @pl.when(last)
    def _():
        for part in range(parts):
            for piece in range(lanes):
                values = staged[part * lanes + piece].reshape(rows, slots, LANES)
                block[part, :, :, piece * LANES : (piece + 1) * LANES] = values.astype(BF16)


def write_owned(source, meta, keep, send):
    height = keep.shape[1]
    for index in range(4):
        start = pl.multiple_of((meta[0] ^ index) * height, 16)
        target = send if index & 1 else keep
        target[index >> 1] = source[pl.ds(start, height), :].astype(BF16)


ANY = pl.BlockSpec(memory_space=pl.ANY)


def whole(*shape):
    return pl.BlockSpec(shape, lambda *_: (0,) * len(shape))


def like(shape, dtype):
    return jax.ShapeDtypeStruct(shape, dtype)


def call(kernel, name, steps, scalars, ins, outs, scratch, cost, aliases=None):
    flops, moved, transcendentals = cost
    return pl.pallas_call(
        kernel,
        out_shape=tuple(item for item, _ in outs),
        grid_spec=pltpu.PrefetchScalarGridSpec(
            num_scalar_prefetch=len(scalars),
            grid=(steps,),
            in_specs=[spec for _, spec in ins],
            out_specs=tuple(spec for _, spec in outs),
            scratch_shapes=scratch,
        ),
        input_output_aliases={len(scalars) + k: v for k, v in (aliases or {}).items()},
        compiler_params=pltpu.CompilerParams(vmem_limit_bytes=VMEM_LIMIT),
        cost_estimate=pl.CostEstimate(
            flops=int(flops), bytes_accessed=int(moved), transcendentals=int(transcendentals)
        ),
        name=name,
    )(*scalars, *[item for item, _ in ins])


def group(count):
    return 2 if count % 2 == 0 else 1


def prepare_kernel(chunks, *refs):
    items, (output, expand, shrink), (vectors, packed) = refs[:8], refs[8:11], refs[11:]
    width = vectors.shape[1]
    row = 0
    for item in items:
        for start in range(0, item.shape[0], width):
            vectors[row : row + 1, :] = item[pl.ds(start, width)].reshape(1, width)
            row += 1
    half = output.shape[0] // 2
    blocks = expand.shape[1] // width
    tall = shrink.shape[0] // (2 * chunks)
    for upper in range(2):
        rows = slice(upper * half, (upper + 1) * half)
        packed[upper, :half, :] = output[rows, :]
        for block in range(blocks):
            start = (1 + block) * half
            packed[upper, start : start + half, :] = expand[
                rows, block * width : (block + 1) * width
            ]
        for number in range(chunks):
            start = (1 + blocks) * half + number * tall
            source = (2 * number + upper) * tall
            packed[upper, start : start + tall, :] = shrink[source : source + tall, :]


def prepare(chunks, items, weights):
    width = weights[0].shape[1]
    count = sum(item.shape[0] for item in items) // width
    total = sum(item.shape[0] * item.shape[1] for item in weights) // (2 * width)
    return call(
        functools.partial(prepare_kernel, chunks),
        "prepare",
        1,
        (),
        [(item, whole(*item.shape)) for item in (*items, *weights)],
        [
            (like((count, width), F32), whole(count, width)),
            (like((2, total, width), BF16), whole(2, total, width)),
        ],
        [],
        (0, 8 * total * width, 0),
    )


def collect_kernel(*refs):
    out = refs[-1]
    width = out.shape[1]
    singles, triples, expands, tables = refs[:6], refs[6:9], refs[9:12], refs[12:-1]
    out[...] = jnp.zeros_like(out)
    for row, item in enumerate(singles):
        out[row : row + 1, :] = item[...]
    size = width // 3
    for number, item in enumerate(triples):
        for part in range(3):
            row = TRIPLE_BIAS + part
            out[row : row + 1, number * size : (number + 1) * size] = item[
                :, part * size : (part + 1) * size
            ]
    for number, item in enumerate(expands):
        for part in range(item.shape[1] // size):
            row = EXPAND_BIAS + part
            out[row : row + 1, number * size : (number + 1) * size] = item[
                :, part * size : (part + 1) * size
            ]
    total = tables[0][...]
    for item in tables[1:]:
        total = total + item[...]
    for piece in range(3):
        out[TABLES : TABLES + 9, piece * LANES : (piece + 1) * LANES] = total[
            9 * piece : 9 * piece + 9, :
        ]


def collect(singles, triples, expands, tables):
    width = singles[0].shape[1]
    items = (*singles, *triples, *expands, *tables)
    return call(
        collect_kernel,
        "collect",
        1,
        (),
        [(item, whole(*item.shape)) for item in items],
        [(like((24, width), F32), whole(24, width))],
        [],
        (0, 16 * 24 * width, 0),
    )[0]


def attend_kernel(
    slabs, before, meta, windows, tokens, vectors, height, width_table, places, blocks, selectors,
    p0, p1, p2, p3, p4, p5, *rest,
):
    (
        rows_out, normed_out, triple_out, probs_out, attended_out,
        full, staged, weight, tables, masked_keys, sems,
    ) = rest[-11:]
    step = pl.program_id(0)
    base_slab = (step + before) * slabs
    width = full.shape[2]

    @pl.when(step == 0)
    def _():
        copies = load_rows(meta, (p0, p1, p2, p3, p4, p5), weight, sems)
        tables[...] = build_tables(height, width_table, places, blocks)
        wait_all(copies)

    gather_quarters(step == 0, tokens, staged, full, base_slab, slabs)
    rows = full[...].reshape(slabs * ROWS, width)
    unit, _ = normalize(rows)
    normed = unit * vectors[FIRST_GAIN : FIRST_GAIN + 1] + vectors[FIRST_SHIFT : FIRST_SHIFT + 1]
    normed = normed.astype(BF16)
    rows_out[...] = rows.astype(BF16).reshape(slabs, ROWS, width)
    normed_out[...] = normed.reshape(slabs, ROWS, width)
    for part in range(3):
        columns = slice(part * width, (part + 1) * width)
        bias = vectors[TRIPLE_BIAS + part : TRIPLE_BIAS + part + 1]
        triple = dot(normed, weight[:, columns]) + bias
        triple_out[:, :, columns] = triple.astype(BF16).reshape(slabs, ROWS, width)

    lane = lax.broadcasted_iota(jnp.int32, (ROWS, LANES), 1)
    within = lane & (SEG - 1)
    upper = lane >= HD
    quads = HEADS // QUAD
    for slab in range(slabs):
        allowed = valid_rows(windows[meta[0], base_slab + slab])
        penalty = jnp.where((lane == WIN) & jnp.logical_not(allowed), PENALTY, 0.0).astype(BF16)
        for head in range(QUAD):
            masked_keys[slab, head] = selectors[head] + penalty

    def one_quad(index, carry):
        slab = index // quads
        quad = index - slab * quads
        allowed = valid_rows(windows[meta[0], base_slab + slab])
        base = pl.multiple_of(quad * QUAD * HD, LANES)
        queries = triple_out[slab, :, pl.ds(base, QUAD * HD)]
        keys = triple_out[slab, :, pl.ds(pl.multiple_of(base + width, LANES), QUAD * HD)]
        values = triple_out[slab, :, pl.ds(pl.multiple_of(base + 2 * width, LANES), QUAD * HD)]
        terms = dot(queries, tables[...])
        high = roll_rows(terms[:, :LANES], False)
        wide = roll_rows(terms[:, LANES:], True)
        constant = jnp.where(lane == WIN, 1.0, 0.0)
        relative = jnp.where(
            within < WIN, high, jnp.where((within >= 16) & (within < 16 + WIN), wide, constant)
        ).astype(BF16)
        queries = queries * jnp.asarray(HD**-0.5, BF16)
        outs = []
        for pair in range(QUAD // 2):
            columns = slice(pair * LANES, (pair + 1) * LANES)
            left = jnp.concatenate([queries[:, columns], relative], axis=1)
            total = None
            for side in range(2):
                head = 2 * pair + side
                mine = upper if side else jnp.logical_not(upper)
                zero = jnp.zeros((ROWS, LANES), BF16)
                right = jnp.concatenate(
                    [jnp.where(mine, keys[:, columns], zero), masked_keys[slab, head]], axis=1
                )
                scores = dot_t(left, right)
                maxima = jnp.max(scores, axis=-1, keepdims=True)
                exponent = jnp.exp(scores - maxima)
                summed = jnp.sum(exponent, axis=-1, keepdims=True)
                probs = (exponent * (1.0 / summed)).astype(BF16)
                probs_out[slab, quad * QUAD + head] = probs
                part = dot(probs, jnp.where(mine, values[:, columns], zero))
                total = part if total is None else total + part
            outs.append(total)
        mixed = jnp.concatenate(outs, axis=1)
        mixed = jnp.where(allowed, mixed, 0.0)
        attended_out[slab, :, pl.ds(base, QUAD * HD)] = mixed.astype(BF16)
        return carry

    lax.fori_loop(0, slabs * quads, one_quad, 0)


def attend(before, steps, meta, windows, tokens, vectors, tables, selectors, pieces, kept):
    parts, rows_dev, slots, width = tokens.shape
    slabs = group(slots)
    block3 = lambda columns: pl.BlockSpec((slabs, ROWS, columns), lambda i, *_: (i + before, 0, 0))
    rows = steps * slabs * ROWS
    ins = [(item, whole(*item.shape)) for item in (tokens, vectors, *tables, selectors)]
    ins += [(item, ANY) for item in pieces]
    aliases = {}
    if kept is not None:
        aliases = {len(ins) + n: n for n in range(len(kept))}
        ins += [(item, ANY) for item in kept]
    return call(
        functools.partial(attend_kernel, slabs, before),
        "attend",
        steps,
        (meta, windows),
        ins,
        [
            (like((slots, ROWS, width), BF16), block3(width)),
            (like((slots, ROWS, width), BF16), block3(width)),
            (like((slots, ROWS, 3 * width), BF16), block3(3 * width)),
            (
                like((slots, HEADS, ROWS, ROWS), BF16),
                pl.BlockSpec((slabs, HEADS, ROWS, ROWS), lambda i, *_: (i + before, 0, 0, 0)),
            ),
            (like((slots, ROWS, width), BF16), block3(width)),
        ],
        [
            pltpu.VMEM((slabs, ROWS, width), F32),
            pltpu.VMEM((parts * width // LANES, rows_dev * slots, LANES), F32),
            pltpu.VMEM((width, 3 * width), BF16),
            pltpu.VMEM((2 * LANES, 2 * LANES), BF16),
            pltpu.VMEM((slabs, QUAD, ROWS, LANES), BF16),
            pltpu.SemaphoreType.DMA((8,)),
        ],
        (
            6 * rows * width * width + steps * slabs * HEADS * 4 * ROWS * ROWS * 256,
            rows * (width * 16 + HEADS * 512) + width * width * 6,
            steps * slabs * HEADS * ROWS * ROWS,
        ),
        aliases,
    )


def project_kernel(
    slabs, meta, windows, attended, rows_in, grads, vectors, p0, p1, p2, p3, p4, p5,
    middle_out, normed_out, branch_out, shrink_bias_out, full, staged, weight, sems,
):
    step = pl.program_id(0)

    @pl.when(step == 0)
    def _():
        wait_all(load_rows(meta, (p0, p1, p2, p3, p4, p5), weight, sems))
        shrink_bias_out[...] = jnp.zeros_like(shrink_bias_out)

    width = full.shape[2]
    count = slabs * ROWS
    middle = (
        rows_in[...].reshape(count, width).astype(F32)
        + dot(attended[...].reshape(count, width), weight[...])
        + vectors[OUTPUT_BIAS : OUTPUT_BIAS + 1]
    )
    unit, _ = normalize(middle)
    middle_out[...] = middle
    normed = unit * vectors[SECOND_GAIN : SECOND_GAIN + 1] + vectors[SECOND_SHIFT : SECOND_SHIFT + 1]
    normed_out[...] = normed.astype(BF16)
    gather_quarters(step == 0, grads, staged, full, step * slabs, slabs)
    for slab in range(slabs):
        allowed = valid_rows(windows[meta[0], step * slabs + slab])
        branch = jnp.where(allowed, full[slab], 0.0)
        branch_out[slab * ROWS : (slab + 1) * ROWS, :] = branch.astype(BF16)
        shrink_bias_out[...] += jnp.sum(branch, axis=0, keepdims=True)


def project(meta, windows, attended, rows_in, grads, vectors, pieces):
    parts, rows_dev, slots, width = grads.shape
    slabs = group(slots)
    block = pl.BlockSpec((slabs, ROWS, width), lambda i, *_: (i, 0, 0))
    flat = pl.BlockSpec((slabs * ROWS, width), lambda i, *_: (i, 0))
    rows = slots * ROWS
    return call(
        functools.partial(project_kernel, slabs),
        "project",
        slots // slabs,
        (meta, windows),
        [(attended, block), (rows_in, block)]
        + [(item, whole(*item.shape)) for item in (grads, vectors)]
        + [(item, ANY) for item in pieces],
        [
            (like((rows, width), F32), flat),
            (like((rows, width), BF16), flat),
            (like((rows, width), BF16), flat),
            (like((1, width), F32), whole(1, width)),
        ],
        [
            pltpu.VMEM((slabs, ROWS, width), F32),
            pltpu.VMEM((parts * width // LANES, rows_dev * slots, LANES), F32),
            pltpu.VMEM((width, width), BF16),
            pltpu.SemaphoreType.DMA((8,)),
        ],
        (2 * rows * width * width, rows * width * 14, 0),
    )


def gate_both(hidden):
    half = 0.5 * (1.0 + lax.erf(hidden * 0.7071067811865476))
    density = jnp.exp(hidden * hidden * -0.5) * 0.3989422804014327
    return hidden * half, half + hidden * density


def feed_kernel(number, first, unit, meta, normed, branch, vectors, *rest):
    pieces, rest = rest[:6], rest[6:]
    if not first:
        out_in, grad_in = rest[:2]
    out_acc, grad_acc, keep, send, bias_grad, expand, shrink, acc_e, acc_s, sems = rest[-10:]
    step = pl.program_id(0)
    last = pl.num_programs(0) - 1
    width, chunk = expand.shape
    blocks = chunk // unit

    @pl.when(step == 0)
    def _():
        pairs = []
        height = width // 8
        tall = chunk // 8
        for source, half, place in weight_places(meta, pieces):
            source = source if half is None else source.at[half]
            start = pl.multiple_of(place * height, 16)
            for block in range(blocks):
                pairs.append(
                    (
                        source.at[
                            pl.ds((1 + block) * height, height), pl.ds(number * unit, unit)
                        ],
                        expand.at[pl.ds(start, height), pl.ds(block * unit, unit)],
                    )
                )
            start = pl.multiple_of(place * tall, 16)
            first_row = (1 + blocks) * height + number * tall
            pairs.append((source.at[pl.ds(first_row, tall), :], shrink.at[pl.ds(start, tall), :]))
        copies = start_copies(pairs, sems)
        acc_e[...] = jnp.zeros_like(acc_e)
        acc_s[...] = jnp.zeros_like(acc_s)
        bias_grad[...] = jnp.zeros_like(bias_grad)
        wait_all(copies)

    rows = normed[...]
    grads = branch[...]
    total_out = None
    total_grad = None
    for block in range(blocks):
        columns = slice(block * unit, (block + 1) * unit)
        bias = vectors[
            EXPAND_BIAS + block : EXPAND_BIAS + block + 1, number * unit : (number + 1) * unit
        ]
        hidden = dot(rows, expand[:, columns]) + bias
        active, slope = gate_both(hidden)
        active = active.astype(BF16)
        part = dot(active, shrink[columns, :])
        total_out = part if total_out is None else total_out + part
        back = (dot_t(grads, shrink[columns, :]) * slope).astype(BF16)
        acc_s[columns, :] += dot_rows(active, grads)
        acc_e[:, columns] += dot_rows(rows, back)
        bias_grad[:, columns] += jnp.sum(back.astype(F32), axis=0, keepdims=True)
        part = dot_t(back, expand[:, columns])
        total_grad = part if total_grad is None else total_grad + part
    if first:
        out_acc[...] = total_out
        grad_acc[...] = total_grad
    else:
        out_acc[...] = out_in[...] + total_out
        grad_acc[...] = grad_in[...] + total_grad

    @pl.when(step == last)
    def _():
        height = width // 4
        third = height // 3
        for index in range(4):
            target = (send if index & 1 else keep).at[index >> 1]
            start = pl.multiple_of((meta[0] ^ index) * unit, 16)
            target[:unit, :] = acc_s[pl.ds(start, unit), :].astype(BF16)
            start = pl.multiple_of((meta[0] ^ index) * height, 16)
            target[unit : unit + height, :] = acc_e[pl.ds(start, height), :width].astype(BF16)
            for piece in range(3):
                here = pl.multiple_of(start + piece * third, 16)
                target[unit + height :, piece * unit : (piece + 1) * unit] = acc_e[
                    pl.ds(here, third), width:
                ].astype(BF16)


def feed(number, count, meta, normed, branch, vectors, pieces, kept):
    rows, width = normed.shape
    chunk = 4 * width // count
    unit = chunk // 4
    block_rows = 2 * ROWS
    block = pl.BlockSpec((block_rows, width), lambda i, *_: (i, 0))
    ins = [(normed, block), (branch, block), (vectors, whole(*vectors.shape))]
    ins += [(item, ANY) for item in pieces]
    aliases = {}
    if kept is not None:
        aliases = {len(ins) + n: n for n in range(2)}
        ins += [(item, block) for item in kept]
    payload = (2, unit + unit, width)
    return call(
        functools.partial(feed_kernel, number, kept is None, unit),
        "feed",
        rows // block_rows,
        (meta,),
        ins,
        [
            (like((rows, width), F32), block),
            (like((rows, width), F32), block),
            (like(payload, BF16), whole(*payload)),
            (like(payload, BF16), whole(*payload)),
            (like((1, chunk), F32), whole(1, chunk)),
        ],
        [
            pltpu.VMEM((width, chunk), BF16),
            pltpu.VMEM((chunk, width), BF16),
            pltpu.VMEM((width, chunk), F32),
            pltpu.VMEM((chunk, width), F32),
            pltpu.SemaphoreType.DMA((40,)),
        ],
        (12 * rows * width * chunk, rows * width * 20 + width * chunk * 8, 2 * rows * chunk),
        aliases,
    )


def middle_kernel(
    slabs, meta, windows, middle, out_acc, grad_acc, branch, attended, vectors,
    p0, p1, p2, p3, p4, p5,
    result_out, d_middle_out, d_attended_out, keep, send, output_bias_grad, gain_grad,
    shift_grad, full, staged, weight, acc, sems,
):
    step = pl.program_id(0)
    last = pl.num_programs(0) - 1

    @pl.when(step == 0)
    def _():
        copies = load_rows(meta, (p0, p1, p2, p3, p4, p5), weight, sems)
        acc[...] = jnp.zeros_like(acc)
        output_bias_grad[...] = jnp.zeros_like(output_bias_grad)
        gain_grad[...] = jnp.zeros_like(gain_grad)
        shift_grad[...] = jnp.zeros_like(shift_grad)
        wait_all(copies)

    width = full.shape[2]
    count = slabs * ROWS
    rows = middle[...]
    result = rows + out_acc[...] + vectors[SHRINK_BIAS : SHRINK_BIAS + 1]
    full[...] = result.reshape(slabs, ROWS, width)
    scatter_quarters(step == last, full, staged, result_out, step * slabs, slabs)
    unit, scale = normalize(rows)
    grad = grad_acc[...]
    gain_grad[...] += jnp.sum(grad * unit, axis=0, keepdims=True)
    shift_grad[...] += jnp.sum(grad, axis=0, keepdims=True)
    d_middle = branch[...].astype(F32) + normalize_back(
        unit, scale, grad, vectors[SECOND_GAIN : SECOND_GAIN + 1]
    )
    d_middle_out[...] = d_middle
    d_output = d_middle.astype(BF16)
    output_bias_grad[...] += jnp.sum(d_output.astype(F32), axis=0, keepdims=True)
    acc[...] += dot_rows(attended[...].reshape(count, width), d_output)
    d_attended = dot_t(d_output, weight[...]).reshape(slabs, ROWS, width)
    for slab in range(slabs):
        allowed = valid_rows(windows[meta[0], step * slabs + slab])
        d_attended_out[slab] = jnp.where(allowed, d_attended[slab], 0.0).astype(BF16)

    @pl.when(step == last)
    def _():
        write_owned(acc, meta, keep, send)


def middle_back(meta, windows, rows_dev, middle, out_acc, grad_acc, branch, attended, vectors, pieces):
    slots, _, width = attended.shape
    parts = WROWS // rows_dev
    slabs = group(slots)
    block = pl.BlockSpec((slabs, ROWS, width), lambda i, *_: (i, 0, 0))
    flat = pl.BlockSpec((slabs * ROWS, width), lambda i, *_: (i, 0))
    rows = slots * ROWS
    vec = (like((1, width), F32), whole(1, width))
    payload = (2, width // 4, width)
    quarter = (parts, rows_dev, slots, width)
    return call(
        functools.partial(middle_kernel, slabs),
        "middle",
        slots // slabs,
        (meta, windows),
        [
            (middle, flat), (out_acc, flat), (grad_acc, flat), (branch, flat), (attended, block),
            (vectors, whole(*vectors.shape)),
        ]
        + [(item, ANY) for item in pieces],
        [
            (like(quarter, BF16), whole(*quarter)),
            (like((rows, width), F32), flat),
            (like((slots, ROWS, width), BF16), block),
            (like(payload, BF16), whole(*payload)),
            (like(payload, BF16), whole(*payload)),
            vec,
            vec,
            vec,
        ],
        [
            pltpu.VMEM((slabs, ROWS, width), F32),
            pltpu.VMEM((parts * width // LANES, rows_dev * slots, LANES), F32),
            pltpu.VMEM((width, width), BF16),
            pltpu.VMEM((width, width), F32),
            pltpu.SemaphoreType.DMA((8,)),
        ],
        (4 * rows * width * width, rows * width * 24, 0),
    )


def attend_back_kernel(
    slabs, meta, normed, queries_in, keys_in, values_in, probs_in, d_mixed_in, mixed_in,
    height, width_table, places, blocks, selectors, sums,
    d_queries, d_keys, d_values, keep, send, bias_grad, table_out, grads, acc, tables, table_grad,
):
    step = pl.program_id(0)
    last = pl.num_programs(0) - 1
    wide4 = QUAD * HD

    @pl.when(step == 0)
    def _():
        acc[...] = jnp.zeros_like(acc)
        bias_grad[...] = jnp.zeros_like(bias_grad)
        table_grad[...] = jnp.zeros_like(table_grad)
        tables[...] = build_tables(height, width_table, places, blocks)

    lane = lax.broadcasted_iota(jnp.int32, (ROWS, LANES), 1)
    within = lane & (SEG - 1)
    upper = lane >= HD
    zero = jnp.zeros((ROWS, LANES), BF16)

    def one_slab(slab, carry):
        queries, keys, values = queries_in[slab], keys_in[slab], values_in[slab]
        d_mixed = d_mixed_in[slab]
        product = d_mixed.astype(F32) * mixed_in[slab].astype(F32)
        product_high = product.astype(BF16)
        product_low = (product - product_high.astype(F32)).astype(BF16)
        inner = dot(product_high, sums[...]) + dot(product_low, sums[...])
        inner_high = inner.astype(BF16)
        inner_low = (inner - inner_high.astype(F32)).astype(BF16)
        inner = jnp.where((lane & 1) == 0, inner_high, inner_low)
        d_relative = None
        dq, dk, dv = [], [], []
        for pair in range(QUAD // 2):
            columns = slice(pair * LANES, (pair + 1) * LANES)
            left = jnp.concatenate([d_mixed[:, columns], inner], axis=1)
            dq_pair = dk_pair = dv_pair = None
            for side in range(2):
                head = 2 * pair + side
                mine = upper if side else jnp.logical_not(upper)
                minus = jnp.where((lane == 2 * head) | (lane == 2 * head + 1), -1.0, 0.0)
                right = jnp.concatenate(
                    [jnp.where(mine, values[:, columns], zero), minus.astype(BF16)], axis=1
                )
                d_probs = dot_t(left, right)
                probs = probs_in[slab, head]
                d_scores = (probs.astype(F32) * d_probs).astype(BF16)
                back = dot(
                    d_scores,
                    jnp.concatenate(
                        [jnp.where(mine, keys[:, columns], zero), selectors[head]], axis=1
                    ),
                )
                part_k = dot_rows(d_scores, jnp.where(mine, queries[:, columns], zero))
                part_v = dot_rows(probs, jnp.where(mine, d_mixed[:, columns], zero))
                if dq_pair is None:
                    dq_pair, dk_pair, dv_pair = back[:, :LANES], part_k, part_v
                else:
                    dq_pair = dq_pair + back[:, :LANES]
                    dk_pair = dk_pair + part_k
                    dv_pair = dv_pair + part_v
                d_relative = back[:, LANES:] if d_relative is None else d_relative + back[:, LANES:]
            dq.append(dq_pair)
            dk.append(dk_pair)
            dv.append(dv_pair)
        high = roll_rows(jnp.where(within < WIN, d_relative, 0.0), False)
        wide = roll_rows(
            jnp.where((within >= 16) & (within < 16 + WIN), d_relative, 0.0), True
        )
        d_terms = jnp.concatenate([high, wide], axis=1).astype(BF16)
        scale = HD**-0.5
        dq = jnp.concatenate(dq, axis=1) * scale + dot_t(d_terms, tables[...])
        table_grad[...] += dot_rows(queries, d_terms)
        dq = dq.astype(BF16)
        dk = (jnp.concatenate(dk, axis=1) * scale).astype(BF16)
        dv = jnp.concatenate(dv, axis=1).astype(BF16)
        d_queries[slab] = dq
        d_keys[slab] = dk
        d_values[slab] = dv
        grads[slab] = jnp.concatenate([dq, dk, dv], axis=1)
        return carry

    lax.fori_loop(0, slabs, one_slab, 0)
    width = normed.shape[2]
    both = grads[...].reshape(slabs * ROWS, 3 * wide4)
    bias_grad[...] += jnp.sum(both.astype(F32), axis=0, keepdims=True)
    acc[...] += dot_rows(normed[...].reshape(slabs * ROWS, width), both)

    @pl.when(step == last)
    def _():
        write_owned(acc, meta, keep, send)
        masked = table_grad[...] * blocks[...].astype(F32)
        folded = masked[:HD]
        for head in range(1, QUAD):
            folded = folded + masked[head * HD : (head + 1) * HD]
        high = folded.astype(BF16)
        low = (folded - high.astype(F32)).astype(BF16)
        for which in range(2):
            table_out[:, which * HD : (which + 1) * HD] = dot_t(places[which], high) + dot_t(
                places[which], low
            )


def attend_back(quad, meta, normed, triple, probs, d_mixed, mixed, tables, selectors, sums):
    slots, _, width = normed.shape
    slabs = group(slots)
    wide4 = QUAD * HD
    quads = HEADS // QUAD
    column = lambda where: pl.BlockSpec((slabs, ROWS, wide4), lambda i, *_: (i, 0, where))
    narrow = (
        like((slots, ROWS, wide4), BF16),
        pl.BlockSpec((slabs, ROWS, wide4), lambda i, *_: (i, 0, 0)),
    )
    rows = slots * ROWS
    payload = (2, width // 4, 3 * wide4)
    return call(
        functools.partial(attend_back_kernel, slabs),
        "attend_back",
        slots // slabs,
        (meta,),
        [
            (normed, pl.BlockSpec((slabs, ROWS, width), lambda i, *_: (i, 0, 0))),
            (triple, column(quad)),
            (triple, column(quads + quad)),
            (triple, column(2 * quads + quad)),
            (probs, pl.BlockSpec((slabs, QUAD, ROWS, ROWS), lambda i, *_: (i, quad, 0, 0))),
            (d_mixed, column(quad)),
            (mixed, column(quad)),
        ]
        + [(item, whole(*item.shape)) for item in (*tables, selectors, sums)],
        [
            narrow,
            narrow,
            narrow,
            (like(payload, BF16), whole(*payload)),
            (like(payload, BF16), whole(*payload)),
            (like((1, 3 * wide4), F32), whole(1, 3 * wide4)),
            (like((REL, 2 * HD), F32), whole(REL, 2 * HD)),
        ],
        [
            pltpu.VMEM((slabs, ROWS, 3 * wide4), BF16),
            pltpu.VMEM((width, 3 * wide4), F32),
            pltpu.VMEM((2 * LANES, 2 * LANES), BF16),
            pltpu.VMEM((2 * LANES, 2 * LANES), F32),
        ],
        (
            2 * rows * width * 3 * wide4 + slots * QUAD * 8 * ROWS * ROWS * 256,
            rows * (width * 2 + wide4 * 16 + QUAD * 512),
            0,
        ),
    )


def first_kernel(slabs, meta, rows_in, d_middle, vectors, *rest):
    grads, pieces = rest[:9], rest[9:15]
    tokens_out, gain_grad, shift_grad, full, staged, weight, sems = rest[15:]
    step = pl.program_id(0)
    last = pl.num_programs(0) - 1

    @pl.when(step == 0)
    def _():
        copies = load_rows(meta, pieces, weight, sems)
        gain_grad[...] = jnp.zeros_like(gain_grad)
        shift_grad[...] = jnp.zeros_like(shift_grad)
        wait_all(copies)

    width = full.shape[2]
    count = slabs * ROWS
    total = None
    wide4 = QUAD * HD
    for index, grad in enumerate(grads):
        part = dot_t(
            grad[...].reshape(count, wide4), weight[:, index * wide4 : (index + 1) * wide4]
        )
        total = part if total is None else total + part
    unit, scale = normalize(rows_in[...].reshape(count, width).astype(F32))
    gain_grad[...] += jnp.sum(total * unit, axis=0, keepdims=True)
    shift_grad[...] += jnp.sum(total, axis=0, keepdims=True)
    back = normalize_back(unit, scale, total, vectors[FIRST_GAIN : FIRST_GAIN + 1])
    full[...] = (d_middle[...] + back).reshape(slabs, ROWS, width)
    scatter_quarters(step == last, full, staged, tokens_out, step * slabs, slabs)


def first_back(before, steps, meta, rows_dev, rows_in, d_middle, vectors, grads, pieces):
    slots, _, width = rows_in.shape
    parts = WROWS // rows_dev
    slabs = group(slots)
    wide4 = QUAD * HD
    block = pl.BlockSpec((slabs, ROWS, width), lambda i, *_: (i + before, 0, 0))
    flat = pl.BlockSpec((slabs * ROWS, width), lambda i, *_: (i + before, 0))
    narrow = pl.BlockSpec((slabs, ROWS, wide4), lambda i, *_: (i + before, 0, 0))
    rows = steps * slabs * ROWS
    quarter = (parts, rows_dev, steps * slabs, width)
    return call(
        functools.partial(first_kernel, slabs),
        "first_back",
        steps,
        (meta,),
        [(rows_in, block), (d_middle, flat), (vectors, whole(*vectors.shape))]
        + [(item, narrow) for item in grads]
        + [(item, ANY) for item in pieces],
        [(like(quarter, BF16), whole(*quarter))] + [(like((1, width), F32), whole(1, width))] * 2,
        [
            pltpu.VMEM((slabs, ROWS, width), F32),
            pltpu.VMEM((parts * width // LANES, rows_dev * steps * slabs, LANES), F32),
            pltpu.VMEM((width, 3 * width), BF16),
            pltpu.SemaphoreType.DMA((8,)),
        ],
        (6 * rows * width * width, rows * width * 14, 0),
    )


def finish_kernel(unit, pairs, meta, *refs):
    items, small, refs = refs[: 2 * pairs], refs[2 * pairs], refs[2 * pairs + 1 :]
    (triple_out, output_out, expand_out, shrink_out), refs = refs[:4], refs[4:]
    vectors, tables, staged = refs[:8], refs[8:10], refs[10:]
    upper = meta[1] > 0
    for number, both in enumerate(staged):
        mine, other = items[2 * number], items[2 * number + 1]
        half = mine.shape[0]

        @pl.when(upper)
        def _():
            both[:half] = other[...]
            both[half:] = mine[...]

        @pl.when(jnp.logical_not(upper))
        def _():
            both[:half] = mine[...]
            both[half:] = other[...]

    shard, width = output_out.shape
    third = shard // 3
    parts = width // shard
    for number, both in enumerate(staged[:3]):
        here = number * unit
        shrink_out[here : here + unit, :] = both[:unit, :].astype(F32)
        for block in range(parts - 1):
            start = block * width + here
            expand_out[:, start : start + unit] = both[
                unit : unit + shard, block * unit : (block + 1) * unit
            ].astype(F32)
        start = (parts - 1) * width + here
        for piece in range(3):
            expand_out[piece * third : (piece + 1) * third, start : start + unit] = both[
                unit + shard :, piece * unit : (piece + 1) * unit
            ].astype(F32)
    output_out[...] = staged[3][:shard, :].astype(F32)
    wide4 = QUAD * HD
    for quad, both in enumerate(staged[3:]):
        values = both[shard:, :] if quad == 0 else both[...]
        for part in range(3):
            start = part * width + quad * wide4
            triple_out[:, start : start + wide4] = values[
                :, part * wide4 : (part + 1) * wide4
            ].astype(F32)
    row = 0
    for item in vectors:
        for start in range(0, item.shape[0], width):
            item[pl.ds(start, width)] = small[row : row + 1, :].reshape(width)
            row += 1
    for which, item in enumerate(tables):
        for piece in range(3):
            start = piece * LANES + which * HD
            item[9 * piece : 9 * piece + 9, :] = small[TABLES : TABLES + 9, start : start + HD]


def finish(meta, shares, small, matrices, vectors, tables, unit):
    items = [item for pair in shares for item in pair]
    outs = [item.shape for item in (*matrices, *vectors, *tables)]
    return call(
        functools.partial(finish_kernel, unit, len(shares)),
        "finish",
        1,
        (meta,),
        [(item, whole(*item.shape)) for item in (*items, small)],
        [(like(shape, F32), whole(*shape)) for shape in outs],
        [pltpu.VMEM((2 * mine.shape[0], mine.shape[1]), BF16) for mine, _ in shares],
        (0, sum(6 * item.size for item in items), 0),
    )


def swap(values, axis, bits):
    count = lax.axis_size(axis)
    return lax.ppermute(values, axis, [(n, n ^ bits) for n in range(count)])


def exchange_windows(values):
    return lax.all_to_all(values, "tensor", split_axis=0, concat_axis=0, tiled=True)


def after(values, *others):
    return lax.optimization_barrier((values, *others))[0]


def far_half(packed):
    bit = lax.axis_index("dp") & 1
    mine = lax.dynamic_index_in_dim(packed, bit, axis=0, keepdims=False)
    return swap(mine, "tensor", 2)


def add(*items):
    total = items[0].astype(F32)
    for item in items[1:]:
        total = total + item.astype(F32)
    return total.astype(BF16)


def halves(axis):
    out, bit = [], 1
    while bit < lax.axis_size(axis):
        out.append(bit)
        bit *= 2
    return out


def reduce_stages(payloads):
    totals = []
    while True:
        keep, send, more = payloads.pop(0)
        (far,) = yield [(send, "tensor", 1)]
        totals.append(add(keep, far))
        if not more:
            break
    total = totals[0] if len(totals) == 1 else jnp.concatenate(totals, axis=1)
    spot = lax.axis_index("dp")
    for bit in halves("dp"):
        size = total.shape[1] // 2
        upper = (spot & bit) > 0
        far = jnp.where(upper, total[:, :size], total[:, size:])
        near = jnp.where(upper, total[:, size:], total[:, :size])
        (far,) = yield [(far, "dp", bit)]
        total = add(near, far)
    (far,) = yield [(total[1], "tensor", 2)]
    total = add(total[0], far)
    for bit in halves("seq"):
        (far,) = yield [(total, "seq", bit)]
        total = add(total, far)
    for bit in reversed(halves("dp")):
        upper = (spot & bit) > 0
        (far,) = yield [(total, "dp", bit)]
        if bit > 1:
            total = jnp.concatenate(
                [jnp.where(upper, far, total), jnp.where(upper, total, far)], axis=0
            )
    return total, far


def sum_stages(values):
    for axis in ("tensor", "dp", "seq"):
        for bit in halves(axis):
            (far,) = yield [(values, axis, bit)]
            values = values + far
    return (values,)


class Exchanges:
    def __init__(self):
        self.running = []
        self.done = {}

    def begin(self, name, stages):
        self.running.append([name, stages, None])

    def step(self, token, meta, *extra):
        asked, ended = [], []
        arrived = [item for entry in self.running for item in (entry[2] or ())]
        if token is not None and arrived:
            token, *arrived = lax.optimization_barrier((token, *arrived))
        arrived = iter(arrived)
        for entry in list(self.running):
            name, stages, waiting = entry
            mine = None if waiting is None else [next(arrived) for _ in waiting]
            try:
                asked.append((entry, stages.send(mine)))
            except StopIteration as stop:
                ended.append((name, stop.value))
                self.running.remove(entry)
        values = [item[0] for _, wanted in asked for item in wanted]
        finished = [item for _, pair in ended for item in pair]
        if meta is not None:
            count = len(values)
            meta, *rest = lax.optimization_barrier((meta, *values, *finished, *extra))
            values = rest[:count]
            finished = rest[count : count + len(finished)]
            extra = rest[count + len(finished) :]
        values, finished = iter(values), iter(finished)
        for entry, wanted in asked:
            entry[2] = [swap(next(values), axis, bits) for _, axis, bits in wanted]
        for name, pair in ended:
            self.done[name] = tuple(next(finished) for _ in pair)
        return (token, meta, *extra)

    def finish(self):
        while self.running:
            self.step(None, None)


def local(
    tokens,
    out_grad,
    slot_window,
    first_gain,
    first_shift,
    triple_weight,
    triple_bias,
    height_table,
    width_table,
    output_weight,
    output_bias,
    second_gain,
    second_shift,
    expand_weight,
    expand_bias,
    shrink_weight,
    shrink_bias,
):
    micros, images, slots, rows_dev, width = tokens.shape
    parts = lax.axis_size("tensor")
    mine = lax.axis_index("tensor")
    shard = width // parts
    chunks = 3
    unit = width // chunks
    bit = lax.axis_index("dp") & 1
    meta = jnp.where(jnp.arange(2) == 0, mine, bit).astype(jnp.int32)

    by_image = lambda values: jnp.swapaxes(values, 2, 3).reshape(parts, rows_dev, slots, width)
    to_image = lambda values: jnp.swapaxes(
        values.reshape(micros, images, rows_dev, slots, width), 2, 3
    )
    windows = slot_window.reshape(parts, slots)

    packed = triple_weight.reshape(2, shard // 2, -1)
    far = far_half(packed)
    rows_in = exchange_windows(by_image(tokens))
    near = swap(packed, "tensor", 1)
    vectors, packed_rest = prepare(
        chunks,
        (
            first_gain, first_shift, output_bias, second_gain, second_shift, shrink_bias,
            triple_bias, expand_bias,
        ),
        (output_weight, expand_weight, shrink_weight),
    )
    sums = np.zeros((QUAD * HD, LANES), np.float32)
    for head in range(QUAD):
        sums[head * HD : (head + 1) * HD, 2 * head : 2 * head + 2] = 1.0
    sums = jnp.asarray(sums, BF16)
    ahead = (height_table, width_table, table_places(False), head_blocks(False))
    behind = (height_table, width_table, table_places(True), head_blocks(True))
    far, vectors, packed_rest, meta = lax.optimization_barrier((far, vectors, packed_rest, meta))
    other = swap(far, "dp", 1)
    triple_pieces = (
        packed, near, far, other, swap(far, "tensor", 1), swap(other, "tensor", 1),
    )

    packed = after(packed_rest, rows_in, far)
    far = far_half(packed)
    near = swap(packed, "tensor", 1)
    steps = slots // group(slots)
    early = max(1, steps // 2)
    selectors = key_selectors(False)
    kept = attend(
        0, early, meta, windows, rows_in, vectors, ahead, selectors, triple_pieces, None
    )
    kept = list(kept)
    kept[4], far, own_grads = lax.optimization_barrier((kept[4], far, by_image(out_grad)))
    meta, far, own_grads = lax.optimization_barrier((meta, far, own_grads))
    other = swap(far, "dp", 1)
    crossed = swap(far, "tensor", 1)
    grads_in = exchange_windows(own_grads)
    if early < steps:
        kept = attend(
            early, steps - early, meta, windows, rows_in, vectors, ahead, selectors,
            triple_pieces, kept,
        )
    full_rows, normed, triple, probs, attended = kept
    attended, other = lax.optimization_barrier((attended, other))
    rest_pieces = (packed, near, far, other, crossed, swap(other, "tensor", 1))

    middle, normed2, branch, shrink_bias_grad = project(
        meta, windows, attended, full_rows, grads_in, vectors, rest_pieces
    )
    exchanges = Exchanges()
    kept = None
    expand_bias_grads = []
    for number in range(chunks):
        *kept, keep, send, bias_grad = feed(
            number, chunks, meta, normed2, branch, vectors, rest_pieces, kept
        )
        exchanges.begin(("feed", number), reduce_stages([(keep, send, False)]))
        bias_grad, meta = exchanges.step(bias_grad, meta)
        expand_bias_grads.append(bias_grad)

    result, d_middle, d_attended, keep, send, output_bias_grad, gain2_grad, shift2_grad = (
        middle_back(
            meta, windows, rows_dev, middle, *kept, branch, attended, vectors, rest_pieces
        )
    )
    payloads = [(keep, send, True)]
    exchanges.begin(("rest", 0), reduce_stages(payloads))
    output_bias_grad, meta = exchanges.step(output_bias_grad, meta)
    result = exchange_windows(result)

    quad_grads, triple_bias_grads, table_grads = [], [], []
    for quad in range(HEADS // QUAD):
        dq, dk, dv, keep, send, bias_grad, table_grad = attend_back(
            quad, meta, normed, triple, probs, d_attended, attended, behind, key_selectors(True), sums
        )
        if quad == 0:
            payloads.append((keep, send, False))
        else:
            exchanges.begin(("rest", quad), reduce_stages([(keep, send, False)]))
        if quad == 1:
            bias_grad, meta, result = exchanges.step(bias_grad, meta, result)
        else:
            bias_grad, meta = exchanges.step(bias_grad, meta)
        quad_grads.append((dq, dk, dv))
        triple_bias_grads.append(bias_grad)
        table_grads.append(table_grad)
    wide4 = QUAD * HD
    grads9 = [quad_grads[quad][part] for part in range(3) for quad in range(HEADS // QUAD)]
    token_grad, gain1_grad, shift1_grad = first_back(
        0, steps, meta, rows_dev, full_rows, d_middle, vectors, grads9, triple_pieces
    )
    tokens_gradient = to_image(exchange_windows(token_grad))
    result = to_image(result)
    gain1_grad, _ = exchanges.step(gain1_grad, None)
    small = collect(
        (gain1_grad, shift1_grad, output_bias_grad, gain2_grad, shift2_grad, shrink_bias_grad),
        triple_bias_grads,
        expand_bias_grads,
        table_grads,
    )
    exchanges.begin("small", sum_stages(small))
    exchanges.finish()
    shares = [exchanges.done["feed", number] for number in range(chunks)]
    shares += [exchanges.done["rest", number] for number in range(HEADS // QUAD)]
    (
        triple_gradient, output_gradient, expand_gradient, shrink_gradient, *outs, high, wide,
    ) = finish(
        meta,
        shares,
        exchanges.done["small"][0],
        (triple_weight, output_weight, expand_weight, shrink_weight),
        (
            first_gain, first_shift, output_bias, second_gain, second_shift, shrink_bias,
            triple_bias, expand_bias,
        ),
        (height_table, width_table),
        unit,
    )
    return (
        result,
        tokens_gradient,
        outs[0],
        outs[1],
        triple_gradient,
        outs[6],
        high,
        wide,
        output_gradient,
        outs[2],
        outs[3],
        outs[4],
        expand_gradient,
        outs[7],
        shrink_gradient,
        outs[5],
    )


def solution(mesh):
    split = P(None, "dp", "seq", "tensor", None)
    rows = P("tensor", None)
    return jax.shard_map(
        local,
        mesh=mesh,
        in_specs=(
            split, split, P(None, "dp", "seq"), P(), P(), rows, P(), P(), P(), rows, P(), P(), P(),
            rows, P(), rows, P(),
        ),
        out_specs=(
            split, split, P(), P(), rows, P(), P(), P(), rows, P(), P(), P(), rows, P(), rows, P(),
        ),
        check_vma=False,
    )
```

```python
import functools

import jax
import jax.numpy as jnp
import numpy as np
from jax import lax
from jax.experimental import pallas as pl
from jax.experimental.pallas import tpu as pltpu
from jax.sharding import PartitionSpec as P

HEADS = 12
HD = 64
WIN = 14
GRID = 64
WGRID = 5
WROWS = WIN * WIN
ROWS = 200
QUAD = 4
LANES = 128
REL = 2 * WIN - 1
SEG = 32
EPSILON = 1e-06
PENALTY = -1e9

F32 = jnp.float32
BF16 = jnp.bfloat16
FIRST_GAIN, FIRST_SHIFT, OUTPUT_BIAS, SECOND_GAIN, SECOND_SHIFT, SHRINK_BIAS = range(6)
TRIPLE_BIAS, EXPAND_BIAS, TABLES = 6, 9, 13
VMEM_LIMIT = 58 * 1024 * 1024


def dot(left, right):
    return lax.dot_general(left, right, (((1,), (0,)), ((), ())), preferred_element_type=F32)


def dot_t(left, right):
    return lax.dot_general(left, right, (((1,), (1,)), ((), ())), preferred_element_type=F32)


def dot_rows(left, right):
    return lax.dot_general(left, right, (((0,), (0,)), ((), ())), preferred_element_type=F32)


def key_selectors(mirrored):
    out = np.zeros((QUAD, ROWS, LANES), np.float32)
    for head in range(QUAD):
        for key in range(WROWS):
            high, wide = key // WIN, key % WIN
            if mirrored:
                high, wide = WIN - 1 - high, WIN - 1 - wide
            out[head, key, SEG * head + high] = 1.0
            out[head, key, SEG * head + 16 + wide] = 1.0
    return jnp.asarray(out, BF16)


def table_places(mirrored):
    out = np.zeros((2, REL, 2 * LANES), np.float32)
    for head in range(QUAD):
        for row in range(REL):
            if mirrored:
                out[0, row, SEG * head + row] = 1.0
                out[1, row, LANES + (SEG * head + 16 + row) % LANES] = 1.0
            else:
                out[0, REL - 1 - row, (SEG * head + row - 13) % LANES] = 1.0
                out[1, REL - 1 - row, LANES + (SEG * head + row + 3) % LANES] = 1.0
    return jnp.asarray(out, BF16)


def head_blocks(mirrored):
    out = np.zeros((QUAD * HD, 2 * LANES), np.float32)
    for head in range(QUAD):
        rows = slice(head * HD, (head + 1) * HD)
        for row in range(REL):
            if mirrored:
                out[rows, SEG * head + row] = 1.0
                out[rows, LANES + (SEG * head + 16 + row) % LANES] = 1.0
            else:
                out[rows, (SEG * head + row - 13) % LANES] = 1.0
                out[rows, LANES + (SEG * head + row + 3) % LANES] = 1.0
    return jnp.asarray(out, BF16)


def valid_rows(window):
    high_place = (window * 13) >> 6
    wide_place = window - high_place * WGRID
    inside = window < WGRID * WGRID
    row = lax.broadcasted_iota(jnp.int32, (ROWS, 1), 0)
    high = (row * 4682) >> 16
    wide = row - high * WIN
    high_limit = jnp.where(inside, GRID - high_place * WIN, 0)
    return (high < high_limit) & (wide < GRID - wide_place * WIN) & (row < WROWS)


def build_tables(height, width, places, blocks):
    both = dot_rows(height[...].astype(BF16), places[0]) + dot_rows(
        width[...].astype(BF16), places[1]
    )
    both = both.astype(BF16)
    return jnp.concatenate([both] * QUAD, axis=0) * blocks[...]


def roll_rows(values, by_width):
    sub = lax.broadcasted_iota(jnp.int32, (8, LANES), 0)
    pieces = []
    for start in range(0, ROWS, 8):
        piece = values[start : start + 8]
        first = start // WIN
        crossing = (first + 1) * WIN - start
        shifts = (first, first + 1)
        if by_width:
            one = pltpu.roll(piece, start - first * WIN, 1, stride=1, stride_axis=0)
        else:
            one = pltpu.roll(piece, first, 1) if first else piece
        if crossing < 8:
            if by_width:
                two = pltpu.roll(piece, LANES - crossing, 1)
                two = pltpu.roll(two, 0, 1, stride=1, stride_axis=0)
            else:
                two = pltpu.roll(piece, shifts[1], 1)
            one = jnp.where(sub < crossing, one, two)
        pieces.append(one)
    return jnp.concatenate(pieces, axis=0)


def normalize(values):
    centre = jnp.mean(values, axis=-1, keepdims=True)
    spread = values - centre
    variance = jnp.mean(spread * spread, axis=-1, keepdims=True)
    scale = lax.rsqrt(variance + EPSILON)
    return spread * scale, scale


def normalize_back(unit, scale, grad, gain):
    scaled = grad * gain
    mean_grad = jnp.mean(scaled, axis=-1, keepdims=True)
    mean_both = jnp.mean(scaled * unit, axis=-1, keepdims=True)
    return (scaled - mean_grad - unit * mean_both) * scale


def quarter_places(meta):
    mine, quarter = meta[0], meta[2]
    return [
        [4 * (mine ^ who) + (quarter ^ flip) for flip in (0, 2, 1, 3)] for who in (2, 3)
    ]


def start_copies(pairs, sems):
    copies = []
    for number, (source, target) in enumerate(pairs):
        copies.append(pltpu.make_async_copy(source, target, sems.at[number]))
    for copy in copies:
        copy.start()
    return copies


def wait_all(copies):
    for copy in copies:
        copy.wait()


def load_rows(meta, pieces, target, sems, first=0):
    own, near, *far = pieces
    columns = target.shape[1]
    quarter = target.shape[0] // 16
    pairs = []
    for source, who in ((own, 0), (near, 1)):
        start = pl.multiple_of(4 * (meta[0] ^ who) * quarter, 16)
        pairs.append((source, target.at[pl.ds(start, 4 * quarter), :]))
    for sources, places in zip(far, quarter_places(meta)):
        for index, place in enumerate(places):
            start = pl.multiple_of(place * quarter, 16)
            pairs.append(
                (sources.at[index, :, pl.ds(first, columns)], target.at[pl.ds(start, quarter), :])
            )
    return start_copies(pairs, sems)


def gather_quarters(first, block, staged, target, base, slabs):
    parts, rows, slots, width = block.shape
    lanes = width // LANES

    @pl.when(first)
    def _():
        for part in range(parts):
            values = block[part].astype(F32).reshape(rows * slots, width)
            for piece in range(lanes):
                staged[part * lanes + piece] = values[:, piece * LANES : (piece + 1) * LANES]
        target[:, parts * rows :, :] = jnp.zeros((slabs, ROWS - parts * rows, width), F32)

    for slab in range(slabs):
        for part in range(parts):
            for piece in range(lanes):
                target[
                    slab, part * rows : (part + 1) * rows, piece * LANES : (piece + 1) * LANES
                ] = staged[part * lanes + piece, pl.ds(base + slab, rows, stride=slots), :]


def scatter_quarters(last, full, staged, block, base, slabs):
    parts, rows, slots, width = block.shape
    lanes = width // LANES
    for slab in range(slabs):
        for part in range(parts):
            for piece in range(lanes):
                staged[part * lanes + piece, pl.ds(base + slab, rows, stride=slots), :] = full[
                    slab, part * rows : (part + 1) * rows, piece * LANES : (piece + 1) * LANES
                ]

    @pl.when(last)
    def _():
        for part in range(parts):
            for piece in range(lanes):
                values = staged[part * lanes + piece].reshape(rows, slots, LANES)
                block[part, :, :, piece * LANES : (piece + 1) * LANES] = values.astype(BF16)


def write_owned(source, meta, keep, send, across):
    height = keep.shape[1]
    for index in range(4):
        start = pl.multiple_of((meta[0] ^ index) * height, 16)
        target = send if index & across else keep
        target[index >> 1 if across == 1 else index & 1] = source[
            pl.ds(start, height), :
        ].astype(BF16)


ANY = pl.BlockSpec(memory_space=pl.ANY)


def whole(*shape):
    return pl.BlockSpec(shape, lambda *_: (0,) * len(shape))


def like(shape, dtype):
    return jax.ShapeDtypeStruct(shape, dtype)


def call(kernel, name, steps, scalars, ins, outs, scratch, cost, aliases=None):
    flops, moved, transcendentals = cost
    return pl.pallas_call(
        kernel,
        out_shape=tuple(item for item, _ in outs),
        grid_spec=pltpu.PrefetchScalarGridSpec(
            num_scalar_prefetch=len(scalars),
            grid=(steps,),
            in_specs=[spec for _, spec in ins],
            out_specs=tuple(spec for _, spec in outs),
            scratch_shapes=scratch,
        ),
        input_output_aliases={len(scalars) + k: v for k, v in (aliases or {}).items()},
        compiler_params=pltpu.CompilerParams(vmem_limit_bytes=VMEM_LIMIT),
        cost_estimate=pl.CostEstimate(
            flops=int(flops), bytes_accessed=int(moved), transcendentals=int(transcendentals)
        ),
        name=name,
    )(*scalars, *[item for item, _ in ins])


def group(count):
    return 2 if count % 2 == 0 else 1


def prepare_kernel(chunks, *refs):
    items, (expand, shrink), (vectors, packed) = refs[:8], refs[8:10], refs[10:]
    width = vectors.shape[1]
    row = 0
    for item in items:
        for start in range(0, item.shape[0], width):
            vectors[row : row + 1, :] = item[pl.ds(start, width)].reshape(1, width)
            row += 1
    quarter = expand.shape[0] // 4
    blocks = expand.shape[1] // width
    tall = shrink.shape[0] // (4 * chunks)
    for index in range(4):
        rows = slice(index * quarter, (index + 1) * quarter)
        for block in range(blocks):
            start = block * quarter
            packed[index, start : start + quarter, :] = expand[
                rows, block * width : (block + 1) * width
            ]
        for number in range(chunks):
            start = blocks * quarter + number * tall
            source = (4 * number + index) * tall
            packed[index, start : start + tall, :] = shrink[source : source + tall, :]


def prepare(chunks, items, weights):
    width = weights[1].shape[1]
    count = sum(item.shape[0] for item in items) // width
    total = sum(item.shape[0] * item.shape[1] for item in weights) // (4 * width)
    return call(
        functools.partial(prepare_kernel, chunks),
        "prepare",
        1,
        (),
        [(item, whole(*item.shape)) for item in (*items, *weights)],
        [
            (like((count, width), F32), whole(count, width)),
            (like((4, total, width), BF16), whole(4, total, width)),
        ],
        [],
        (0, 8 * total * width, 0),
    )


def collect_kernel(*refs):
    out = refs[-1]
    width = out.shape[1]
    singles, triples, expands, tables = refs[:6], refs[6:9], refs[9:12], refs[12:-1]
    out[...] = jnp.zeros_like(out)
    for row, item in enumerate(singles):
        out[row : row + 1, :] = item[...]
    size = width // 3
    for number, item in enumerate(triples):
        for part in range(3):
            row = TRIPLE_BIAS + part
            out[row : row + 1, number * size : (number + 1) * size] = item[
                :, part * size : (part + 1) * size
            ]
    for number, item in enumerate(expands):
        for part in range(item.shape[1] // size):
            row = EXPAND_BIAS + part
            out[row : row + 1, number * size : (number + 1) * size] = item[
                :, part * size : (part + 1) * size
            ]
    total = tables[0][...]
    for item in tables[1:]:
        total = total + item[...]
    for piece in range(3):
        out[TABLES : TABLES + 9, piece * LANES : (piece + 1) * LANES] = total[
            9 * piece : 9 * piece + 9, :
        ]


def collect(singles, triples, expands, tables):
    width = singles[0].shape[1]
    items = (*singles, *triples, *expands, *tables)
    return call(
        collect_kernel,
        "collect",
        1,
        (),
        [(item, whole(*item.shape)) for item in items],
        [(like((24, width), F32), whole(24, width))],
        [],
        (0, 16 * 24 * width, 0),
    )[0]


def attend_kernel(
    slabs, before, meta, windows, tokens, vectors, height, width_table, places, blocks, selectors,
    *rest,
):
    (
        rows_out, normed_out, triple_out, probs_out, attended_out,
        full, staged, weight, tables, masked_keys, sems,
    ) = rest[-11:]
    pieces = rest[:4]
    step = pl.program_id(0)
    base_slab = (step + before) * slabs
    width = full.shape[2]

    @pl.when(step == 0)
    def _():
        copies = load_rows(meta, pieces, weight, sems)
        tables[...] = build_tables(height, width_table, places, blocks)
        wait_all(copies)

    gather_quarters(step == 0, tokens, staged, full, base_slab, slabs)
    rows = full[...].reshape(slabs * ROWS, width)
    unit, _ = normalize(rows)
    normed = unit * vectors[FIRST_GAIN : FIRST_GAIN + 1] + vectors[FIRST_SHIFT : FIRST_SHIFT + 1]
    normed = normed.astype(BF16)
    rows_out[...] = rows.astype(BF16).reshape(slabs, ROWS, width)
    normed_out[...] = normed.reshape(slabs, ROWS, width)
    for part in range(3):
        columns = slice(part * width, (part + 1) * width)
        bias = vectors[TRIPLE_BIAS + part : TRIPLE_BIAS + part + 1]
        triple = dot(normed, weight[:, columns]) + bias
        triple_out[:, :, columns] = triple.astype(BF16).reshape(slabs, ROWS, width)

    lane = lax.broadcasted_iota(jnp.int32, (ROWS, LANES), 1)
    within = lane & (SEG - 1)
    upper = lane >= HD
    quads = HEADS // QUAD
    for slab in range(slabs):
        allowed = valid_rows(windows[meta[0], base_slab + slab])
        penalty = jnp.where((lane == WIN) & jnp.logical_not(allowed), PENALTY, 0.0).astype(BF16)
        for head in range(QUAD):
            masked_keys[slab, head] = selectors[head] + penalty

    sides = (jnp.logical_not(upper), upper)
    zero = jnp.zeros((ROWS, LANES), BF16)
    halves_of = lambda values, head: jnp.where(
        sides[head & 1], values[:, (head >> 1) * LANES : ((head >> 1) + 1) * LANES], zero
    )
    every = [(slab, head) for slab in range(slabs) for head in range(QUAD)]
    constant = jnp.where(lane == WIN, 1.0, 0.0)

    def one_quad(quad, carry):
        base = pl.multiple_of(quad * QUAD * HD, LANES)
        near = pl.multiple_of(base + width, LANES)
        far = pl.multiple_of(base + 2 * width, LANES)
        queries = [triple_out[slab, :, pl.ds(base, QUAD * HD)] for slab in range(slabs)]
        keys = [triple_out[slab, :, pl.ds(near, QUAD * HD)] for slab in range(slabs)]
        values = [triple_out[slab, :, pl.ds(far, QUAD * HD)] for slab in range(slabs)]
        terms = [dot(item, tables[...]) for item in queries]
        lefts = []
        for slab in range(slabs):
            high = roll_rows(terms[slab][:, :LANES], False)
            wide = roll_rows(terms[slab][:, LANES:], True)
            relative = jnp.where(
                within < WIN, high, jnp.where((within >= 16) & (within < 16 + WIN), wide, constant)
            ).astype(BF16)
            scaled = queries[slab] * jnp.asarray(HD**-0.5, BF16)
            lefts.append(
                [
                    jnp.concatenate([scaled[:, pair * LANES : (pair + 1) * LANES], relative], axis=1)
                    for pair in range(QUAD // 2)
                ]
            )
        scores = [
            dot_t(
                lefts[slab][head >> 1],
                jnp.concatenate([halves_of(keys[slab], head), masked_keys[slab, head]], axis=1),
            )
            for slab, head in every
        ]
        probs = []
        for (slab, head), score in zip(every, scores):
            maxima = jnp.max(score, axis=-1, keepdims=True)
            exponent = jnp.exp(score - maxima)
            summed = jnp.sum(exponent, axis=-1, keepdims=True)
            probs.append((exponent * (1.0 / summed)).astype(BF16))
            probs_out[slab, quad * QUAD + head] = probs[-1]
        parts = [dot(prob, halves_of(values[slab], head)) for (slab, head), prob in zip(every, probs)]
        for slab in range(slabs):
            mine = parts[slab * QUAD : (slab + 1) * QUAD]
            mixed = jnp.concatenate(
                [mine[2 * pair] + mine[2 * pair + 1] for pair in range(QUAD // 2)], axis=1
            )
            allowed = valid_rows(windows[meta[0], base_slab + slab])
            mixed = jnp.where(allowed, mixed, 0.0)
            attended_out[slab, :, pl.ds(base, QUAD * HD)] = mixed.astype(BF16)
        return carry

    lax.fori_loop(0, quads, one_quad, 0, unroll=True)


def attend(before, steps, meta, windows, tokens, vectors, tables, selectors, pieces, kept):
    parts, rows_dev, slots, width = tokens.shape
    slabs = group(slots)
    block3 = lambda columns: pl.BlockSpec((slabs, ROWS, columns), lambda i, *_: (i + before, 0, 0))
    rows = steps * slabs * ROWS
    ins = [(item, whole(*item.shape)) for item in (tokens, vectors, *tables, selectors)]
    ins += [(item, ANY) for item in pieces]
    aliases = {}
    if kept is not None:
        aliases = {len(ins) + n: n for n in range(len(kept))}
        ins += [(item, ANY) for item in kept]
    return call(
        functools.partial(attend_kernel, slabs, before),
        "attend",
        steps,
        (meta, windows),
        ins,
        [
            (like((slots, ROWS, width), BF16), block3(width)),
            (like((slots, ROWS, width), BF16), block3(width)),
            (like((slots, ROWS, 3 * width), BF16), block3(3 * width)),
            (
                like((slots, HEADS, ROWS, ROWS), BF16),
                pl.BlockSpec((slabs, HEADS, ROWS, ROWS), lambda i, *_: (i + before, 0, 0, 0)),
            ),
            (like((slots, ROWS, width), BF16), block3(width)),
        ],
        [
            pltpu.VMEM((slabs, ROWS, width), F32),
            pltpu.VMEM((parts * width // LANES, rows_dev * slots, LANES), F32),
            pltpu.VMEM((width, 3 * width), BF16),
            pltpu.VMEM((2 * LANES, 2 * LANES), BF16),
            pltpu.VMEM((slabs, QUAD, ROWS, LANES), BF16),
            pltpu.SemaphoreType.DMA((10,)),
        ],
        (
            6 * rows * width * width + steps * slabs * HEADS * 4 * ROWS * ROWS * 256,
            rows * (width * 16 + HEADS * 512) + width * width * 6,
            steps * slabs * HEADS * ROWS * ROWS,
        ),
        aliases,
    )


def project_kernel(
    slabs, first, meta, windows, attended, rows_in, grads, vectors, *rest,
):
    pieces = rest[:4]
    middle_out, normed_out, branch_out, shrink_bias_out, full, staged, weight, sems = rest[4:]
    step = pl.program_id(0)

    @pl.when(step == 0)
    def _():
        wait_all(load_rows(meta, pieces, weight, sems, first))
        shrink_bias_out[...] = jnp.zeros_like(shrink_bias_out)

    width = full.shape[2]
    count = slabs * ROWS
    middle = (
        rows_in[...].reshape(count, width).astype(F32)
        + dot(attended[...].reshape(count, width), weight[...])
        + vectors[OUTPUT_BIAS : OUTPUT_BIAS + 1]
    )
    unit, _ = normalize(middle)
    middle_out[...] = middle
    normed = unit * vectors[SECOND_GAIN : SECOND_GAIN + 1] + vectors[SECOND_SHIFT : SECOND_SHIFT + 1]
    normed_out[...] = normed.astype(BF16)
    gather_quarters(step == 0, grads, staged, full, step * slabs, slabs)
    for slab in range(slabs):
        allowed = valid_rows(windows[meta[0], step * slabs + slab])
        branch = jnp.where(allowed, full[slab], 0.0)
        branch_out[slab * ROWS : (slab + 1) * ROWS, :] = branch.astype(BF16)
        shrink_bias_out[...] += jnp.sum(branch, axis=0, keepdims=True)


def project(meta, windows, attended, rows_in, grads, vectors, pieces):
    parts, rows_dev, slots, width = grads.shape
    slabs = group(slots)
    block = pl.BlockSpec((slabs, ROWS, width), lambda i, *_: (i, 0, 0))
    flat = pl.BlockSpec((slabs * ROWS, width), lambda i, *_: (i, 0))
    rows = slots * ROWS
    return call(
        functools.partial(project_kernel, slabs, 3 * width),
        "project",
        slots // slabs,
        (meta, windows),
        [(attended, block), (rows_in, block)]
        + [(item, whole(*item.shape)) for item in (grads, vectors)]
        + [(item, ANY) for item in pieces],
        [
            (like((rows, width), F32), flat),
            (like((rows, width), BF16), flat),
            (like((rows, width), BF16), flat),
            (like((1, width), F32), whole(1, width)),
        ],
        [
            pltpu.VMEM((slabs, ROWS, width), F32),
            pltpu.VMEM((parts * width // LANES, rows_dev * slots, LANES), F32),
            pltpu.VMEM((width, width), BF16),
            pltpu.SemaphoreType.DMA((10,)),
        ],
        (2 * rows * width * width, rows * width * 14, 0),
    )


def gate_both(hidden):
    half = 0.5 * (1.0 + lax.erf(hidden * 0.7071067811865476))
    density = jnp.exp(hidden * hidden * -0.5) * 0.3989422804014327
    return hidden * half, half + hidden * density


def feed_kernel(number, first, unit, meta, normed, branch, vectors, *rest):
    pieces, rest = rest[:10], rest[10:]
    if not first:
        out_in, grad_in = rest[:2]
    out_acc, grad_acc, keep, send, bias_grad, expand, shrink, acc_e, acc_s, sems = rest[-10:]
    step = pl.program_id(0)
    last = pl.num_programs(0) - 1
    width, chunk = acc_e.shape
    blocks = chunk // unit

    @pl.when(step == 0)
    def _():
        pairs = []
        quarter, tall = expand.shape[1], shrink.shape[1]
        here = blocks * quarter + number * tall
        columns = pl.ds(number * unit, unit)
        for source, who in zip(pieces[:2], (0, 1)):
            places = pl.ds(4 * (meta[0] ^ who), 4)
            for block in range(blocks):
                pairs.append(
                    (
                        source.at[:, pl.ds(block * quarter, quarter), columns],
                        expand.at[places, :, pl.ds(block * unit, unit)],
                    )
                )
            pairs.append((source.at[:, pl.ds(here, tall), :], shrink.at[places]))
        for fetched, places in zip((pieces[2:6], pieces[6:10]), quarter_places(meta)):
            for source, place in zip(fetched, places):
                for block in range(blocks):
                    pairs.append(
                        (
                            source.at[pl.ds(block * quarter, quarter), columns],
                            expand.at[place, :, pl.ds(block * unit, unit)],
                        )
                    )
                pairs.append((source.at[pl.ds(here, tall), :], shrink.at[place]))
        copies = start_copies(pairs, sems)
        acc_e[...] = jnp.zeros_like(acc_e)
        acc_s[...] = jnp.zeros_like(acc_s)
        bias_grad[...] = jnp.zeros_like(bias_grad)
        wait_all(copies)

    rows = normed[...]
    grads = branch[...]
    bias = jnp.concatenate(
        [
            vectors[
                EXPAND_BIAS + block : EXPAND_BIAS + block + 1, number * unit : (number + 1) * unit
            ]
            for block in range(blocks)
        ],
        axis=1,
    )
    whole_expand = expand[...].reshape(width, chunk)
    whole_shrink = shrink[...].reshape(chunk, width)
    hidden = dot(rows, whole_expand) + bias
    d_active = dot_t(grads, whole_shrink)
    active, slope = gate_both(hidden)
    active = active.astype(BF16)
    back = (d_active * slope).astype(BF16)
    bias_grad[...] += jnp.sum(back.astype(F32), axis=0, keepdims=True)
    acc_s[...] += dot_rows(active, grads)
    acc_e[...] += dot_rows(rows, back)
    total_out = dot(active, whole_shrink)
    total_grad = dot_t(back, whole_expand)
    if first:
        out_acc[...] = total_out.astype(BF16)
        grad_acc[...] = total_grad.astype(BF16)
    else:
        out_acc[...] = (out_in[...].astype(F32) + total_out).astype(BF16)
        grad_acc[...] = (grad_in[...].astype(F32) + total_grad).astype(BF16)

    @pl.when(step == last)
    def _():
        height = width // 4
        third = height // 3
        for index in range(4):
            target = (send if index & 1 else keep).at[index >> 1]
            start = pl.multiple_of((meta[0] ^ index) * unit, 16)
            target[:unit, :] = acc_s[pl.ds(start, unit), :].astype(BF16)
            start = pl.multiple_of((meta[0] ^ index) * height, 16)
            target[unit : unit + height, :] = acc_e[pl.ds(start, height), :width].astype(BF16)
            for piece in range(3):
                here = pl.multiple_of(start + piece * third, 16)
                target[unit + height :, piece * unit : (piece + 1) * unit] = acc_e[
                    pl.ds(here, third), width:
                ].astype(BF16)


def feed(number, count, meta, normed, branch, vectors, pieces, kept):
    rows, width = normed.shape
    chunk = 4 * width // count
    unit = chunk // 4
    block_rows = 2 * ROWS
    block = pl.BlockSpec((block_rows, width), lambda i, *_: (i, 0))
    ins = [(normed, block), (branch, block), (vectors, whole(*vectors.shape))]
    ins += [(item, ANY) for item in pieces]
    aliases = {}
    if kept is not None:
        aliases = {len(ins) + n: n for n in range(2)}
        ins += [(item, block) for item in kept]
    payload = (2, unit + unit, width)
    return call(
        functools.partial(feed_kernel, number, kept is None, unit),
        "feed",
        rows // block_rows,
        (meta,),
        ins,
        [
            (like((rows, width), BF16), block),
            (like((rows, width), BF16), block),
            (like(payload, BF16), whole(*payload)),
            (like(payload, BF16), whole(*payload)),
            (like((1, chunk), F32), whole(1, chunk)),
        ],
        [
            pltpu.VMEM((16, width // 16, chunk), BF16),
            pltpu.VMEM((16, chunk // 16, width), BF16),
            pltpu.VMEM((width, chunk), F32),
            pltpu.VMEM((chunk, width), F32),
            pltpu.SemaphoreType.DMA((64,)),
        ],
        (12 * rows * width * chunk, rows * width * 12 + width * chunk * 8, 2 * rows * chunk),
        aliases,
    )


def middle_kernel(
    slabs, first, meta, windows, middle, out_acc, grad_acc, branch, attended, vectors,
    *rest,
):
    pieces = rest[:4]
    (
        result_out, d_middle_out, d_attended_out, keep, send, output_bias_grad, gain_grad,
        shift_grad, full, staged, weight, acc, sems,
    ) = rest[4:]
    step = pl.program_id(0)
    last = pl.num_programs(0) - 1

    @pl.when(step == 0)
    def _():
        copies = load_rows(meta, pieces, weight, sems, first)
        acc[...] = jnp.zeros_like(acc)
        output_bias_grad[...] = jnp.zeros_like(output_bias_grad)
        gain_grad[...] = jnp.zeros_like(gain_grad)
        shift_grad[...] = jnp.zeros_like(shift_grad)
        wait_all(copies)

    width = full.shape[2]
    count = slabs * ROWS
    rows = middle[...]
    result = rows + out_acc[...].astype(F32) + vectors[SHRINK_BIAS : SHRINK_BIAS + 1]
    full[...] = result.reshape(slabs, ROWS, width)
    scatter_quarters(step == last, full, staged, result_out, step * slabs, slabs)
    unit, scale = normalize(rows)
    grad = grad_acc[...].astype(F32)
    gain_grad[...] += jnp.sum(grad * unit, axis=0, keepdims=True)
    shift_grad[...] += jnp.sum(grad, axis=0, keepdims=True)
    d_middle = branch[...].astype(F32) + normalize_back(
        unit, scale, grad, vectors[SECOND_GAIN : SECOND_GAIN + 1]
    )
    d_output = d_middle.astype(BF16)
    d_middle_out[...] = d_output
    output_bias_grad[...] += jnp.sum(d_output.astype(F32), axis=0, keepdims=True)
    acc[...] += dot_rows(attended[...].reshape(count, width), d_output)
    d_attended = dot_t(d_output, weight[...]).reshape(slabs, ROWS, width)
    for slab in range(slabs):
        allowed = valid_rows(windows[meta[0], step * slabs + slab])
        d_attended_out[slab] = jnp.where(allowed, d_attended[slab], 0.0).astype(BF16)

    @pl.when(step == last)
    def _():
        write_owned(acc, meta, keep, send, 1)


def middle_back(meta, windows, rows_dev, middle, out_acc, grad_acc, branch, attended, vectors, pieces):
    slots, _, width = attended.shape
    parts = WROWS // rows_dev
    slabs = group(slots)
    block = pl.BlockSpec((slabs, ROWS, width), lambda i, *_: (i, 0, 0))
    flat = pl.BlockSpec((slabs * ROWS, width), lambda i, *_: (i, 0))
    rows = slots * ROWS
    vec = (like((1, width), F32), whole(1, width))
    payload = (2, width // 4, width)
    quarter = (parts, rows_dev, slots, width)
    return call(
        functools.partial(middle_kernel, slabs, 3 * width),
        "middle",
        slots // slabs,
        (meta, windows),
        [
            (middle, flat), (out_acc, flat), (grad_acc, flat), (branch, flat), (attended, block),
            (vectors, whole(*vectors.shape)),
        ]
        + [(item, ANY) for item in pieces],
        [
            (like(quarter, BF16), whole(*quarter)),
            (like((rows, width), BF16), flat),
            (like((slots, ROWS, width), BF16), block),
            (like(payload, BF16), whole(*payload)),
            (like(payload, BF16), whole(*payload)),
            vec,
            vec,
            vec,
        ],
        [
            pltpu.VMEM((slabs, ROWS, width), F32),
            pltpu.VMEM((parts * width // LANES, rows_dev * slots, LANES), F32),
            pltpu.VMEM((width, width), BF16),
            pltpu.VMEM((width, width), F32),
            pltpu.SemaphoreType.DMA((10,)),
        ],
        (4 * rows * width * width, rows * width * 18, 0),
    )


def attend_back_kernel(
    slabs, across, meta, normed, queries_in, keys_in, values_in, probs_in, d_mixed_in, mixed_in,
    height, width_table, places, blocks, selectors, sums,
    d_queries, d_keys, d_values, keep, send, bias_grad, table_out, grads, acc, tables, table_grad,
):
    step = pl.program_id(0)
    last = pl.num_programs(0) - 1
    wide4 = QUAD * HD

    @pl.when(step == 0)
    def _():
        acc[...] = jnp.zeros_like(acc)
        bias_grad[...] = jnp.zeros_like(bias_grad)
        table_grad[...] = jnp.zeros_like(table_grad)
        tables[...] = build_tables(height, width_table, places, blocks)

    lane = lax.broadcasted_iota(jnp.int32, (ROWS, LANES), 1)
    within = lane & (SEG - 1)
    upper = lane >= HD
    zero = jnp.zeros((ROWS, LANES), BF16)

    sides = (jnp.logical_not(upper), upper)
    halves_of = lambda items, head: jnp.where(
        sides[head & 1], items[:, (head >> 1) * LANES : ((head >> 1) + 1) * LANES], zero
    )
    minus = [
        jnp.where((lane == 2 * head) | (lane == 2 * head + 1), -1.0, 0.0).astype(BF16)
        for head in range(QUAD)
    ]
    every = [(slab, head) for slab in range(slabs) for head in range(QUAD)]
    lefts = []
    for slab in range(slabs):
        d_mixed = d_mixed_in[slab]
        product = d_mixed.astype(F32) * mixed_in[slab].astype(F32)
        product_high = product.astype(BF16)
        product_low = (product - product_high.astype(F32)).astype(BF16)
        inner = dot(product_high, sums[...]) + dot(product_low, sums[...])
        inner_high = inner.astype(BF16)
        inner_low = (inner - inner_high.astype(F32)).astype(BF16)
        inner = jnp.where((lane & 1) == 0, inner_high, inner_low)
        lefts.append(
            [
                jnp.concatenate([d_mixed[:, pair * LANES : (pair + 1) * LANES], inner], axis=1)
                for pair in range(QUAD // 2)
            ]
        )
    d_probs = [
        dot_t(
            lefts[slab][head >> 1],
            jnp.concatenate([halves_of(values_in[slab], head), minus[head]], axis=1),
        )
        for slab, head in every
    ]
    parts_v = [
        dot_rows(probs_in[slab, head], halves_of(d_mixed_in[slab], head)) for slab, head in every
    ]
    d_scores = [
        (probs_in[slab, head].astype(F32) * item).astype(BF16)
        for (slab, head), item in zip(every, d_probs)
    ]
    backs = [
        dot(
            item,
            jnp.concatenate([halves_of(keys_in[slab], head), selectors[head]], axis=1),
        )
        for (slab, head), item in zip(every, d_scores)
    ]
    parts_k = [
        dot_rows(item, halves_of(queries_in[slab], head))
        for (slab, head), item in zip(every, d_scores)
    ]
    scale = HD**-0.5
    joined = lambda items: jnp.concatenate(
        [items[2 * pair] + items[2 * pair + 1] for pair in range(QUAD // 2)], axis=1
    )
    for slab in range(slabs):
        mine = slice(slab * QUAD, (slab + 1) * QUAD)
        d_relative = backs[slab * QUAD][:, LANES:]
        for head in range(1, QUAD):
            d_relative = d_relative + backs[slab * QUAD + head][:, LANES:]
        high = roll_rows(jnp.where(within < WIN, d_relative, 0.0), False)
        wide = roll_rows(jnp.where((within >= 16) & (within < 16 + WIN), d_relative, 0.0), True)
        d_terms = jnp.concatenate([high, wide], axis=1).astype(BF16)
        dq = joined([item[:, :LANES] for item in backs[mine]]) * scale
        dq = (dq + dot_t(d_terms, tables[...])).astype(BF16)
        table_grad[...] += dot_rows(queries_in[slab], d_terms)
        dk = (joined(parts_k[mine]) * scale).astype(BF16)
        dv = joined(parts_v[mine]).astype(BF16)
        d_queries[slab] = dq
        d_keys[slab] = dk
        d_values[slab] = dv
        grads[slab] = jnp.concatenate([dq, dk, dv], axis=1)

    width = normed.shape[2]
    both = grads[...].reshape(slabs * ROWS, 3 * wide4)
    bias_grad[...] += jnp.sum(both.astype(F32), axis=0, keepdims=True)
    acc[...] += dot_rows(normed[...].reshape(slabs * ROWS, width), both)

    @pl.when(step == last)
    def _():
        write_owned(acc, meta, keep, send, across)
        masked = table_grad[...] * blocks[...].astype(F32)
        folded = masked[:HD]
        for head in range(1, QUAD):
            folded = folded + masked[head * HD : (head + 1) * HD]
        high = folded.astype(BF16)
        low = (folded - high.astype(F32)).astype(BF16)
        for which in range(2):
            table_out[:, which * HD : (which + 1) * HD] = dot_t(places[which], high) + dot_t(
                places[which], low
            )


def attend_back(quad, across, meta, normed, triple, probs, d_mixed, mixed, tables, selectors, sums):
    slots, _, width = normed.shape
    slabs = group(slots)
    wide4 = QUAD * HD
    quads = HEADS // QUAD
    column = lambda where: pl.BlockSpec((slabs, ROWS, wide4), lambda i, *_: (i, 0, where))
    narrow = (
        like((slots, ROWS, wide4), BF16),
        pl.BlockSpec((slabs, ROWS, wide4), lambda i, *_: (i, 0, 0)),
    )
    rows = slots * ROWS
    payload = (2, width // 4, 3 * wide4)
    return call(
        functools.partial(attend_back_kernel, slabs, across),
        "attend_back",
        slots // slabs,
        (meta,),
        [
            (normed, pl.BlockSpec((slabs, ROWS, width), lambda i, *_: (i, 0, 0))),
            (triple, column(quad)),
            (triple, column(quads + quad)),
            (triple, column(2 * quads + quad)),
            (probs, pl.BlockSpec((slabs, QUAD, ROWS, ROWS), lambda i, *_: (i, quad, 0, 0))),
            (d_mixed, column(quad)),
            (mixed, column(quad)),
        ]
        + [(item, whole(*item.shape)) for item in (*tables, selectors, sums)],
        [
            narrow,
            narrow,
            narrow,
            (like(payload, BF16), whole(*payload)),
            (like(payload, BF16), whole(*payload)),
            (like((1, 3 * wide4), F32), whole(1, 3 * wide4)),
            (like((REL, 2 * HD), F32), whole(REL, 2 * HD)),
        ],
        [
            pltpu.VMEM((slabs, ROWS, 3 * wide4), BF16),
            pltpu.VMEM((width, 3 * wide4), F32),
            pltpu.VMEM((2 * LANES, 2 * LANES), BF16),
            pltpu.VMEM((2 * LANES, 2 * LANES), F32),
        ],
        (
            2 * rows * width * 3 * wide4 + slots * QUAD * 8 * ROWS * ROWS * 256,
            rows * (width * 2 + wide4 * 16 + QUAD * 512),
            0,
        ),
    )


def first_kernel(slabs, meta, rows_in, d_middle, vectors, *rest):
    grads, pieces = rest[:9], rest[9:13]
    tokens_out, gain_grad, shift_grad, full, staged, weight, sems = rest[13:]
    step = pl.program_id(0)
    last = pl.num_programs(0) - 1

    @pl.when(step == 0)
    def _():
        copies = load_rows(meta, pieces, weight, sems)
        gain_grad[...] = jnp.zeros_like(gain_grad)
        shift_grad[...] = jnp.zeros_like(shift_grad)
        wait_all(copies)

    width = full.shape[2]
    count = slabs * ROWS
    wide4 = QUAD * HD
    both = jnp.concatenate([grad[...].reshape(count, wide4) for grad in grads], axis=1)
    total = dot_t(both, weight[...])
    unit, scale = normalize(rows_in[...].reshape(count, width).astype(F32))
    gain_grad[...] += jnp.sum(total * unit, axis=0, keepdims=True)
    shift_grad[...] += jnp.sum(total, axis=0, keepdims=True)
    back = normalize_back(unit, scale, total, vectors[FIRST_GAIN : FIRST_GAIN + 1])
    full[...] = (d_middle[...].astype(F32) + back).reshape(slabs, ROWS, width)
    scatter_quarters(step == last, full, staged, tokens_out, step * slabs, slabs)


def first_back(before, steps, meta, rows_dev, rows_in, d_middle, vectors, grads, pieces):
    slots, _, width = rows_in.shape
    parts = WROWS // rows_dev
    slabs = group(slots)
    wide4 = QUAD * HD
    block = pl.BlockSpec((slabs, ROWS, width), lambda i, *_: (i + before, 0, 0))
    flat = pl.BlockSpec((slabs * ROWS, width), lambda i, *_: (i + before, 0))
    narrow = pl.BlockSpec((slabs, ROWS, wide4), lambda i, *_: (i + before, 0, 0))
    rows = steps * slabs * ROWS
    quarter = (parts, rows_dev, steps * slabs, width)
    return call(
        functools.partial(first_kernel, slabs),
        "first_back",
        steps,
        (meta,),
        [(rows_in, block), (d_middle, flat), (vectors, whole(*vectors.shape))]
        + [(item, narrow) for item in grads]
        + [(item, ANY) for item in pieces],
        [(like(quarter, BF16), whole(*quarter))] + [(like((1, width), F32), whole(1, width))] * 2,
        [
            pltpu.VMEM((slabs, ROWS, width), F32),
            pltpu.VMEM((parts * width // LANES, rows_dev * steps * slabs, LANES), F32),
            pltpu.VMEM((width, 3 * width), BF16),
            pltpu.SemaphoreType.DMA((10,)),
        ],
        (6 * rows * width * width, rows * width * 14, 0),
    )


def join_halves(meta, items, staged):
    upper = meta[1] > 0
    for number, both in enumerate(staged):
        mine, other = items[2 * number], items[2 * number + 1]
        half = mine.shape[0]

        @pl.when(upper)
        def _():
            both[:half] = other[...]
            both[half:] = mine[...]

        @pl.when(jnp.logical_not(upper))
        def _():
            both[:half] = mine[...]
            both[half:] = other[...]


def finish_feed_kernel(unit, pairs, meta, *refs):
    items, (expand_out, shrink_out), staged = (
        refs[: 2 * pairs], refs[2 * pairs : 2 * pairs + 2], refs[2 * pairs + 2 :]
    )
    join_halves(meta, items, staged)
    shard, width = expand_out.shape[0], shrink_out.shape[1]
    third = shard // 3
    parts = width // shard
    for number, both in enumerate(staged):
        here = number * unit
        shrink_out[here : here + unit, :] = both[:unit, :].astype(F32)
        for block in range(parts - 1):
            start = block * width + here
            expand_out[:, start : start + unit] = both[
                unit : unit + shard, block * unit : (block + 1) * unit
            ].astype(F32)
        start = (parts - 1) * width + here
        for piece in range(3):
            expand_out[piece * third : (piece + 1) * third, start : start + unit] = both[
                unit + shard :, piece * unit : (piece + 1) * unit
            ].astype(F32)


def finish_rest_kernel(pairs, meta, *refs):
    items, small, refs = refs[: 2 * pairs], refs[2 * pairs], refs[2 * pairs + 1 :]
    (triple_out, output_out), refs = refs[:2], refs[2:]
    vectors, tables, staged = refs[:8], refs[8:10], refs[10:]
    join_halves(meta, items, staged)
    shard, width = output_out.shape
    output_out[...] = staged[0][:shard, :].astype(F32)
    wide4 = QUAD * HD
    for quad, both in enumerate(staged):
        values = both[shard:, :] if quad == 0 else both[...]
        for part in range(3):
            start = part * width + quad * wide4
            triple_out[:, start : start + wide4] = values[
                :, part * wide4 : (part + 1) * wide4
            ].astype(F32)
    row = 0
    for item in vectors:
        for start in range(0, item.shape[0], width):
            item[pl.ds(start, width)] = small[row : row + 1, :].reshape(width)
            row += 1
    for which, item in enumerate(tables):
        for piece in range(3):
            start = piece * LANES + which * HD
            item[9 * piece : 9 * piece + 9, :] = small[TABLES : TABLES + 9, start : start + HD]


def finish(kernel, name, meta, shares, others, outs):
    items = [item for pair in shares for item in pair]
    return call(
        kernel,
        name,
        1,
        (meta,),
        [(item, whole(*item.shape)) for item in (*items, *others)],
        [(like(item.shape, F32), whole(*item.shape)) for item in outs],
        [pltpu.VMEM((2 * mine.shape[0], mine.shape[1]), BF16) for mine, _ in shares],
        (0, sum(6 * item.size for item in items), 0),
    )


def swap(values, axis, bits):
    count = lax.axis_size(axis)
    return lax.ppermute(values, axis, [(n, n ^ bits) for n in range(count)])


def swap_diagonal(values):
    across = lax.axis_size("seq")
    count = lax.axis_size("dp") * across
    perm = [(n, (n // across ^ 1) * across + (n % across ^ 1)) for n in range(count)]
    return lax.ppermute(values, ("dp", "seq"), perm)


def spread(far):
    return far, swap(far, "dp", 1), swap(far, "seq", 1), swap_diagonal(far)


def exchange_windows(values):
    return lax.all_to_all(values, "tensor", split_axis=0, concat_axis=0, tiled=True)


def after(values, *others):
    return lax.optimization_barrier((values, *others))[0]


def far_quarter(packed):
    which = 2 * (lax.axis_index("dp") & 1) + (lax.axis_index("seq") & 1)
    return lax.dynamic_index_in_dim(packed, which, axis=0, keepdims=False)


def add(*items):
    total = items[0].astype(F32)
    for item in items[1:]:
        total = total + item.astype(F32)
    return total.astype(BF16)


def halves(axis):
    out, bit = [], 1
    while bit < lax.axis_size(axis):
        out.append(bit)
        bit *= 2
    return out


def reduce_stages(payloads, plan):
    bits_of = {"c": 1, "y": 2}
    totals = []
    while True:
        keep, send, more = payloads.pop(0)
        (far,) = yield [(send, "tensor", bits_of[plan[0]])]
        totals.append(add(keep, far))
        if not more:
            break
    total = totals[0] if len(totals) == 1 else jnp.concatenate(totals, axis=1)
    spot = lax.axis_index("dp")
    place = lax.axis_index("seq")

    def split(values, upper):
        size = values.shape[-2] // 2
        low, high = values[..., :size, :], values[..., size:, :]
        return jnp.where(upper, high, low), jnp.where(upper, low, high)

    def join(mine, far, upper):
        return jnp.concatenate([jnp.where(upper, far, mine), jnp.where(upper, mine, far)], axis=0)

    for letter in plan[1:]:
        if letter in bits_of:
            (far,) = yield [(total[1], "tensor", bits_of[letter])]
            total = add(total[0], far)
        elif letter == "x":
            for bit in halves("dp"):
                near, far = split(total, (spot & bit) > 0)
                (far,) = yield [(far, "dp", bit)]
                total = add(near, far)
        else:
            if letter == "s":
                near, far = split(total, (place & 1) > 0)
                (far,) = yield [(far, "seq", 1)]
                total = add(near, far)
            for bit in halves("seq"):
                if letter == "s" and bit == 1:
                    continue
                (far,) = yield [(total, "seq", bit)]
                total = add(total, far)
            if letter == "s":
                (far,) = yield [(total, "seq", 1)]
                total = join(total, far, (place & 1) > 0)
    for bit in reversed(halves("dp")):
        (far,) = yield [(total, "dp", bit)]
        if bit > 1:
            total = join(total, far, (spot & bit) > 0)
    return total, far


def sum_stages(values):
    steps = [(axis, bit) for axis in ("tensor", "dp", "seq") for bit in halves(axis)]
    steps = [("tensor", 2)] + [item for item in steps if item != ("tensor", 2)]
    for axis, bit in steps:
        (far,) = yield [(values, axis, bit)]
        values = values + far
    return (values,)


class Exchanges:
    def __init__(self):
        self.running = []
        self.done = {}

    def begin(self, name, stages):
        self.running.append([name, stages, None])

    def step(self, names, token, meta, *extra):
        asked, ended = [], []
        chosen = [entry for entry in self.running if names is None or entry[0] in names]
        arrived = [item for entry in chosen for item in (entry[2] or ())]
        if token is not None and arrived:
            token, *arrived = lax.optimization_barrier((token, *arrived))
        arrived = iter(arrived)
        for entry in chosen:
            name, stages, waiting = entry
            mine = None if waiting is None else [next(arrived) for _ in waiting]
            try:
                asked.append((entry, stages.send(mine)))
            except StopIteration as stop:
                ended.append((name, stop.value))
                self.running.remove(entry)
        values = [item[0] for _, wanted in asked for item in wanted]
        finished = [item for _, pair in ended for item in pair]
        if meta is not None:
            count = len(values)
            meta, *rest = lax.optimization_barrier((meta, *values, *finished, *extra))
            values = rest[:count]
            finished = rest[count : count + len(finished)]
            extra = rest[count + len(finished) :]
        values, finished = iter(values), iter(finished)
        for entry, wanted in asked:
            entry[2] = [swap(next(values), axis, bits) for _, axis, bits in wanted]
        for name, pair in ended:
            self.done[name] = tuple(next(finished) for _ in pair)
        return (token, meta, *extra)

    def finish(self):
        while self.running:
            self.step(None, None, None)


def local(
    tokens,
    out_grad,
    slot_window,
    first_gain,
    first_shift,
    triple_weight,
    triple_bias,
    height_table,
    width_table,
    output_weight,
    output_bias,
    second_gain,
    second_shift,
    expand_weight,
    expand_bias,
    shrink_weight,
    shrink_bias,
):
    micros, images, slots, rows_dev, width = tokens.shape
    parts = lax.axis_size("tensor")
    mine = lax.axis_index("tensor")
    shard = width // parts
    chunks = 3
    unit = width // chunks
    bit = lax.axis_index("dp") & 1
    quarter = 2 * bit + (lax.axis_index("seq") & 1)
    meta = jnp.where(
        jnp.arange(3) == 0, mine, jnp.where(jnp.arange(3) == 1, bit, quarter)
    ).astype(jnp.int32)

    by_image = lambda values: jnp.swapaxes(values, 2, 3).reshape(parts, rows_dev, slots, width)
    to_image = lambda values: jnp.swapaxes(
        values.reshape(micros, images, rows_dev, slots, width), 2, 3
    )
    windows = slot_window.reshape(parts, slots)

    far = jnp.concatenate(
        [
            far_quarter(triple_weight.reshape(4, shard // 4, -1)),
            far_quarter(output_weight.reshape(4, shard // 4, -1)),
        ],
        axis=1,
    )
    far = swap(far, "tensor", 2)
    near_triple = swap(triple_weight, "tensor", 1)
    near_output = swap(output_weight, "tensor", 1)
    vectors, packed_rest = prepare(
        chunks,
        (
            first_gain, first_shift, output_bias, second_gain, second_shift, shrink_bias,
            triple_bias, expand_bias,
        ),
        (expand_weight, shrink_weight),
    )
    sums = np.zeros((QUAD * HD, LANES), np.float32)
    for head in range(QUAD):
        sums[head * HD : (head + 1) * HD, 2 * head : 2 * head + 2] = 1.0
    sums = jnp.asarray(sums, BF16)
    ahead = (height_table, width_table, table_places(False), head_blocks(False))
    behind = (height_table, width_table, table_places(True), head_blocks(True))
    far, vectors, packed_rest, meta, own_tokens = lax.optimization_barrier(
        (far, vectors, packed_rest, meta, by_image(tokens))
    )
    rows_in = exchange_windows(own_tokens)
    fetched = jnp.stack(spread(far))
    crossed = swap(fetched, "tensor", 1)

    packed, rows_in, fetched, crossed = lax.optimization_barrier(
        (packed_rest, rows_in, fetched, crossed)
    )
    triple_pieces = (triple_weight, near_triple, fetched, crossed)
    output_pieces = (output_weight, near_output, fetched, crossed)
    far = swap(far_quarter(packed), "tensor", 2)
    near = swap(packed, "tensor", 1)
    steps = slots // group(slots)
    early = max(1, steps // 4)
    selectors = key_selectors(False)
    kept = attend(
        0, early, meta, windows, rows_in, vectors, ahead, selectors, triple_pieces, None
    )
    kept = list(kept)
    kept[4], far, own_grads = lax.optimization_barrier((kept[4], far, by_image(out_grad)))
    meta, far, near, own_grads = lax.optimization_barrier((meta, far, near, own_grads))
    grads_in = exchange_windows(own_grads)
    fetched = spread(far)
    crossed = (swap(far, "tensor", 1),)
    if early < steps:
        kept = attend(
            early, steps - early, meta, windows, rows_in, vectors, ahead, selectors,
            triple_pieces, kept,
        )
    full_rows, normed, triple, probs, attended = kept
    attended, *others = lax.optimization_barrier((attended, *fetched[1:]))
    meta, *others = lax.optimization_barrier((meta, *others))
    crossed += tuple(swap(item, "tensor", 1) for item in others)
    middle_stage = project(
        meta, windows, attended, full_rows, grads_in, vectors, output_pieces
    )
    shrink_bias_grad = middle_stage[3]
    rest_pieces = (packed, near, far, *others, *crossed)
    middle, normed2, branch = middle_stage[:3]
    exchanges = Exchanges()
    kept = None
    expand_bias_grads = []
    for number in range(chunks):
        *kept, keep, send, bias_grad = feed(
            number, chunks, meta, normed2, branch, vectors, rest_pieces, kept
        )
        plan = ("cyxz", "cyxz", "cxyz")[number]
        exchanges.begin(("feed", number), reduce_stages([(keep, send, False)], plan))
        bias_grad, meta = exchanges.step(None, bias_grad, meta)
        expand_bias_grads.append(bias_grad)

    result, d_middle, d_attended, keep, send, output_bias_grad, gain2_grad, shift2_grad = (
        middle_back(
            meta, windows, rows_dev, middle, *kept, branch, attended, vectors, output_pieces
        )
    )
    payloads = [(keep, send, True)]
    exchanges.begin(("rest", 0), reduce_stages(payloads, "cyxs"))
    output_bias_grad, meta = exchanges.step(None, output_bias_grad, meta)
    result = exchange_windows(result)

    quad_grads, triple_bias_grads, table_grads = [], [], []
    for quad in range(HEADS // QUAD):
        dq, dk, dv, keep, send, bias_grad, table_grad = attend_back(
            quad, 2 if quad == 2 else 1, meta, normed, triple, probs, d_attended, attended, behind, key_selectors(True), sums
        )
        if quad == 0:
            payloads.append((keep, send, False))
        else:
            plan = "cyxz" if quad == 1 else "ycxz"
            exchanges.begin(("rest", quad), reduce_stages([(keep, send, False)], plan))
        if quad == 1:
            bias_grad, meta, result = exchanges.step(None, bias_grad, meta, result)
        else:
            bias_grad, meta = exchanges.step(None, bias_grad, meta)
        quad_grads.append((dq, dk, dv))
        triple_bias_grads.append(bias_grad)
        table_grads.append(table_grad)
    wide4 = QUAD * HD
    grads9 = [quad_grads[quad][part] for part in range(3) for quad in range(HEADS // QUAD)]
    token_grad, gain1_grad, shift1_grad = first_back(
        0, steps, meta, rows_dev, full_rows, d_middle, vectors, grads9, triple_pieces
    )
    result = to_image(result)
    gain1_grad, _ = exchanges.step(None, gain1_grad, None)
    small = collect(
        (gain1_grad, shift1_grad, output_bias_grad, gain2_grad, shift2_grad, shrink_bias_grad),
        triple_bias_grads,
        expand_bias_grads,
        table_grads,
    )
    exchanges.begin("small", sum_stages(small))
    exchanges.step(["small"], None, None)
    first_far = exchanges.running[-1][2][0]
    tokens_gradient = to_image(exchange_windows(after(token_grad, first_far)))
    exchanges.finish()
    shares = [exchanges.done["feed", number] for number in range(chunks)]
    expand_gradient, shrink_gradient = finish(
        functools.partial(finish_feed_kernel, unit, chunks),
        "finish_feed",
        meta,
        shares,
        (),
        (expand_weight, shrink_weight),
    )
    shares = [exchanges.done["rest", number] for number in range(HEADS // QUAD)]
    triple_gradient, output_gradient, *outs, high, wide = finish(
        functools.partial(finish_rest_kernel, len(shares)),
        "finish_rest",
        meta,
        shares,
        exchanges.done["small"],
        (
            triple_weight, output_weight, first_gain, first_shift, output_bias, second_gain,
            second_shift, shrink_bias, triple_bias, expand_bias, height_table, width_table,
        ),
    )
    return (
        result,
        tokens_gradient,
        outs[0],
        outs[1],
        triple_gradient,
        outs[6],
        high,
        wide,
        output_gradient,
        outs[2],
        outs[3],
        outs[4],
        expand_gradient,
        outs[7],
        shrink_gradient,
        outs[5],
    )


def solution(mesh):
    split = P(None, "dp", "seq", "tensor", None)
    rows = P("tensor", None)
    return jax.shard_map(
        local,
        mesh=mesh,
        in_specs=(
            split, split, P(None, "dp", "seq"), P(), P(), rows, P(), P(), P(), rows, P(), P(), P(),
            rows, P(), rows, P(),
        ),
        out_specs=(
            split, split, P(), P(), rows, P(), P(), P(), rows, P(), P(), P(), rows, P(), rows, P(),
        ),
        check_vma=False,
    )
```

```python
import functools

import jax
import jax.numpy as jnp
import numpy as np
from jax import lax
from jax.experimental import pallas as pl
from jax.experimental.pallas import tpu as pltpu
from jax.sharding import PartitionSpec as P

HEADS = 12
HD = 64
WIN = 14
GRID = 64
WGRID = 5
WROWS = WIN * WIN
ROWS = 200
QUAD = 4
LANES = 128
REL = 2 * WIN - 1
SEG = 32
EPSILON = 1e-06
PENALTY = -1e9

F32 = jnp.float32
BF16 = jnp.bfloat16
FIRST_GAIN, FIRST_SHIFT, OUTPUT_BIAS, SECOND_GAIN, SECOND_SHIFT, SHRINK_BIAS = range(6)
TRIPLE_BIAS, EXPAND_BIAS, TABLES = 6, 9, 13
VMEM_LIMIT = 58 * 1024 * 1024


def dot(left, right):
    return lax.dot_general(left, right, (((1,), (0,)), ((), ())), preferred_element_type=F32)


def dot_t(left, right):
    return lax.dot_general(left, right, (((1,), (1,)), ((), ())), preferred_element_type=F32)


def dot_rows(left, right):
    return lax.dot_general(left, right, (((0,), (0,)), ((), ())), preferred_element_type=F32)


def key_selectors(mirrored):
    out = np.zeros((QUAD, ROWS, LANES), np.float32)
    for head in range(QUAD):
        for key in range(WROWS):
            high, wide = key // WIN, key % WIN
            if mirrored:
                high, wide = WIN - 1 - high, WIN - 1 - wide
            out[head, key, SEG * head + high] = 1.0
            out[head, key, SEG * head + 16 + wide] = 1.0
    return jnp.asarray(out, BF16)


def table_places(mirrored):
    out = np.zeros((2, REL, 2 * LANES), np.float32)
    for head in range(QUAD):
        for row in range(REL):
            if mirrored:
                out[0, row, SEG * head + row] = 1.0
                out[1, row, LANES + (SEG * head + 16 + row) % LANES] = 1.0
            else:
                out[0, REL - 1 - row, (SEG * head + row - 13) % LANES] = 1.0
                out[1, REL - 1 - row, LANES + (SEG * head + row + 3) % LANES] = 1.0
    return jnp.asarray(out, BF16)


def head_blocks(mirrored):
    out = np.zeros((QUAD * HD, 2 * LANES), np.float32)
    for head in range(QUAD):
        rows = slice(head * HD, (head + 1) * HD)
        for row in range(REL):
            if mirrored:
                out[rows, SEG * head + row] = 1.0
                out[rows, LANES + (SEG * head + 16 + row) % LANES] = 1.0
            else:
                out[rows, (SEG * head + row - 13) % LANES] = 1.0
                out[rows, LANES + (SEG * head + row + 3) % LANES] = 1.0
    return jnp.asarray(out, BF16)


def valid_rows(window):
    high_place = (window * 13) >> 6
    wide_place = window - high_place * WGRID
    inside = window < WGRID * WGRID
    row = lax.broadcasted_iota(jnp.int32, (ROWS, 1), 0)
    high = (row * 4682) >> 16
    wide = row - high * WIN
    high_limit = jnp.where(inside, GRID - high_place * WIN, 0)
    return (high < high_limit) & (wide < GRID - wide_place * WIN) & (row < WROWS)


def build_tables(height, width, places, blocks):
    both = dot_rows(height[...].astype(BF16), places[0]) + dot_rows(
        width[...].astype(BF16), places[1]
    )
    both = both.astype(BF16)
    return jnp.concatenate([both] * QUAD, axis=0) * blocks[...]


def roll_rows(values, by_width):
    sub = lax.broadcasted_iota(jnp.int32, (8, LANES), 0)
    pieces = []
    for start in range(0, ROWS, 8):
        piece = values[start : start + 8]
        first = start // WIN
        crossing = (first + 1) * WIN - start
        shifts = (first, first + 1)
        if by_width:
            one = pltpu.roll(piece, start - first * WIN, 1, stride=1, stride_axis=0)
        else:
            one = pltpu.roll(piece, first, 1) if first else piece
        if crossing < 8:
            if by_width:
                two = pltpu.roll(piece, LANES - crossing, 1)
                two = pltpu.roll(two, 0, 1, stride=1, stride_axis=0)
            else:
                two = pltpu.roll(piece, shifts[1], 1)
            one = jnp.where(sub < crossing, one, two)
        pieces.append(one)
    return jnp.concatenate(pieces, axis=0)


def normalize(values):
    centre = jnp.mean(values, axis=-1, keepdims=True)
    spread = values - centre
    variance = jnp.mean(spread * spread, axis=-1, keepdims=True)
    scale = lax.rsqrt(variance + EPSILON)
    return spread * scale, scale


def normalize_back(unit, scale, grad, gain):
    scaled = grad * gain
    mean_grad = jnp.mean(scaled, axis=-1, keepdims=True)
    mean_both = jnp.mean(scaled * unit, axis=-1, keepdims=True)
    return (scaled - mean_grad - unit * mean_both) * scale


def quarter_places(meta):
    mine, quarter = meta[0], meta[2]
    return [
        [4 * (mine ^ who) + (quarter ^ flip) for flip in (0, 2, 1, 3)] for who in (2, 3)
    ]


def start_copies(pairs, sems):
    copies = []
    for number, (source, target) in enumerate(pairs):
        copies.append(pltpu.make_async_copy(source, target, sems.at[number]))
    for copy in copies:
        copy.start()
    return copies


def wait_all(copies):
    for copy in copies:
        copy.wait()


def load_rows(meta, pieces, target, sems, first=0):
    own, near, *far = pieces
    columns = target.shape[1]
    quarter = target.shape[0] // 16
    pairs = []
    for source, who in ((own, 0), (near, 1)):
        start = pl.multiple_of(4 * (meta[0] ^ who) * quarter, 16)
        pairs.append((source, target.at[pl.ds(start, 4 * quarter), :]))
    for sources, places in zip(far, quarter_places(meta)):
        for index, place in enumerate(places):
            start = pl.multiple_of(place * quarter, 16)
            pairs.append(
                (sources.at[index, :, pl.ds(first, columns)], target.at[pl.ds(start, quarter), :])
            )
    return start_copies(pairs, sems)


def gather_quarters(first, block, staged, target, base, slabs):
    parts, rows, slots, width = block.shape
    lanes = width // LANES

    @pl.when(first)
    def _():
        for part in range(parts):
            values = block[part].astype(F32).reshape(rows * slots, width)
            for piece in range(lanes):
                staged[part * lanes + piece] = values[:, piece * LANES : (piece + 1) * LANES]
        target[:, parts * rows :, :] = jnp.zeros((slabs, ROWS - parts * rows, width), F32)

    for slab in range(slabs):
        for part in range(parts):
            for piece in range(lanes):
                target[
                    slab, part * rows : (part + 1) * rows, piece * LANES : (piece + 1) * LANES
                ] = staged[part * lanes + piece, pl.ds(base + slab, rows, stride=slots), :]


def scatter_quarters(last, full, staged, block, base, slabs):
    parts, rows, slots, width = block.shape
    lanes = width // LANES
    for slab in range(slabs):
        for part in range(parts):
            for piece in range(lanes):
                staged[part * lanes + piece, pl.ds(base + slab, rows, stride=slots), :] = full[
                    slab, part * rows : (part + 1) * rows, piece * LANES : (piece + 1) * LANES
                ]

    @pl.when(last)
    def _():
        for part in range(parts):
            for piece in range(lanes):
                values = staged[part * lanes + piece].reshape(rows, slots, LANES)
                block[part, :, :, piece * LANES : (piece + 1) * LANES] = values.astype(BF16)


def write_owned(source, meta, keep, send, across):
    height = keep.shape[1]
    for index in range(4):
        start = pl.multiple_of((meta[0] ^ index) * height, 16)
        target = send if index & across else keep
        target[index >> 1 if across == 1 else index & 1] = source[
            pl.ds(start, height), :
        ].astype(BF16)


ANY = pl.BlockSpec(memory_space=pl.ANY)


def whole(*shape):
    return pl.BlockSpec(shape, lambda *_: (0,) * len(shape))


def like(shape, dtype):
    return jax.ShapeDtypeStruct(shape, dtype)


def call(kernel, name, steps, scalars, ins, outs, scratch, cost, aliases=None):
    flops, moved, transcendentals = cost
    return pl.pallas_call(
        kernel,
        out_shape=tuple(item for item, _ in outs),
        grid_spec=pltpu.PrefetchScalarGridSpec(
            num_scalar_prefetch=len(scalars),
            grid=(steps,),
            in_specs=[spec for _, spec in ins],
            out_specs=tuple(spec for _, spec in outs),
            scratch_shapes=scratch,
        ),
        input_output_aliases={len(scalars) + k: v for k, v in (aliases or {}).items()},
        compiler_params=pltpu.CompilerParams(vmem_limit_bytes=VMEM_LIMIT),
        cost_estimate=pl.CostEstimate(
            flops=int(flops), bytes_accessed=int(moved), transcendentals=int(transcendentals)
        ),
        name=name,
    )(*scalars, *[item for item, _ in ins])


def group(count):
    return 2 if count % 2 == 0 else 1


def prepare_kernel(chunks, *refs):
    items, (expand, shrink), (vectors, packed) = refs[:8], refs[8:10], refs[10:]
    width = vectors.shape[1]
    row = 0
    for item in items:
        for start in range(0, item.shape[0], width):
            vectors[row : row + 1, :] = item[pl.ds(start, width)].reshape(1, width)
            row += 1
    quarter = expand.shape[0] // 4
    blocks = expand.shape[1] // width
    tall = shrink.shape[0] // (4 * chunks)
    for index in range(4):
        rows = slice(index * quarter, (index + 1) * quarter)
        for block in range(blocks):
            start = block * quarter
            packed[index, start : start + quarter, :] = expand[
                rows, block * width : (block + 1) * width
            ]
        for number in range(chunks):
            start = blocks * quarter + number * tall
            source = (4 * number + index) * tall
            packed[index, start : start + tall, :] = shrink[source : source + tall, :]


def prepare(chunks, items, weights):
    width = weights[1].shape[1]
    count = sum(item.shape[0] for item in items) // width
    total = sum(item.shape[0] * item.shape[1] for item in weights) // (4 * width)
    return call(
        functools.partial(prepare_kernel, chunks),
        "prepare",
        1,
        (),
        [(item, whole(*item.shape)) for item in (*items, *weights)],
        [
            (like((count, width), F32), whole(count, width)),
            (like((4, total, width), BF16), whole(4, total, width)),
        ],
        [],
        (0, 8 * total * width, 0),
    )


def collect_kernel(*refs):
    out = refs[-1]
    width = out.shape[1]
    singles, triples, expands, tables = refs[:6], refs[6:9], refs[9:12], refs[12:-1]
    out[...] = jnp.zeros_like(out)
    for row, item in enumerate(singles):
        out[row : row + 1, :] = item[...]
    size = width // 3
    for number, item in enumerate(triples):
        for part in range(3):
            row = TRIPLE_BIAS + part
            out[row : row + 1, number * size : (number + 1) * size] = item[
                :, part * size : (part + 1) * size
            ]
    for number, item in enumerate(expands):
        for part in range(item.shape[1] // size):
            row = EXPAND_BIAS + part
            out[row : row + 1, number * size : (number + 1) * size] = item[
                :, part * size : (part + 1) * size
            ]
    total = tables[0][...]
    for item in tables[1:]:
        total = total + item[...]
    for piece in range(3):
        out[TABLES : TABLES + 9, piece * LANES : (piece + 1) * LANES] = total[
            9 * piece : 9 * piece + 9, :
        ]


def collect(singles, triples, expands, tables):
    width = singles[0].shape[1]
    items = (*singles, *triples, *expands, *tables)
    return call(
        collect_kernel,
        "collect",
        1,
        (),
        [(item, whole(*item.shape)) for item in items],
        [(like((24, width), F32), whole(24, width))],
        [],
        (0, 16 * 24 * width, 0),
    )[0]


def attend_kernel(
    slabs, before, meta, windows, tokens, vectors, height, width_table, places, blocks, selectors,
    *rest,
):
    (
        rows_out, normed_out, triple_out, probs_out, attended_out,
        full, staged, weight, tables, masked_keys, sems,
    ) = rest[-11:]
    pieces = rest[:4]
    step = pl.program_id(0)
    base_slab = (step + before) * slabs
    width = full.shape[2]

    @pl.when(step == 0)
    def _():
        copies = load_rows(meta, pieces, weight, sems)
        tables[...] = build_tables(height, width_table, places, blocks)
        wait_all(copies)

    gather_quarters(step == 0, tokens, staged, full, base_slab, slabs)
    rows = full[...].reshape(slabs * ROWS, width)
    unit, _ = normalize(rows)
    normed = unit * vectors[FIRST_GAIN : FIRST_GAIN + 1] + vectors[FIRST_SHIFT : FIRST_SHIFT + 1]
    normed = normed.astype(BF16)
    rows_out[...] = rows.astype(BF16).reshape(slabs, ROWS, width)
    normed_out[...] = normed.reshape(slabs, ROWS, width)
    for part in range(3):
        columns = slice(part * width, (part + 1) * width)
        bias = vectors[TRIPLE_BIAS + part : TRIPLE_BIAS + part + 1]
        triple = dot(normed, weight[:, columns]) + bias
        triple_out[:, :, columns] = triple.astype(BF16).reshape(slabs, ROWS, width)

    lane = lax.broadcasted_iota(jnp.int32, (ROWS, LANES), 1)
    within = lane & (SEG - 1)
    upper = lane >= HD
    quads = HEADS // QUAD
    for slab in range(slabs):
        allowed = valid_rows(windows[meta[0], base_slab + slab])
        penalty = jnp.where((lane == WIN) & jnp.logical_not(allowed), PENALTY, 0.0).astype(BF16)
        for head in range(QUAD):
            masked_keys[slab, head] = selectors[head] + penalty

    sides = (jnp.logical_not(upper), upper)
    zero = jnp.zeros((ROWS, LANES), BF16)
    halves_of = lambda values, head: jnp.where(
        sides[head & 1], values[:, (head >> 1) * LANES : ((head >> 1) + 1) * LANES], zero
    )
    every = [(slab, head) for slab in range(slabs) for head in range(QUAD)]
    constant = jnp.where(lane == WIN, 1.0, 0.0)

    def one_quad(quad, carry):
        base = pl.multiple_of(quad * QUAD * HD, LANES)
        near = pl.multiple_of(base + width, LANES)
        far = pl.multiple_of(base + 2 * width, LANES)
        queries = [triple_out[slab, :, pl.ds(base, QUAD * HD)] for slab in range(slabs)]
        keys = [triple_out[slab, :, pl.ds(near, QUAD * HD)] for slab in range(slabs)]
        values = [triple_out[slab, :, pl.ds(far, QUAD * HD)] for slab in range(slabs)]
        terms = [dot(item, tables[...]) for item in queries]
        lefts = []
        for slab in range(slabs):
            high = roll_rows(terms[slab][:, :LANES], False)
            wide = roll_rows(terms[slab][:, LANES:], True)
            relative = jnp.where(
                within < WIN, high, jnp.where((within >= 16) & (within < 16 + WIN), wide, constant)
            ).astype(BF16)
            scaled = queries[slab] * jnp.asarray(HD**-0.5, BF16)
            lefts.append(
                [
                    jnp.concatenate([scaled[:, pair * LANES : (pair + 1) * LANES], relative], axis=1)
                    for pair in range(QUAD // 2)
                ]
            )
        scores = [
            dot_t(
                lefts[slab][head >> 1],
                jnp.concatenate([halves_of(keys[slab], head), masked_keys[slab, head]], axis=1),
            )
            for slab, head in every
        ]
        probs = []
        for (slab, head), score in zip(every, scores):
            maxima = jnp.max(score, axis=-1, keepdims=True)
            exponent = jnp.exp(score - maxima)
            summed = jnp.sum(exponent, axis=-1, keepdims=True)
            probs.append((exponent * (1.0 / summed)).astype(BF16))
            probs_out[slab, quad * QUAD + head] = probs[-1]
        parts = [dot(prob, halves_of(values[slab], head)) for (slab, head), prob in zip(every, probs)]
        for slab in range(slabs):
            mine = parts[slab * QUAD : (slab + 1) * QUAD]
            mixed = jnp.concatenate(
                [mine[2 * pair] + mine[2 * pair + 1] for pair in range(QUAD // 2)], axis=1
            )
            allowed = valid_rows(windows[meta[0], base_slab + slab])
            mixed = jnp.where(allowed, mixed, 0.0)
            attended_out[slab, :, pl.ds(base, QUAD * HD)] = mixed.astype(BF16)
        return carry

    lax.fori_loop(0, quads, one_quad, 0, unroll=True)


def attend(before, steps, meta, windows, tokens, vectors, tables, selectors, pieces, kept):
    parts, rows_dev, slots, width = tokens.shape
    slabs = group(slots)
    block3 = lambda columns: pl.BlockSpec((slabs, ROWS, columns), lambda i, *_: (i + before, 0, 0))
    rows = steps * slabs * ROWS
    ins = [(item, whole(*item.shape)) for item in (tokens, vectors, *tables, selectors)]
    ins += [(item, ANY) for item in pieces]
    aliases = {}
    if kept is not None:
        aliases = {len(ins) + n: n for n in range(len(kept))}
        ins += [(item, ANY) for item in kept]
    return call(
        functools.partial(attend_kernel, slabs, before),
        "attend",
        steps,
        (meta, windows),
        ins,
        [
            (like((slots, ROWS, width), BF16), block3(width)),
            (like((slots, ROWS, width), BF16), block3(width)),
            (like((slots, ROWS, 3 * width), BF16), block3(3 * width)),
            (
                like((slots, HEADS, ROWS, ROWS), BF16),
                pl.BlockSpec((slabs, HEADS, ROWS, ROWS), lambda i, *_: (i + before, 0, 0, 0)),
            ),
            (like((slots, ROWS, width), BF16), block3(width)),
        ],
        [
            pltpu.VMEM((slabs, ROWS, width), F32),
            pltpu.VMEM((parts * width // LANES, rows_dev * slots, LANES), F32),
            pltpu.VMEM((width, 3 * width), BF16),
            pltpu.VMEM((2 * LANES, 2 * LANES), BF16),
            pltpu.VMEM((slabs, QUAD, ROWS, LANES), BF16),
            pltpu.SemaphoreType.DMA((10,)),
        ],
        (
            6 * rows * width * width + steps * slabs * HEADS * 4 * ROWS * ROWS * 256,
            rows * (width * 16 + HEADS * 512) + width * width * 6,
            steps * slabs * HEADS * ROWS * ROWS,
        ),
        aliases,
    )


def project_kernel(
    slabs, first, meta, windows, attended, rows_in, grads, vectors, *rest,
):
    pieces = rest[:4]
    middle_out, normed_out, branch_out, shrink_bias_out, full, staged, weight, sems = rest[4:]
    step = pl.program_id(0)

    @pl.when(step == 0)
    def _():
        wait_all(load_rows(meta, pieces, weight, sems, first))
        shrink_bias_out[...] = jnp.zeros_like(shrink_bias_out)

    width = full.shape[2]
    count = slabs * ROWS
    middle = (
        rows_in[...].reshape(count, width).astype(F32)
        + dot(attended[...].reshape(count, width), weight[...])
        + vectors[OUTPUT_BIAS : OUTPUT_BIAS + 1]
    )
    unit, _ = normalize(middle)
    middle_out[...] = middle
    normed = unit * vectors[SECOND_GAIN : SECOND_GAIN + 1] + vectors[SECOND_SHIFT : SECOND_SHIFT + 1]
    normed_out[...] = normed.astype(BF16)
    gather_quarters(step == 0, grads, staged, full, step * slabs, slabs)
    for slab in range(slabs):
        allowed = valid_rows(windows[meta[0], step * slabs + slab])
        branch = jnp.where(allowed, full[slab], 0.0)
        branch_out[slab * ROWS : (slab + 1) * ROWS, :] = branch.astype(BF16)
        shrink_bias_out[...] += jnp.sum(branch, axis=0, keepdims=True)


def project(meta, windows, attended, rows_in, grads, vectors, pieces):
    parts, rows_dev, slots, width = grads.shape
    slabs = group(slots)
    block = pl.BlockSpec((slabs, ROWS, width), lambda i, *_: (i, 0, 0))
    flat = pl.BlockSpec((slabs * ROWS, width), lambda i, *_: (i, 0))
    rows = slots * ROWS
    return call(
        functools.partial(project_kernel, slabs, 3 * width),
        "project",
        slots // slabs,
        (meta, windows),
        [(attended, block), (rows_in, block)]
        + [(item, whole(*item.shape)) for item in (grads, vectors)]
        + [(item, ANY) for item in pieces],
        [
            (like((rows, width), F32), flat),
            (like((rows, width), BF16), flat),
            (like((rows, width), BF16), flat),
            (like((1, width), F32), whole(1, width)),
        ],
        [
            pltpu.VMEM((slabs, ROWS, width), F32),
            pltpu.VMEM((parts * width // LANES, rows_dev * slots, LANES), F32),
            pltpu.VMEM((width, width), BF16),
            pltpu.SemaphoreType.DMA((10,)),
        ],
        (2 * rows * width * width, rows * width * 14, 0),
    )


def gate_both(hidden):
    half = 0.5 * (1.0 + lax.erf(hidden * 0.7071067811865476))
    density = jnp.exp(hidden * hidden * -0.5) * 0.3989422804014327
    return hidden * half, half + hidden * density


def feed_kernel(number, first, unit, meta, normed, branch, vectors, *rest):
    pieces, rest = rest[:10], rest[10:]
    if not first:
        out_in, grad_in = rest[:2]
    out_acc, grad_acc, keep, send, bias_grad, expand, shrink, acc_e, acc_s, sems = rest[-10:]
    step = pl.program_id(0)
    last = pl.num_programs(0) - 1
    width, chunk = acc_e.shape
    blocks = chunk // unit

    @pl.when(step == 0)
    def _():
        pairs = []
        quarter, tall = expand.shape[1], shrink.shape[1]
        here = blocks * quarter + number * tall
        columns = pl.ds(number * unit, unit)
        for source, who in zip(pieces[:2], (0, 1)):
            places = pl.ds(4 * (meta[0] ^ who), 4)
            for block in range(blocks):
                pairs.append(
                    (
                        source.at[:, pl.ds(block * quarter, quarter), columns],
                        expand.at[places, :, pl.ds(block * unit, unit)],
                    )
                )
            pairs.append((source.at[:, pl.ds(here, tall), :], shrink.at[places]))
        for fetched, places in zip((pieces[2:6], pieces[6:10]), quarter_places(meta)):
            for source, place in zip(fetched, places):
                for block in range(blocks):
                    pairs.append(
                        (
                            source.at[pl.ds(block * quarter, quarter), columns],
                            expand.at[place, :, pl.ds(block * unit, unit)],
                        )
                    )
                pairs.append((source.at[pl.ds(here, tall), :], shrink.at[place]))
        copies = start_copies(pairs, sems)
        acc_e[...] = jnp.zeros_like(acc_e)
        acc_s[...] = jnp.zeros_like(acc_s)
        bias_grad[...] = jnp.zeros_like(bias_grad)
        wait_all(copies)

    rows = normed[...]
    grads = branch[...]
    bias = jnp.concatenate(
        [
            vectors[
                EXPAND_BIAS + block : EXPAND_BIAS + block + 1, number * unit : (number + 1) * unit
            ]
            for block in range(blocks)
        ],
        axis=1,
    )
    whole_expand = expand[...].reshape(width, chunk)
    whole_shrink = shrink[...].reshape(chunk, width)
    hidden = dot(rows, whole_expand) + bias
    d_active = dot_t(grads, whole_shrink)
    active, slope = gate_both(hidden)
    active = active.astype(BF16)
    back = (d_active * slope).astype(BF16)
    bias_grad[...] += jnp.sum(back.astype(F32), axis=0, keepdims=True)
    acc_s[...] += dot_rows(active, grads)
    acc_e[...] += dot_rows(rows, back)
    total_out = dot(active, whole_shrink)
    total_grad = dot_t(back, whole_expand)
    if first:
        out_acc[...] = total_out.astype(BF16)
        grad_acc[...] = total_grad.astype(BF16)
    else:
        out_acc[...] = (out_in[...].astype(F32) + total_out).astype(BF16)
        grad_acc[...] = (grad_in[...].astype(F32) + total_grad).astype(BF16)

    @pl.when(step == last)
    def _():
        height = width // 4
        third = height // 3
        for index in range(4):
            target = (send if index & 1 else keep).at[index >> 1]
            start = pl.multiple_of((meta[0] ^ index) * unit, 16)
            target[:unit, :] = acc_s[pl.ds(start, unit), :].astype(BF16)
            start = pl.multiple_of((meta[0] ^ index) * height, 16)
            target[unit : unit + height, :] = acc_e[pl.ds(start, height), :width].astype(BF16)
            for piece in range(3):
                here = pl.multiple_of(start + piece * third, 16)
                target[unit + height :, piece * unit : (piece + 1) * unit] = acc_e[
                    pl.ds(here, third), width:
                ].astype(BF16)


def feed(number, count, meta, normed, branch, vectors, pieces, kept):
    rows, width = normed.shape
    chunk = 4 * width // count
    unit = chunk // 4
    block_rows = 2 * ROWS
    block = pl.BlockSpec((block_rows, width), lambda i, *_: (i, 0))
    ins = [(normed, block), (branch, block), (vectors, whole(*vectors.shape))]
    ins += [(item, ANY) for item in pieces]
    aliases = {}
    if kept is not None:
        aliases = {len(ins) + n: n for n in range(2)}
        ins += [(item, block) for item in kept]
    payload = (2, unit + unit, width)
    return call(
        functools.partial(feed_kernel, number, kept is None, unit),
        "feed",
        rows // block_rows,
        (meta,),
        ins,
        [
            (like((rows, width), BF16), block),
            (like((rows, width), BF16), block),
            (like(payload, BF16), whole(*payload)),
            (like(payload, BF16), whole(*payload)),
            (like((1, chunk), F32), whole(1, chunk)),
        ],
        [
            pltpu.VMEM((16, width // 16, chunk), BF16),
            pltpu.VMEM((16, chunk // 16, width), BF16),
            pltpu.VMEM((width, chunk), F32),
            pltpu.VMEM((chunk, width), F32),
            pltpu.SemaphoreType.DMA((64,)),
        ],
        (12 * rows * width * chunk, rows * width * 12 + width * chunk * 8, 2 * rows * chunk),
        aliases,
    )


def middle_kernel(
    slabs, first, meta, windows, middle, out_acc, grad_acc, branch, attended, vectors,
    *rest,
):
    pieces = rest[:4]
    (
        result_out, d_middle_out, d_attended_out, keep, send, output_bias_grad, gain_grad,
        shift_grad, full, staged, weight, acc, sems,
    ) = rest[4:]
    step = pl.program_id(0)
    last = pl.num_programs(0) - 1

    @pl.when(step == 0)
    def _():
        copies = load_rows(meta, pieces, weight, sems, first)
        acc[...] = jnp.zeros_like(acc)
        output_bias_grad[...] = jnp.zeros_like(output_bias_grad)
        gain_grad[...] = jnp.zeros_like(gain_grad)
        shift_grad[...] = jnp.zeros_like(shift_grad)
        wait_all(copies)

    width = full.shape[2]
    count = slabs * ROWS
    rows = middle[...]
    result = rows + out_acc[...].astype(F32) + vectors[SHRINK_BIAS : SHRINK_BIAS + 1]
    full[...] = result.reshape(slabs, ROWS, width)
    scatter_quarters(step == last, full, staged, result_out, step * slabs, slabs)
    unit, scale = normalize(rows)
    grad = grad_acc[...].astype(F32)
    gain_grad[...] += jnp.sum(grad * unit, axis=0, keepdims=True)
    shift_grad[...] += jnp.sum(grad, axis=0, keepdims=True)
    d_middle = branch[...].astype(F32) + normalize_back(
        unit, scale, grad, vectors[SECOND_GAIN : SECOND_GAIN + 1]
    )
    d_output = d_middle.astype(BF16)
    d_middle_out[...] = d_output
    output_bias_grad[...] += jnp.sum(d_output.astype(F32), axis=0, keepdims=True)
    acc[...] += dot_rows(attended[...].reshape(count, width), d_output)
    d_attended = dot_t(d_output, weight[...]).reshape(slabs, ROWS, width)
    for slab in range(slabs):
        allowed = valid_rows(windows[meta[0], step * slabs + slab])
        d_attended_out[slab] = jnp.where(allowed, d_attended[slab], 0.0).astype(BF16)

    @pl.when(step == last)
    def _():
        write_owned(acc, meta, keep, send, 1)


def middle_back(meta, windows, rows_dev, middle, out_acc, grad_acc, branch, attended, vectors, pieces):
    slots, _, width = attended.shape
    parts = WROWS // rows_dev
    slabs = group(slots)
    block = pl.BlockSpec((slabs, ROWS, width), lambda i, *_: (i, 0, 0))
    flat = pl.BlockSpec((slabs * ROWS, width), lambda i, *_: (i, 0))
    rows = slots * ROWS
    vec = (like((1, width), F32), whole(1, width))
    payload = (2, width // 4, width)
    quarter = (parts, rows_dev, slots, width)
    return call(
        functools.partial(middle_kernel, slabs, 3 * width),
        "middle",
        slots // slabs,
        (meta, windows),
        [
            (middle, flat), (out_acc, flat), (grad_acc, flat), (branch, flat), (attended, block),
            (vectors, whole(*vectors.shape)),
        ]
        + [(item, ANY) for item in pieces],
        [
            (like(quarter, BF16), whole(*quarter)),
            (like((rows, width), BF16), flat),
            (like((slots, ROWS, width), BF16), block),
            (like(payload, BF16), whole(*payload)),
            (like(payload, BF16), whole(*payload)),
            vec,
            vec,
            vec,
        ],
        [
            pltpu.VMEM((slabs, ROWS, width), F32),
            pltpu.VMEM((parts * width // LANES, rows_dev * slots, LANES), F32),
            pltpu.VMEM((width, width), BF16),
            pltpu.VMEM((width, width), F32),
            pltpu.SemaphoreType.DMA((10,)),
        ],
        (4 * rows * width * width, rows * width * 18, 0),
    )


def attend_back_kernel(
    slabs, across, meta, normed, queries_in, keys_in, values_in, probs_in, d_mixed_in, mixed_in,
    height, width_table, places, blocks, selectors, sums,
    d_queries, d_keys, d_values, keep, send, bias_grad, table_out, grads, acc, tables, table_grad,
):
    step = pl.program_id(0)
    last = pl.num_programs(0) - 1
    wide4 = QUAD * HD

    @pl.when(step == 0)
    def _():
        acc[...] = jnp.zeros_like(acc)
        bias_grad[...] = jnp.zeros_like(bias_grad)
        table_grad[...] = jnp.zeros_like(table_grad)
        tables[...] = build_tables(height, width_table, places, blocks)

    lane = lax.broadcasted_iota(jnp.int32, (ROWS, LANES), 1)
    within = lane & (SEG - 1)
    upper = lane >= HD
    zero = jnp.zeros((ROWS, LANES), BF16)

    sides = (jnp.logical_not(upper), upper)
    halves_of = lambda items, head: jnp.where(
        sides[head & 1], items[:, (head >> 1) * LANES : ((head >> 1) + 1) * LANES], zero
    )
    minus = [
        jnp.where((lane == 2 * head) | (lane == 2 * head + 1), -1.0, 0.0).astype(BF16)
        for head in range(QUAD)
    ]
    every = [(slab, head) for slab in range(slabs) for head in range(QUAD)]
    lefts = []
    for slab in range(slabs):
        d_mixed = d_mixed_in[slab]
        product = d_mixed.astype(F32) * mixed_in[slab].astype(F32)
        product_high = product.astype(BF16)
        product_low = (product - product_high.astype(F32)).astype(BF16)
        inner = dot(product_high, sums[...]) + dot(product_low, sums[...])
        inner_high = inner.astype(BF16)
        inner_low = (inner - inner_high.astype(F32)).astype(BF16)
        inner = jnp.where((lane & 1) == 0, inner_high, inner_low)
        lefts.append(
            [
                jnp.concatenate([d_mixed[:, pair * LANES : (pair + 1) * LANES], inner], axis=1)
                for pair in range(QUAD // 2)
            ]
        )
    d_probs = [
        dot_t(
            lefts[slab][head >> 1],
            jnp.concatenate([halves_of(values_in[slab], head), minus[head]], axis=1),
        )
        for slab, head in every
    ]
    parts_v = [
        dot_rows(probs_in[slab, head], halves_of(d_mixed_in[slab], head)) for slab, head in every
    ]
    d_scores = [
        (probs_in[slab, head].astype(F32) * item).astype(BF16)
        for (slab, head), item in zip(every, d_probs)
    ]
    backs = [
        dot(
            item,
            jnp.concatenate([halves_of(keys_in[slab], head), selectors[head]], axis=1),
        )
        for (slab, head), item in zip(every, d_scores)
    ]
    parts_k = [
        dot_rows(item, halves_of(queries_in[slab], head))
        for (slab, head), item in zip(every, d_scores)
    ]
    scale = HD**-0.5
    joined = lambda items: jnp.concatenate(
        [items[2 * pair] + items[2 * pair + 1] for pair in range(QUAD // 2)], axis=1
    )
    for slab in range(slabs):
        mine = slice(slab * QUAD, (slab + 1) * QUAD)
        d_relative = backs[slab * QUAD][:, LANES:]
        for head in range(1, QUAD):
            d_relative = d_relative + backs[slab * QUAD + head][:, LANES:]
        high = roll_rows(jnp.where(within < WIN, d_relative, 0.0), False)
        wide = roll_rows(jnp.where((within >= 16) & (within < 16 + WIN), d_relative, 0.0), True)
        d_terms = jnp.concatenate([high, wide], axis=1).astype(BF16)
        dq = joined([item[:, :LANES] for item in backs[mine]]) * scale
        dq = (dq + dot_t(d_terms, tables[...])).astype(BF16)
        table_grad[...] += dot_rows(queries_in[slab], d_terms)
        dk = (joined(parts_k[mine]) * scale).astype(BF16)
        dv = joined(parts_v[mine]).astype(BF16)
        d_queries[slab] = dq
        d_keys[slab] = dk
        d_values[slab] = dv
        grads[slab] = jnp.concatenate([dq, dk, dv], axis=1)

    width = normed.shape[2]
    both = grads[...].reshape(slabs * ROWS, 3 * wide4)
    bias_grad[...] += jnp.sum(both.astype(F32), axis=0, keepdims=True)
    acc[...] += dot_rows(normed[...].reshape(slabs * ROWS, width), both)

    @pl.when(step == last)
    def _():
        write_owned(acc, meta, keep, send, across)
        masked = table_grad[...] * blocks[...].astype(F32)
        folded = masked[:HD]
        for head in range(1, QUAD):
            folded = folded + masked[head * HD : (head + 1) * HD]
        high = folded.astype(BF16)
        low = (folded - high.astype(F32)).astype(BF16)
        for which in range(2):
            table_out[:, which * HD : (which + 1) * HD] = dot_t(places[which], high) + dot_t(
                places[which], low
            )


def attend_back(quad, across, meta, normed, triple, probs, d_mixed, mixed, tables, selectors, sums):
    slots, _, width = normed.shape
    slabs = group(slots)
    wide4 = QUAD * HD
    quads = HEADS // QUAD
    column = lambda where: pl.BlockSpec((slabs, ROWS, wide4), lambda i, *_: (i, 0, where))
    narrow = (
        like((slots, ROWS, wide4), BF16),
        pl.BlockSpec((slabs, ROWS, wide4), lambda i, *_: (i, 0, 0)),
    )
    rows = slots * ROWS
    payload = (2, width // 4, 3 * wide4)
    return call(
        functools.partial(attend_back_kernel, slabs, across),
        "attend_back",
        slots // slabs,
        (meta,),
        [
            (normed, pl.BlockSpec((slabs, ROWS, width), lambda i, *_: (i, 0, 0))),
            (triple, column(quad)),
            (triple, column(quads + quad)),
            (triple, column(2 * quads + quad)),
            (probs, pl.BlockSpec((slabs, QUAD, ROWS, ROWS), lambda i, *_: (i, quad, 0, 0))),
            (d_mixed, column(quad)),
            (mixed, column(quad)),
        ]
        + [(item, whole(*item.shape)) for item in (*tables, selectors, sums)],
        [
            narrow,
            narrow,
            narrow,
            (like(payload, BF16), whole(*payload)),
            (like(payload, BF16), whole(*payload)),
            (like((1, 3 * wide4), F32), whole(1, 3 * wide4)),
            (like((REL, 2 * HD), F32), whole(REL, 2 * HD)),
        ],
        [
            pltpu.VMEM((slabs, ROWS, 3 * wide4), BF16),
            pltpu.VMEM((width, 3 * wide4), F32),
            pltpu.VMEM((2 * LANES, 2 * LANES), BF16),
            pltpu.VMEM((2 * LANES, 2 * LANES), F32),
        ],
        (
            2 * rows * width * 3 * wide4 + slots * QUAD * 8 * ROWS * ROWS * 256,
            rows * (width * 2 + wide4 * 16 + QUAD * 512),
            0,
        ),
    )


def first_kernel(slabs, meta, rows_in, d_middle, vectors, *rest):
    grads, pieces = rest[:9], rest[9:13]
    tokens_out, gain_grad, shift_grad, full, staged, weight, sems = rest[13:]
    step = pl.program_id(0)
    last = pl.num_programs(0) - 1

    @pl.when(step == 0)
    def _():
        copies = load_rows(meta, pieces, weight, sems)
        gain_grad[...] = jnp.zeros_like(gain_grad)
        shift_grad[...] = jnp.zeros_like(shift_grad)
        wait_all(copies)

    width = full.shape[2]
    count = slabs * ROWS
    wide4 = QUAD * HD
    both = jnp.concatenate([grad[...].reshape(count, wide4) for grad in grads], axis=1)
    total = dot_t(both, weight[...])
    unit, scale = normalize(rows_in[...].reshape(count, width).astype(F32))
    gain_grad[...] += jnp.sum(total * unit, axis=0, keepdims=True)
    shift_grad[...] += jnp.sum(total, axis=0, keepdims=True)
    back = normalize_back(unit, scale, total, vectors[FIRST_GAIN : FIRST_GAIN + 1])
    full[...] = (d_middle[...].astype(F32) + back).reshape(slabs, ROWS, width)
    scatter_quarters(step == last, full, staged, tokens_out, step * slabs, slabs)


def first_back(before, steps, meta, rows_dev, rows_in, d_middle, vectors, grads, pieces):
    slots, _, width = rows_in.shape
    parts = WROWS // rows_dev
    slabs = group(slots)
    wide4 = QUAD * HD
    block = pl.BlockSpec((slabs, ROWS, width), lambda i, *_: (i + before, 0, 0))
    flat = pl.BlockSpec((slabs * ROWS, width), lambda i, *_: (i + before, 0))
    narrow = pl.BlockSpec((slabs, ROWS, wide4), lambda i, *_: (i + before, 0, 0))
    rows = steps * slabs * ROWS
    quarter = (parts, rows_dev, steps * slabs, width)
    return call(
        functools.partial(first_kernel, slabs),
        "first_back",
        steps,
        (meta,),
        [(rows_in, block), (d_middle, flat), (vectors, whole(*vectors.shape))]
        + [(item, narrow) for item in grads]
        + [(item, ANY) for item in pieces],
        [(like(quarter, BF16), whole(*quarter))] + [(like((1, width), F32), whole(1, width))] * 2,
        [
            pltpu.VMEM((slabs, ROWS, width), F32),
            pltpu.VMEM((parts * width // LANES, rows_dev * steps * slabs, LANES), F32),
            pltpu.VMEM((width, 3 * width), BF16),
            pltpu.SemaphoreType.DMA((10,)),
        ],
        (6 * rows * width * width, rows * width * 14, 0),
    )


def join_halves(meta, items, staged):
    upper = meta[1] > 0
    for number, both in enumerate(staged):
        mine, other = items[2 * number], items[2 * number + 1]
        half = mine.shape[0]

        @pl.when(upper)
        def _():
            both[:half] = other[...]
            both[half:] = mine[...]

        @pl.when(jnp.logical_not(upper))
        def _():
            both[:half] = mine[...]
            both[half:] = other[...]


def finish_feed_kernel(unit, pairs, meta, *refs):
    items, (expand_out, shrink_out), staged = (
        refs[: 2 * pairs], refs[2 * pairs : 2 * pairs + 2], refs[2 * pairs + 2 :]
    )
    join_halves(meta, items, staged)
    shard, width = expand_out.shape[0], shrink_out.shape[1]
    third = shard // 3
    parts = width // shard
    for number, both in enumerate(staged):
        here = number * unit
        shrink_out[here : here + unit, :] = both[:unit, :].astype(F32)
        for block in range(parts - 1):
            start = block * width + here
            expand_out[:, start : start + unit] = both[
                unit : unit + shard, block * unit : (block + 1) * unit
            ].astype(F32)
        start = (parts - 1) * width + here
        for piece in range(3):
            expand_out[piece * third : (piece + 1) * third, start : start + unit] = both[
                unit + shard :, piece * unit : (piece + 1) * unit
            ].astype(F32)


def finish_rest_kernel(pairs, meta, *refs):
    items, small, refs = refs[: 2 * pairs], refs[2 * pairs], refs[2 * pairs + 1 :]
    (triple_out, output_out), refs = refs[:2], refs[2:]
    vectors, tables, staged = refs[:8], refs[8:10], refs[10:]
    join_halves(meta, items, staged)
    shard, width = output_out.shape
    output_out[...] = staged[0][:shard, :].astype(F32)
    wide4 = QUAD * HD
    for quad, both in enumerate(staged):
        values = both[shard:, :] if quad == 0 else both[...]
        for part in range(3):
            start = part * width + quad * wide4
            triple_out[:, start : start + wide4] = values[
                :, part * wide4 : (part + 1) * wide4
            ].astype(F32)
    row = 0
    for item in vectors:
        for start in range(0, item.shape[0], width):
            item[pl.ds(start, width)] = small[row : row + 1, :].reshape(width)
            row += 1
    for which, item in enumerate(tables):
        for piece in range(3):
            start = piece * LANES + which * HD
            item[9 * piece : 9 * piece + 9, :] = small[TABLES : TABLES + 9, start : start + HD]


def finish(kernel, name, meta, shares, others, outs):
    items = [item for pair in shares for item in pair]
    return call(
        kernel,
        name,
        1,
        (meta,),
        [(item, whole(*item.shape)) for item in (*items, *others)],
        [(like(item.shape, F32), whole(*item.shape)) for item in outs],
        [pltpu.VMEM((2 * mine.shape[0], mine.shape[1]), BF16) for mine, _ in shares],
        (0, sum(6 * item.size for item in items), 0),
    )


def swap(values, axis, bits):
    count = lax.axis_size(axis)
    return lax.ppermute(values, axis, [(n, n ^ bits) for n in range(count)])


def swap_diagonal(values):
    across = lax.axis_size("seq")
    count = lax.axis_size("dp") * across
    perm = [(n, (n // across ^ 1) * across + (n % across ^ 1)) for n in range(count)]
    return lax.ppermute(values, ("dp", "seq"), perm)


def spread(far):
    return far, swap(far, "dp", 1), swap(far, "seq", 1), swap_diagonal(far)


def exchange_windows(values):
    return lax.all_to_all(values, "tensor", split_axis=0, concat_axis=0, tiled=True)


def after(values, *others):
    return lax.optimization_barrier((values, *others))[0]


def far_quarter(packed):
    which = 2 * (lax.axis_index("dp") & 1) + (lax.axis_index("seq") & 1)
    return lax.dynamic_index_in_dim(packed, which, axis=0, keepdims=False)


def add(*items):
    total = items[0].astype(F32)
    for item in items[1:]:
        total = total + item.astype(F32)
    return total.astype(BF16)


def halves(axis):
    out, bit = [], 1
    while bit < lax.axis_size(axis):
        out.append(bit)
        bit *= 2
    return out


def reduce_stages(payloads, plan, hook=None):
    bits_of = {"c": 1, "y": 2}
    totals = []
    while True:
        keep, send, more = payloads.pop(0)
        (far,) = yield [(send, "tensor", bits_of[plan[0]])]
        totals.append(add(keep, far))
        if not more:
            break
    total = totals[0] if len(totals) == 1 else jnp.concatenate(totals, axis=1)
    spot = lax.axis_index("dp")
    place = lax.axis_index("seq")

    def split(values, upper):
        size = values.shape[-2] // 2
        low, high = values[..., :size, :], values[..., size:, :]
        return jnp.where(upper, high, low), jnp.where(upper, low, high)

    def join(mine, far, upper):
        return jnp.concatenate([jnp.where(upper, far, mine), jnp.where(upper, mine, far)], axis=0)

    for letter in plan[1:]:
        if letter == "w":
            total = hook(total)
        elif letter in bits_of:
            (far,) = yield [(total[1], "tensor", bits_of[letter])]
            total = add(total[0], far)
        elif letter == "x":
            for bit in halves("dp"):
                near, far = split(total, (spot & bit) > 0)
                (far,) = yield [(far, "dp", bit)]
                total = add(near, far)
        else:
            if letter == "s":
                near, far = split(total, (place & 1) > 0)
                (far,) = yield [(far, "seq", 1)]
                total = add(near, far)
            for bit in halves("seq"):
                if letter == "s" and bit == 1:
                    continue
                (far,) = yield [(total, "seq", bit)]
                total = add(total, far)
            if letter == "s":
                (far,) = yield [(total, "seq", 1)]
                total = join(total, far, (place & 1) > 0)
    for bit in reversed(halves("dp")):
        (far,) = yield [(total, "dp", bit)]
        if bit > 1:
            total = join(total, far, (spot & bit) > 0)
    return total, far


def sum_stages(values):
    steps = [(axis, bit) for axis in ("tensor", "dp", "seq") for bit in halves(axis)]
    steps = [("tensor", 2)] + [item for item in steps if item != ("tensor", 2)]
    for axis, bit in steps:
        (far,) = yield [(values, axis, bit)]
        values = values + far
    return (values,)


class Exchanges:
    def __init__(self):
        self.running = []
        self.done = {}

    def begin(self, name, stages):
        self.running.append([name, stages, None])

    def step(self, names, token, meta, *extra):
        asked, ended = [], []
        chosen = [entry for entry in self.running if names is None or entry[0] in names]
        arrived = [item for entry in chosen for item in (entry[2] or ())]
        if token is not None and arrived:
            token, *arrived = lax.optimization_barrier((token, *arrived))
        arrived = iter(arrived)
        for entry in chosen:
            name, stages, waiting = entry
            mine = None if waiting is None else [next(arrived) for _ in waiting]
            try:
                asked.append((entry, stages.send(mine)))
            except StopIteration as stop:
                ended.append((name, stop.value))
                self.running.remove(entry)
        values = [item[0] for _, wanted in asked for item in wanted]
        finished = [item for _, pair in ended for item in pair]
        if meta is not None:
            count = len(values)
            meta, *rest = lax.optimization_barrier((meta, *values, *finished, *extra))
            values = rest[:count]
            finished = rest[count : count + len(finished)]
            extra = rest[count + len(finished) :]
        values, finished = iter(values), iter(finished)
        for entry, wanted in asked:
            entry[2] = [swap(next(values), axis, bits) for _, axis, bits in wanted]
        for name, pair in ended:
            self.done[name] = tuple(next(finished) for _ in pair)
        return (token, meta, *extra)

    def finish(self, names):
        while any(entry[0] in names for entry in self.running):
            self.step(names, None, None)


def local(
    tokens,
    out_grad,
    slot_window,
    first_gain,
    first_shift,
    triple_weight,
    triple_bias,
    height_table,
    width_table,
    output_weight,
    output_bias,
    second_gain,
    second_shift,
    expand_weight,
    expand_bias,
    shrink_weight,
    shrink_bias,
):
    micros, images, slots, rows_dev, width = tokens.shape
    parts = lax.axis_size("tensor")
    mine = lax.axis_index("tensor")
    shard = width // parts
    chunks = 3
    unit = width // chunks
    bit = lax.axis_index("dp") & 1
    quarter = 2 * bit + (lax.axis_index("seq") & 1)
    meta = jnp.where(
        jnp.arange(3) == 0, mine, jnp.where(jnp.arange(3) == 1, bit, quarter)
    ).astype(jnp.int32)

    by_image = lambda values: jnp.swapaxes(values, 2, 3).reshape(parts, rows_dev, slots, width)
    to_image = lambda values: jnp.swapaxes(
        values.reshape(micros, images, rows_dev, slots, width), 2, 3
    )
    windows = slot_window.reshape(parts, slots)

    far = jnp.concatenate(
        [
            far_quarter(triple_weight.reshape(4, shard // 4, -1)),
            far_quarter(output_weight.reshape(4, shard // 4, -1)),
        ],
        axis=1,
    )
    far = swap(far, "tensor", 2)
    near_triple = swap(triple_weight, "tensor", 1)
    near_output = swap(output_weight, "tensor", 1)
    vectors, packed_rest = prepare(
        chunks,
        (
            first_gain, first_shift, output_bias, second_gain, second_shift, shrink_bias,
            triple_bias, expand_bias,
        ),
        (expand_weight, shrink_weight),
    )
    sums = np.zeros((QUAD * HD, LANES), np.float32)
    for head in range(QUAD):
        sums[head * HD : (head + 1) * HD, 2 * head : 2 * head + 2] = 1.0
    sums = jnp.asarray(sums, BF16)
    ahead = (height_table, width_table, table_places(False), head_blocks(False))
    behind = (height_table, width_table, table_places(True), head_blocks(True))
    first_rest = far_quarter(packed_rest)
    far, vectors, packed_rest, first_rest, meta, own_tokens, near_triple, near_output = (
        lax.optimization_barrier(
            (
                far, vectors, packed_rest, first_rest, meta, by_image(tokens), near_triple,
                near_output,
            )
        )
    )
    rows_in = exchange_windows(own_tokens)
    fetched = jnp.stack(spread(far))
    crossed = swap(fetched, "tensor", 1)

    packed, first_rest, rows_in, fetched, crossed = lax.optimization_barrier(
        (packed_rest, first_rest, rows_in, fetched, crossed)
    )
    triple_pieces = (triple_weight, near_triple, fetched, crossed)
    output_pieces = (output_weight, near_output, fetched, crossed)
    far = swap(first_rest, "tensor", 2)
    near = swap(packed, "tensor", 1)
    steps = slots // group(slots)
    early = max(1, steps // 4)
    selectors = key_selectors(False)
    kept = attend(
        0, early, meta, windows, rows_in, vectors, ahead, selectors, triple_pieces, None
    )
    kept = list(kept)
    kept[4], far, own_grads = lax.optimization_barrier((kept[4], far, by_image(out_grad)))
    meta, far, near, own_grads = lax.optimization_barrier((meta, far, near, own_grads))
    grads_in = exchange_windows(own_grads)
    fetched = spread(far)
    crossed = (swap(far, "tensor", 1),)
    if early < steps:
        kept = attend(
            early, steps - early, meta, windows, rows_in, vectors, ahead, selectors,
            triple_pieces, kept,
        )
    full_rows, normed, triple, probs, attended = kept
    attended, *others = lax.optimization_barrier((attended, *fetched[1:]))
    meta, *others = lax.optimization_barrier((meta, *others))
    crossed += tuple(swap(item, "tensor", 1) for item in others)
    middle_stage = project(
        meta, windows, attended, full_rows, grads_in, vectors, output_pieces
    )
    shrink_bias_grad = middle_stage[3]
    rest_pieces = (packed, near, far, *others, *crossed)
    middle, normed2, branch = middle_stage[:3]
    exchanges = Exchanges()
    kept = None
    expand_bias_grads = []
    for number in range(chunks):
        *kept, keep, send, bias_grad = feed(
            number, chunks, meta, normed2, branch, vectors, rest_pieces, kept
        )
        plan = ("cyxz", "cyxz", "cxyz")[number]
        exchanges.begin(("feed", number), reduce_stages([(keep, send, False)], plan))
        bias_grad, meta = exchanges.step(None, bias_grad, meta)
        expand_bias_grads.append(bias_grad)

    result, d_middle, d_attended, keep, send, output_bias_grad, gain2_grad, shift2_grad = (
        middle_back(
            meta, windows, rows_dev, middle, *kept, branch, attended, vectors, output_pieces
        )
    )
    payloads = [(keep, send, True)]
    exchanges.begin(("rest", 0), reduce_stages(payloads, "cyxs"))
    output_bias_grad, meta = exchanges.step(None, output_bias_grad, meta)
    result = exchange_windows(result)

    quad_grads, triple_bias_grads, table_grads = [], [], []
    for quad in range(HEADS // QUAD):
        dq, dk, dv, keep, send, bias_grad, table_grad = attend_back(
            quad, 2 if quad == 2 else 1, meta, normed, triple, probs, d_attended, attended, behind, key_selectors(True), sums
        )
        if quad == 0:
            payloads.append((keep, send, False))
        else:
            plan = "cyxz" if quad == 1 else "ycxzw"
            hook = lambda total: after(total, *feed_gradients)
            exchanges.begin(("rest", quad), reduce_stages([(keep, send, False)], plan, hook))
        if quad == 1:
            bias_grad, meta, result = exchanges.step(None, bias_grad, meta, result)
        else:
            bias_grad, meta = exchanges.step(None, bias_grad, meta)
        quad_grads.append((dq, dk, dv))
        triple_bias_grads.append(bias_grad)
        table_grads.append(table_grad)
    wide4 = QUAD * HD
    grads9 = [quad_grads[quad][part] for part in range(3) for quad in range(HEADS // QUAD)]
    token_grad, gain1_grad, shift1_grad = first_back(
        0, steps, meta, rows_dev, full_rows, d_middle, vectors, grads9, triple_pieces
    )
    result = to_image(result)
    gain1_grad, _ = exchanges.step(None, gain1_grad, None)
    small = collect(
        (gain1_grad, shift1_grad, output_bias_grad, gain2_grad, shift2_grad, shrink_bias_grad),
        triple_bias_grads,
        expand_bias_grads,
        table_grads,
    )
    exchanges.begin("small", sum_stages(small))
    exchanges.step(["small"], None, None)
    first_far = exchanges.running[-1][2][0]
    tokens_gradient = to_image(exchange_windows(after(token_grad, first_far)))
    names = [("feed", number) for number in range(chunks)]
    exchanges.finish(names)
    shares = [exchanges.done[name] for name in names]
    feed_gradients = finish(
        functools.partial(finish_feed_kernel, unit, chunks),
        "finish_feed",
        meta,
        shares,
        (),
        (expand_weight, shrink_weight),
    )
    expand_gradient, shrink_gradient = feed_gradients
    exchanges.finish([("rest", number) for number in range(HEADS // QUAD)] + ["small"])
    shares = [exchanges.done["rest", number] for number in range(HEADS // QUAD)]
    triple_gradient, output_gradient, *outs, high, wide = finish(
        functools.partial(finish_rest_kernel, len(shares)),
        "finish_rest",
        meta,
        shares,
        exchanges.done["small"],
        (
            triple_weight, output_weight, first_gain, first_shift, output_bias, second_gain,
            second_shift, shrink_bias, triple_bias, expand_bias, height_table, width_table,
        ),
    )
    return (
        result,
        tokens_gradient,
        outs[0],
        outs[1],
        triple_gradient,
        outs[6],
        high,
        wide,
        output_gradient,
        outs[2],
        outs[3],
        outs[4],
        expand_gradient,
        outs[7],
        shrink_gradient,
        outs[5],
    )


def solution(mesh):
    split = P(None, "dp", "seq", "tensor", None)
    rows = P("tensor", None)
    return jax.shard_map(
        local,
        mesh=mesh,
        in_specs=(
            split, split, P(None, "dp", "seq"), P(), P(), rows, P(), P(), P(), rows, P(), P(), P(),
            rows, P(), rows, P(),
        ),
        out_specs=(
            split, split, P(), P(), rows, P(), P(), P(), rows, P(), P(), P(), rows, P(), rows, P(),
        ),
        check_vma=False,
    )
```

```python
import functools

import jax
import jax.numpy as jnp
import numpy as np
from jax import lax
from jax.experimental import pallas as pl
from jax.experimental.pallas import tpu as pltpu
from jax.sharding import PartitionSpec as P

HEADS = 12
HD = 64
WIN = 14
GRID = 64
WGRID = 5
WROWS = WIN * WIN
ROWS = 200
QUAD = 4
LANES = 128
REL = 2 * WIN - 1
SEG = 32
EPSILON = 1e-06
PENALTY = -1e9

F32 = jnp.float32
BF16 = jnp.bfloat16
FIRST_GAIN, FIRST_SHIFT, OUTPUT_BIAS, SECOND_GAIN, SECOND_SHIFT, SHRINK_BIAS = range(6)
TRIPLE_BIAS, EXPAND_BIAS, TABLES = 6, 9, 13
VMEM_LIMIT = 58 * 1024 * 1024


def dot(left, right):
    return lax.dot_general(left, right, (((1,), (0,)), ((), ())), preferred_element_type=F32)


def dot_t(left, right):
    return lax.dot_general(left, right, (((1,), (1,)), ((), ())), preferred_element_type=F32)


def dot_rows(left, right):
    return lax.dot_general(left, right, (((0,), (0,)), ((), ())), preferred_element_type=F32)


def key_selectors(mirrored):
    out = np.zeros((QUAD, ROWS, LANES), np.float32)
    for head in range(QUAD):
        for key in range(WROWS):
            high, wide = key // WIN, key % WIN
            if mirrored:
                high, wide = WIN - 1 - high, WIN - 1 - wide
            out[head, key, SEG * head + high] = 1.0
            out[head, key, SEG * head + 16 + wide] = 1.0
    return jnp.asarray(out, BF16)


def table_places(mirrored):
    out = np.zeros((2, REL, 2 * LANES), np.float32)
    for head in range(QUAD):
        for row in range(REL):
            if mirrored:
                out[0, row, SEG * head + row] = 1.0
                out[1, row, LANES + (SEG * head + 16 + row) % LANES] = 1.0
            else:
                out[0, REL - 1 - row, (SEG * head + row - 13) % LANES] = 1.0
                out[1, REL - 1 - row, LANES + (SEG * head + row + 3) % LANES] = 1.0
    return jnp.asarray(out, BF16)


def head_blocks(mirrored):
    out = np.zeros((QUAD * HD, 2 * LANES), np.float32)
    for head in range(QUAD):
        rows = slice(head * HD, (head + 1) * HD)
        for row in range(REL):
            if mirrored:
                out[rows, SEG * head + row] = 1.0
                out[rows, LANES + (SEG * head + 16 + row) % LANES] = 1.0
            else:
                out[rows, (SEG * head + row - 13) % LANES] = 1.0
                out[rows, LANES + (SEG * head + row + 3) % LANES] = 1.0
    return jnp.asarray(out, BF16)


def valid_rows(window):
    high_place = (window * 13) >> 6
    wide_place = window - high_place * WGRID
    inside = window < WGRID * WGRID
    row = lax.broadcasted_iota(jnp.int32, (ROWS, 1), 0)
    high = (row * 4682) >> 16
    wide = row - high * WIN
    high_limit = jnp.where(inside, GRID - high_place * WIN, 0)
    return (high < high_limit) & (wide < GRID - wide_place * WIN) & (row < WROWS)


def build_tables(height, width, places, blocks):
    both = dot_rows(height[...].astype(BF16), places[0]) + dot_rows(
        width[...].astype(BF16), places[1]
    )
    both = both.astype(BF16)
    return jnp.concatenate([both] * QUAD, axis=0) * blocks[...]


def roll_rows(values, by_width):
    sub = lax.broadcasted_iota(jnp.int32, (8, LANES), 0)
    pieces = []
    for start in range(0, ROWS, 8):
        piece = values[start : start + 8]
        first = start // WIN
        crossing = (first + 1) * WIN - start
        shifts = (first, first + 1)
        if by_width:
            one = pltpu.roll(piece, start - first * WIN, 1, stride=1, stride_axis=0)
        else:
            one = pltpu.roll(piece, first, 1) if first else piece
        if crossing < 8:
            if by_width:
                two = pltpu.roll(piece, LANES - crossing, 1)
                two = pltpu.roll(two, 0, 1, stride=1, stride_axis=0)
            else:
                two = pltpu.roll(piece, shifts[1], 1)
            one = jnp.where(sub < crossing, one, two)
        pieces.append(one)
    return jnp.concatenate(pieces, axis=0)


def normalize(values):
    centre = jnp.mean(values, axis=-1, keepdims=True)
    spread = values - centre
    variance = jnp.mean(spread * spread, axis=-1, keepdims=True)
    scale = lax.rsqrt(variance + EPSILON)
    return spread * scale, scale


def normalize_back(unit, scale, grad, gain):
    scaled = grad * gain
    mean_grad = jnp.mean(scaled, axis=-1, keepdims=True)
    mean_both = jnp.mean(scaled * unit, axis=-1, keepdims=True)
    return (scaled - mean_grad - unit * mean_both) * scale


def quarter_places(meta):
    mine, quarter = meta[0], meta[2]
    return [
        [4 * (mine ^ who) + (quarter ^ flip) for flip in (0, 2, 1, 3)] for who in (2, 3)
    ]


def start_copies(pairs, sems):
    copies = []
    for number, (source, target) in enumerate(pairs):
        copies.append(pltpu.make_async_copy(source, target, sems.at[number]))
    for copy in copies:
        copy.start()
    return copies


def wait_all(copies):
    for copy in copies:
        copy.wait()


def load_rows(meta, pieces, target, sems, first=0):
    own, near, *far = pieces
    columns = target.shape[1]
    quarter = target.shape[0] // 16
    pairs = []
    for source, who in ((own, 0), (near, 1)):
        start = pl.multiple_of(4 * (meta[0] ^ who) * quarter, 16)
        pairs.append((source, target.at[pl.ds(start, 4 * quarter), :]))
    for sources, places in zip(far, quarter_places(meta)):
        for index, place in enumerate(places):
            start = pl.multiple_of(place * quarter, 16)
            pairs.append(
                (sources.at[index, :, pl.ds(first, columns)], target.at[pl.ds(start, quarter), :])
            )
    return start_copies(pairs, sems)


def gather_quarters(first, block, staged, target, base, slabs):
    parts, rows, slots, width = block.shape
    lanes = width // LANES

    @pl.when(first)
    def _():
        for part in range(parts):
            values = block[part].astype(F32).reshape(rows * slots, width)
            for piece in range(lanes):
                staged[part * lanes + piece] = values[:, piece * LANES : (piece + 1) * LANES]
        target[:, parts * rows :, :] = jnp.zeros((slabs, ROWS - parts * rows, width), F32)

    for slab in range(slabs):
        for part in range(parts):
            for piece in range(lanes):
                target[
                    slab, part * rows : (part + 1) * rows, piece * LANES : (piece + 1) * LANES
                ] = staged[part * lanes + piece, pl.ds(base + slab, rows, stride=slots), :]


def scatter_quarters(last, full, staged, block, base, slabs):
    parts, rows, slots, width = block.shape
    lanes = width // LANES
    for slab in range(slabs):
        for part in range(parts):
            for piece in range(lanes):
                staged[part * lanes + piece, pl.ds(base + slab, rows, stride=slots), :] = full[
                    slab, part * rows : (part + 1) * rows, piece * LANES : (piece + 1) * LANES
                ]

    @pl.when(last)
    def _():
        for part in range(parts):
            for piece in range(lanes):
                values = staged[part * lanes + piece].reshape(rows, slots, LANES)
                block[part, :, :, piece * LANES : (piece + 1) * LANES] = values.astype(BF16)


def write_owned(source, meta, keep, send, across):
    height = keep.shape[1]
    for index in range(4):
        start = pl.multiple_of((meta[0] ^ index) * height, 16)
        target = send if index & across else keep
        target[index >> 1 if across == 1 else index & 1] = source[
            pl.ds(start, height), :
        ].astype(BF16)


ANY = pl.BlockSpec(memory_space=pl.ANY)


def whole(*shape):
    return pl.BlockSpec(shape, lambda *_: (0,) * len(shape))


def like(shape, dtype):
    return jax.ShapeDtypeStruct(shape, dtype)


def call(kernel, name, steps, scalars, ins, outs, scratch, cost, aliases=None):
    flops, moved, transcendentals = cost
    return pl.pallas_call(
        kernel,
        out_shape=tuple(item for item, _ in outs),
        grid_spec=pltpu.PrefetchScalarGridSpec(
            num_scalar_prefetch=len(scalars),
            grid=(steps,),
            in_specs=[spec for _, spec in ins],
            out_specs=tuple(spec for _, spec in outs),
            scratch_shapes=scratch,
        ),
        input_output_aliases={len(scalars) + k: v for k, v in (aliases or {}).items()},
        compiler_params=pltpu.CompilerParams(vmem_limit_bytes=VMEM_LIMIT),
        cost_estimate=pl.CostEstimate(
            flops=int(flops), bytes_accessed=int(moved), transcendentals=int(transcendentals)
        ),
        name=name,
    )(*scalars, *[item for item, _ in ins])


def group(count):
    return 2 if count % 2 == 0 else 1


def prepare_kernel(chunks, *refs):
    items, (expand, shrink), (vectors, packed) = refs[:8], refs[8:10], refs[10:]
    width = vectors.shape[1]
    row = 0
    for item in items:
        for start in range(0, item.shape[0], width):
            vectors[row : row + 1, :] = item[pl.ds(start, width)].reshape(1, width)
            row += 1
    quarter = expand.shape[0] // 4
    blocks = expand.shape[1] // width
    tall = shrink.shape[0] // (4 * chunks)
    for index in range(4):
        rows = slice(index * quarter, (index + 1) * quarter)
        for block in range(blocks):
            start = block * quarter
            packed[index, start : start + quarter, :] = expand[
                rows, block * width : (block + 1) * width
            ]
        for number in range(chunks):
            start = blocks * quarter + number * tall
            source = (4 * number + index) * tall
            packed[index, start : start + tall, :] = shrink[source : source + tall, :]


def prepare(chunks, items, weights):
    width = weights[1].shape[1]
    count = sum(item.shape[0] for item in items) // width
    total = sum(item.shape[0] * item.shape[1] for item in weights) // (4 * width)
    return call(
        functools.partial(prepare_kernel, chunks),
        "prepare",
        1,
        (),
        [(item, whole(*item.shape)) for item in (*items, *weights)],
        [
            (like((count, width), F32), whole(count, width)),
            (like((4, total, width), BF16), whole(4, total, width)),
        ],
        [],
        (0, 8 * total * width, 0),
    )


def collect_kernel(*refs):
    out = refs[-1]
    width = out.shape[1]
    singles, triples, expands, tables = refs[:6], refs[6:9], refs[9:12], refs[12:-1]
    out[...] = jnp.zeros_like(out)
    for row, item in enumerate(singles):
        out[row : row + 1, :] = item[...]
    size = width // 3
    for number, item in enumerate(triples):
        for part in range(3):
            row = TRIPLE_BIAS + part
            out[row : row + 1, number * size : (number + 1) * size] = item[
                :, part * size : (part + 1) * size
            ]
    for number, item in enumerate(expands):
        for part in range(item.shape[1] // size):
            row = EXPAND_BIAS + part
            out[row : row + 1, number * size : (number + 1) * size] = item[
                :, part * size : (part + 1) * size
            ]
    total = tables[0][...]
    for item in tables[1:]:
        total = total + item[...]
    for piece in range(3):
        out[TABLES : TABLES + 9, piece * LANES : (piece + 1) * LANES] = total[
            9 * piece : 9 * piece + 9, :
        ]


def collect(singles, triples, expands, tables):
    width = singles[0].shape[1]
    items = (*singles, *triples, *expands, *tables)
    return call(
        collect_kernel,
        "collect",
        1,
        (),
        [(item, whole(*item.shape)) for item in items],
        [(like((24, width), F32), whole(24, width))],
        [],
        (0, 16 * 24 * width, 0),
    )[0]


def attend_kernel(
    slabs, before, meta, windows, tokens, vectors, height, width_table, places, blocks, selectors,
    *rest,
):
    (
        rows_out, normed_out, triple_out, probs_out, attended_out,
        full, staged, weight, tables, masked_keys, sems,
    ) = rest[-11:]
    pieces = rest[:4]
    step = pl.program_id(0)
    base_slab = (step + before) * slabs
    width = full.shape[2]

    @pl.when(step == 0)
    def _():
        copies = load_rows(meta, pieces, weight, sems)
        tables[...] = build_tables(height, width_table, places, blocks)
        wait_all(copies)

    gather_quarters(step == 0, tokens, staged, full, base_slab, slabs)
    rows = full[...].reshape(slabs * ROWS, width)
    unit, _ = normalize(rows)
    normed = unit * vectors[FIRST_GAIN : FIRST_GAIN + 1] + vectors[FIRST_SHIFT : FIRST_SHIFT + 1]
    normed = normed.astype(BF16)
    rows_out[...] = rows.astype(BF16).reshape(slabs, ROWS, width)
    normed_out[...] = normed.reshape(slabs, ROWS, width)
    for part in range(3):
        columns = slice(part * width, (part + 1) * width)
        bias = vectors[TRIPLE_BIAS + part : TRIPLE_BIAS + part + 1]
        triple = dot(normed, weight[:, columns]) + bias
        triple_out[:, :, columns] = triple.astype(BF16).reshape(slabs, ROWS, width)

    lane = lax.broadcasted_iota(jnp.int32, (ROWS, LANES), 1)
    within = lane & (SEG - 1)
    upper = lane >= HD
    quads = HEADS // QUAD
    for slab in range(slabs):
        allowed = valid_rows(windows[meta[0], base_slab + slab])
        penalty = jnp.where((lane == WIN) & jnp.logical_not(allowed), PENALTY, 0.0).astype(BF16)
        for head in range(QUAD):
            masked_keys[slab, head] = selectors[head] + penalty

    sides = (jnp.logical_not(upper), upper)
    zero = jnp.zeros((ROWS, LANES), BF16)
    halves_of = lambda values, head: jnp.where(
        sides[head & 1], values[:, (head >> 1) * LANES : ((head >> 1) + 1) * LANES], zero
    )
    every = [(slab, head) for slab in range(slabs) for head in range(QUAD)]
    constant = jnp.where(lane == WIN, 1.0, 0.0)

    def one_quad(quad, carry):
        base = pl.multiple_of(quad * QUAD * HD, LANES)
        near = pl.multiple_of(base + width, LANES)
        far = pl.multiple_of(base + 2 * width, LANES)
        queries = [triple_out[slab, :, pl.ds(base, QUAD * HD)] for slab in range(slabs)]
        keys = [triple_out[slab, :, pl.ds(near, QUAD * HD)] for slab in range(slabs)]
        values = [triple_out[slab, :, pl.ds(far, QUAD * HD)] for slab in range(slabs)]
        terms = [dot(item, tables[...]) for item in queries]
        lefts = []
        for slab in range(slabs):
            high = roll_rows(terms[slab][:, :LANES], False)
            wide = roll_rows(terms[slab][:, LANES:], True)
            relative = jnp.where(
                within < WIN, high, jnp.where((within >= 16) & (within < 16 + WIN), wide, constant)
            ).astype(BF16)
            scaled = queries[slab] * jnp.asarray(HD**-0.5, BF16)
            lefts.append(
                [
                    jnp.concatenate([scaled[:, pair * LANES : (pair + 1) * LANES], relative], axis=1)
                    for pair in range(QUAD // 2)
                ]
            )
        scores = [
            dot_t(
                lefts[slab][head >> 1],
                jnp.concatenate([halves_of(keys[slab], head), masked_keys[slab, head]], axis=1),
            )
            for slab, head in every
        ]
        probs = []
        for (slab, head), score in zip(every, scores):
            maxima = jnp.max(score, axis=-1, keepdims=True)
            exponent = jnp.exp(score - maxima)
            summed = jnp.sum(exponent, axis=-1, keepdims=True)
            probs.append((exponent * (1.0 / summed)).astype(BF16))
            probs_out[slab, quad * QUAD + head] = probs[-1]
        parts = [dot(prob, halves_of(values[slab], head)) for (slab, head), prob in zip(every, probs)]
        for slab in range(slabs):
            mine = parts[slab * QUAD : (slab + 1) * QUAD]
            mixed = jnp.concatenate(
                [mine[2 * pair] + mine[2 * pair + 1] for pair in range(QUAD // 2)], axis=1
            )
            allowed = valid_rows(windows[meta[0], base_slab + slab])
            mixed = jnp.where(allowed, mixed, 0.0)
            attended_out[slab, :, pl.ds(base, QUAD * HD)] = mixed.astype(BF16)
        return carry

    lax.fori_loop(0, quads, one_quad, 0, unroll=True)


def attend(before, steps, meta, windows, tokens, vectors, tables, selectors, pieces, kept):
    parts, rows_dev, slots, width = tokens.shape
    slabs = group(slots)
    block3 = lambda columns: pl.BlockSpec((slabs, ROWS, columns), lambda i, *_: (i + before, 0, 0))
    rows = steps * slabs * ROWS
    ins = [(item, whole(*item.shape)) for item in (tokens, vectors, *tables, selectors)]
    ins += [(item, ANY) for item in pieces]
    aliases = {}
    if kept is not None:
        aliases = {len(ins) + n: n for n in range(len(kept))}
        ins += [(item, ANY) for item in kept]
    return call(
        functools.partial(attend_kernel, slabs, before),
        "attend",
        steps,
        (meta, windows),
        ins,
        [
            (like((slots, ROWS, width), BF16), block3(width)),
            (like((slots, ROWS, width), BF16), block3(width)),
            (like((slots, ROWS, 3 * width), BF16), block3(3 * width)),
            (
                like((slots, HEADS, ROWS, ROWS), BF16),
                pl.BlockSpec((slabs, HEADS, ROWS, ROWS), lambda i, *_: (i + before, 0, 0, 0)),
            ),
            (like((slots, ROWS, width), BF16), block3(width)),
        ],
        [
            pltpu.VMEM((slabs, ROWS, width), F32),
            pltpu.VMEM((parts * width // LANES, rows_dev * slots, LANES), F32),
            pltpu.VMEM((width, 3 * width), BF16),
            pltpu.VMEM((2 * LANES, 2 * LANES), BF16),
            pltpu.VMEM((slabs, QUAD, ROWS, LANES), BF16),
            pltpu.SemaphoreType.DMA((10,)),
        ],
        (
            6 * rows * width * width + steps * slabs * HEADS * 4 * ROWS * ROWS * 256,
            rows * (width * 16 + HEADS * 512) + width * width * 6,
            steps * slabs * HEADS * ROWS * ROWS,
        ),
        aliases,
    )


def project_kernel(
    slabs, first, meta, windows, attended, rows_in, grads, vectors, *rest,
):
    pieces = rest[:4]
    middle_out, normed_out, branch_out, shrink_bias_out, full, staged, weight, sems = rest[4:]
    step = pl.program_id(0)

    @pl.when(step == 0)
    def _():
        wait_all(load_rows(meta, pieces, weight, sems, first))
        shrink_bias_out[...] = jnp.zeros_like(shrink_bias_out)

    width = full.shape[2]
    count = slabs * ROWS
    middle = (
        rows_in[...].reshape(count, width).astype(F32)
        + dot(attended[...].reshape(count, width), weight[...])
        + vectors[OUTPUT_BIAS : OUTPUT_BIAS + 1]
    )
    unit, _ = normalize(middle)
    middle_out[...] = middle
    normed = unit * vectors[SECOND_GAIN : SECOND_GAIN + 1] + vectors[SECOND_SHIFT : SECOND_SHIFT + 1]
    normed_out[...] = normed.astype(BF16)
    gather_quarters(step == 0, grads, staged, full, step * slabs, slabs)
    for slab in range(slabs):
        allowed = valid_rows(windows[meta[0], step * slabs + slab])
        branch = jnp.where(allowed, full[slab], 0.0)
        branch_out[slab * ROWS : (slab + 1) * ROWS, :] = branch.astype(BF16)
        shrink_bias_out[...] += jnp.sum(branch, axis=0, keepdims=True)


def project(meta, windows, attended, rows_in, grads, vectors, pieces):
    parts, rows_dev, slots, width = grads.shape
    slabs = group(slots)
    block = pl.BlockSpec((slabs, ROWS, width), lambda i, *_: (i, 0, 0))
    flat = pl.BlockSpec((slabs * ROWS, width), lambda i, *_: (i, 0))
    rows = slots * ROWS
    return call(
        functools.partial(project_kernel, slabs, 3 * width),
        "project",
        slots // slabs,
        (meta, windows),
        [(attended, block), (rows_in, block)]
        + [(item, whole(*item.shape)) for item in (grads, vectors)]
        + [(item, ANY) for item in pieces],
        [
            (like((rows, width), F32), flat),
            (like((rows, width), BF16), flat),
            (like((rows, width), BF16), flat),
            (like((1, width), F32), whole(1, width)),
        ],
        [
            pltpu.VMEM((slabs, ROWS, width), F32),
            pltpu.VMEM((parts * width // LANES, rows_dev * slots, LANES), F32),
            pltpu.VMEM((width, width), BF16),
            pltpu.SemaphoreType.DMA((10,)),
        ],
        (2 * rows * width * width, rows * width * 14, 0),
    )


def gate_both(hidden):
    half = 0.5 * (1.0 + lax.erf(hidden * 0.7071067811865476))
    density = jnp.exp(hidden * hidden * -0.5) * 0.3989422804014327
    return hidden * half, half + hidden * density


def feed_kernel(number, first, unit, meta, normed, branch, vectors, *rest):
    pieces, rest = rest[:10], rest[10:]
    if not first:
        out_in, grad_in = rest[:2]
    out_acc, grad_acc, keep, send, bias_grad, expand, shrink, acc_e, acc_s, sems = rest[-10:]
    step = pl.program_id(0)
    last = pl.num_programs(0) - 1
    width, chunk = acc_e.shape
    blocks = chunk // unit

    @pl.when(step == 0)
    def _():
        pairs = []
        quarter, tall = expand.shape[1], shrink.shape[1]
        here = blocks * quarter + number * tall
        columns = pl.ds(number * unit, unit)
        for source, who in zip(pieces[:2], (0, 1)):
            places = pl.ds(4 * (meta[0] ^ who), 4)
            for block in range(blocks):
                pairs.append(
                    (
                        source.at[:, pl.ds(block * quarter, quarter), columns],
                        expand.at[places, :, pl.ds(block * unit, unit)],
                    )
                )
            pairs.append((source.at[:, pl.ds(here, tall), :], shrink.at[places]))
        for fetched, places in zip((pieces[2:6], pieces[6:10]), quarter_places(meta)):
            for source, place in zip(fetched, places):
                for block in range(blocks):
                    pairs.append(
                        (
                            source.at[pl.ds(block * quarter, quarter), columns],
                            expand.at[place, :, pl.ds(block * unit, unit)],
                        )
                    )
                pairs.append((source.at[pl.ds(here, tall), :], shrink.at[place]))
        copies = start_copies(pairs, sems)
        acc_e[...] = jnp.zeros_like(acc_e)
        acc_s[...] = jnp.zeros_like(acc_s)
        bias_grad[...] = jnp.zeros_like(bias_grad)
        wait_all(copies)

    rows = normed[...]
    grads = branch[...]
    bias = jnp.concatenate(
        [
            vectors[
                EXPAND_BIAS + block : EXPAND_BIAS + block + 1, number * unit : (number + 1) * unit
            ]
            for block in range(blocks)
        ],
        axis=1,
    )
    whole_expand = expand[...].reshape(width, chunk)
    whole_shrink = shrink[...].reshape(chunk, width)
    hidden = dot(rows, whole_expand) + bias
    d_active = dot_t(grads, whole_shrink)
    active, slope = gate_both(hidden)
    active = active.astype(BF16)
    back = (d_active * slope).astype(BF16)
    bias_grad[...] += jnp.sum(back.astype(F32), axis=0, keepdims=True)
    acc_s[...] += dot_rows(active, grads)
    acc_e[...] += dot_rows(rows, back)
    total_out = dot(active, whole_shrink)
    total_grad = dot_t(back, whole_expand)
    if first:
        out_acc[...] = total_out.astype(BF16)
        grad_acc[...] = total_grad.astype(BF16)
    else:
        out_acc[...] = (out_in[...].astype(F32) + total_out).astype(BF16)
        grad_acc[...] = (grad_in[...].astype(F32) + total_grad).astype(BF16)

    @pl.when(step == last)
    def _():
        height = width // 4
        third = height // 3
        for index in range(4):
            target = (send if index & 1 else keep).at[index >> 1]
            start = pl.multiple_of((meta[0] ^ index) * unit, 16)
            target[:unit, :] = acc_s[pl.ds(start, unit), :].astype(BF16)
            start = pl.multiple_of((meta[0] ^ index) * height, 16)
            target[unit : unit + height, :] = acc_e[pl.ds(start, height), :width].astype(BF16)
            for piece in range(3):
                here = pl.multiple_of(start + piece * third, 16)
                target[unit + height :, piece * unit : (piece + 1) * unit] = acc_e[
                    pl.ds(here, third), width:
                ].astype(BF16)


def feed(number, count, meta, normed, branch, vectors, pieces, kept):
    rows, width = normed.shape
    chunk = 4 * width // count
    unit = chunk // 4
    block_rows = 2 * ROWS
    block = pl.BlockSpec((block_rows, width), lambda i, *_: (i, 0))
    ins = [(normed, block), (branch, block), (vectors, whole(*vectors.shape))]
    ins += [(item, ANY) for item in pieces]
    aliases = {}
    if kept is not None:
        aliases = {len(ins) + n: n for n in range(2)}
        ins += [(item, block) for item in kept]
    payload = (2, unit + unit, width)
    return call(
        functools.partial(feed_kernel, number, kept is None, unit),
        "feed",
        rows // block_rows,
        (meta,),
        ins,
        [
            (like((rows, width), BF16), block),
            (like((rows, width), BF16), block),
            (like(payload, BF16), whole(*payload)),
            (like(payload, BF16), whole(*payload)),
            (like((1, chunk), F32), whole(1, chunk)),
        ],
        [
            pltpu.VMEM((16, width // 16, chunk), BF16),
            pltpu.VMEM((16, chunk // 16, width), BF16),
            pltpu.VMEM((width, chunk), F32),
            pltpu.VMEM((chunk, width), F32),
            pltpu.SemaphoreType.DMA((64,)),
        ],
        (12 * rows * width * chunk, rows * width * 12 + width * chunk * 8, 2 * rows * chunk),
        aliases,
    )


def middle_kernel(
    slabs, first, meta, windows, middle, out_acc, grad_acc, branch, attended, vectors,
    *rest,
):
    pieces = rest[:4]
    (
        result_out, d_middle_out, d_attended_out, keep, send, output_bias_grad, gain_grad,
        shift_grad, full, staged, weight, acc, sems,
    ) = rest[4:]
    step = pl.program_id(0)
    last = pl.num_programs(0) - 1

    @pl.when(step == 0)
    def _():
        copies = load_rows(meta, pieces, weight, sems, first)
        acc[...] = jnp.zeros_like(acc)
        output_bias_grad[...] = jnp.zeros_like(output_bias_grad)
        gain_grad[...] = jnp.zeros_like(gain_grad)
        shift_grad[...] = jnp.zeros_like(shift_grad)
        wait_all(copies)

    width = full.shape[2]
    count = slabs * ROWS
    rows = middle[...]
    result = rows + out_acc[...].astype(F32) + vectors[SHRINK_BIAS : SHRINK_BIAS + 1]
    full[...] = result.reshape(slabs, ROWS, width)
    scatter_quarters(step == last, full, staged, result_out, step * slabs, slabs)
    unit, scale = normalize(rows)
    grad = grad_acc[...].astype(F32)
    gain_grad[...] += jnp.sum(grad * unit, axis=0, keepdims=True)
    shift_grad[...] += jnp.sum(grad, axis=0, keepdims=True)
    d_middle = branch[...].astype(F32) + normalize_back(
        unit, scale, grad, vectors[SECOND_GAIN : SECOND_GAIN + 1]
    )
    d_output = d_middle.astype(BF16)
    d_middle_out[...] = d_output
    output_bias_grad[...] += jnp.sum(d_output.astype(F32), axis=0, keepdims=True)
    acc[...] += dot_rows(attended[...].reshape(count, width), d_output)
    d_attended = dot_t(d_output, weight[...]).reshape(slabs, ROWS, width)
    for slab in range(slabs):
        allowed = valid_rows(windows[meta[0], step * slabs + slab])
        d_attended_out[slab] = jnp.where(allowed, d_attended[slab], 0.0).astype(BF16)

    @pl.when(step == last)
    def _():
        write_owned(acc, meta, keep, send, 1)


def middle_back(meta, windows, rows_dev, middle, out_acc, grad_acc, branch, attended, vectors, pieces):
    slots, _, width = attended.shape
    parts = WROWS // rows_dev
    slabs = group(slots)
    block = pl.BlockSpec((slabs, ROWS, width), lambda i, *_: (i, 0, 0))
    flat = pl.BlockSpec((slabs * ROWS, width), lambda i, *_: (i, 0))
    rows = slots * ROWS
    vec = (like((1, width), F32), whole(1, width))
    payload = (2, width // 4, width)
    quarter = (parts, rows_dev, slots, width)
    return call(
        functools.partial(middle_kernel, slabs, 3 * width),
        "middle",
        slots // slabs,
        (meta, windows),
        [
            (middle, flat), (out_acc, flat), (grad_acc, flat), (branch, flat), (attended, block),
            (vectors, whole(*vectors.shape)),
        ]
        + [(item, ANY) for item in pieces],
        [
            (like(quarter, BF16), whole(*quarter)),
            (like((rows, width), BF16), flat),
            (like((slots, ROWS, width), BF16), block),
            (like(payload, BF16), whole(*payload)),
            (like(payload, BF16), whole(*payload)),
            vec,
            vec,
            vec,
        ],
        [
            pltpu.VMEM((slabs, ROWS, width), F32),
            pltpu.VMEM((parts * width // LANES, rows_dev * slots, LANES), F32),
            pltpu.VMEM((width, width), BF16),
            pltpu.VMEM((width, width), F32),
            pltpu.SemaphoreType.DMA((10,)),
        ],
        (4 * rows * width * width, rows * width * 18, 0),
    )


def attend_back_kernel(
    slabs, across, meta, normed, queries_in, keys_in, values_in, probs_in, d_mixed_in, mixed_in,
    height, width_table, places, blocks, selectors, sums,
    d_queries, d_keys, d_values, keep, send, bias_grad, table_out, grads, acc, tables, table_grad,
):
    step = pl.program_id(0)
    last = pl.num_programs(0) - 1
    wide4 = QUAD * HD

    @pl.when(step == 0)
    def _():
        acc[...] = jnp.zeros_like(acc)
        bias_grad[...] = jnp.zeros_like(bias_grad)
        table_grad[...] = jnp.zeros_like(table_grad)
        tables[...] = build_tables(height, width_table, places, blocks)

    lane = lax.broadcasted_iota(jnp.int32, (ROWS, LANES), 1)
    within = lane & (SEG - 1)
    upper = lane >= HD
    zero = jnp.zeros((ROWS, LANES), BF16)

    sides = (jnp.logical_not(upper), upper)
    halves_of = lambda items, head: jnp.where(
        sides[head & 1], items[:, (head >> 1) * LANES : ((head >> 1) + 1) * LANES], zero
    )
    minus = [
        jnp.where((lane == 2 * head) | (lane == 2 * head + 1), -1.0, 0.0).astype(BF16)
        for head in range(QUAD)
    ]
    every = [(slab, head) for slab in range(slabs) for head in range(QUAD)]
    lefts = []
    for slab in range(slabs):
        d_mixed = d_mixed_in[slab]
        product = d_mixed.astype(F32) * mixed_in[slab].astype(F32)
        product_high = product.astype(BF16)
        product_low = (product - product_high.astype(F32)).astype(BF16)
        inner = dot(product_high, sums[...]) + dot(product_low, sums[...])
        inner_high = inner.astype(BF16)
        inner_low = (inner - inner_high.astype(F32)).astype(BF16)
        inner = jnp.where((lane & 1) == 0, inner_high, inner_low)
        lefts.append(
            [
                jnp.concatenate([d_mixed[:, pair * LANES : (pair + 1) * LANES], inner], axis=1)
                for pair in range(QUAD // 2)
            ]
        )
    d_probs = [
        dot_t(
            lefts[slab][head >> 1],
            jnp.concatenate([halves_of(values_in[slab], head), minus[head]], axis=1),
        )
        for slab, head in every
    ]
    parts_v = [
        dot_rows(probs_in[slab, head], halves_of(d_mixed_in[slab], head)) for slab, head in every
    ]
    d_scores = [
        (probs_in[slab, head].astype(F32) * item).astype(BF16)
        for (slab, head), item in zip(every, d_probs)
    ]
    backs = [
        dot(
            item,
            jnp.concatenate([halves_of(keys_in[slab], head), selectors[head]], axis=1),
        )
        for (slab, head), item in zip(every, d_scores)
    ]
    parts_k = [
        dot_rows(item, halves_of(queries_in[slab], head))
        for (slab, head), item in zip(every, d_scores)
    ]
    scale = HD**-0.5
    joined = lambda items: jnp.concatenate(
        [items[2 * pair] + items[2 * pair + 1] for pair in range(QUAD // 2)], axis=1
    )
    for slab in range(slabs):
        mine = slice(slab * QUAD, (slab + 1) * QUAD)
        d_relative = backs[slab * QUAD][:, LANES:]
        for head in range(1, QUAD):
            d_relative = d_relative + backs[slab * QUAD + head][:, LANES:]
        high = roll_rows(jnp.where(within < WIN, d_relative, 0.0), False)
        wide = roll_rows(jnp.where((within >= 16) & (within < 16 + WIN), d_relative, 0.0), True)
        d_terms = jnp.concatenate([high, wide], axis=1).astype(BF16)
        dq = joined([item[:, :LANES] for item in backs[mine]]) * scale
        dq = (dq + dot_t(d_terms, tables[...])).astype(BF16)
        table_grad[...] += dot_rows(queries_in[slab], d_terms)
        dk = (joined(parts_k[mine]) * scale).astype(BF16)
        dv = joined(parts_v[mine]).astype(BF16)
        d_queries[slab] = dq
        d_keys[slab] = dk
        d_values[slab] = dv
        grads[slab] = jnp.concatenate([dq, dk, dv], axis=1)

    width = normed.shape[2]
    both = grads[...].reshape(slabs * ROWS, 3 * wide4)
    bias_grad[...] += jnp.sum(both.astype(F32), axis=0, keepdims=True)
    acc[...] += dot_rows(normed[...].reshape(slabs * ROWS, width), both)

    @pl.when(step == last)
    def _():
        write_owned(acc, meta, keep, send, across)
        masked = table_grad[...] * blocks[...].astype(F32)
        folded = masked[:HD]
        for head in range(1, QUAD):
            folded = folded + masked[head * HD : (head + 1) * HD]
        high = folded.astype(BF16)
        low = (folded - high.astype(F32)).astype(BF16)
        for which in range(2):
            table_out[:, which * HD : (which + 1) * HD] = dot_t(places[which], high) + dot_t(
                places[which], low
            )


def attend_back(quad, across, meta, normed, triple, probs, d_mixed, mixed, tables, selectors, sums):
    slots, _, width = normed.shape
    slabs = group(slots)
    wide4 = QUAD * HD
    quads = HEADS // QUAD
    column = lambda where: pl.BlockSpec((slabs, ROWS, wide4), lambda i, *_: (i, 0, where))
    narrow = (
        like((slots, ROWS, wide4), BF16),
        pl.BlockSpec((slabs, ROWS, wide4), lambda i, *_: (i, 0, 0)),
    )
    rows = slots * ROWS
    payload = (2, width // 4, 3 * wide4)
    return call(
        functools.partial(attend_back_kernel, slabs, across),
        "attend_back",
        slots // slabs,
        (meta,),
        [
            (normed, pl.BlockSpec((slabs, ROWS, width), lambda i, *_: (i, 0, 0))),
            (triple, column(quad)),
            (triple, column(quads + quad)),
            (triple, column(2 * quads + quad)),
            (probs, pl.BlockSpec((slabs, QUAD, ROWS, ROWS), lambda i, *_: (i, quad, 0, 0))),
            (d_mixed, column(quad)),
            (mixed, column(quad)),
        ]
        + [(item, whole(*item.shape)) for item in (*tables, selectors, sums)],
        [
            narrow,
            narrow,
            narrow,
            (like(payload, BF16), whole(*payload)),
            (like(payload, BF16), whole(*payload)),
            (like((1, 3 * wide4), F32), whole(1, 3 * wide4)),
            (like((REL, 2 * HD), F32), whole(REL, 2 * HD)),
        ],
        [
            pltpu.VMEM((slabs, ROWS, 3 * wide4), BF16),
            pltpu.VMEM((width, 3 * wide4), F32),
            pltpu.VMEM((2 * LANES, 2 * LANES), BF16),
            pltpu.VMEM((2 * LANES, 2 * LANES), F32),
        ],
        (
            2 * rows * width * 3 * wide4 + slots * QUAD * 8 * ROWS * ROWS * 256,
            rows * (width * 2 + wide4 * 16 + QUAD * 512),
            0,
        ),
    )


def first_kernel(slabs, meta, rows_in, d_middle, vectors, *rest):
    grads, pieces = rest[:9], rest[9:13]
    tokens_out, gain_grad, shift_grad, full, staged, weight, sems = rest[13:]
    step = pl.program_id(0)
    last = pl.num_programs(0) - 1

    @pl.when(step == 0)
    def _():
        copies = load_rows(meta, pieces, weight, sems)
        gain_grad[...] = jnp.zeros_like(gain_grad)
        shift_grad[...] = jnp.zeros_like(shift_grad)
        wait_all(copies)

    width = full.shape[2]
    count = slabs * ROWS
    wide4 = QUAD * HD
    both = jnp.concatenate([grad[...].reshape(count, wide4) for grad in grads], axis=1)
    total = dot_t(both, weight[...])
    unit, scale = normalize(rows_in[...].reshape(count, width).astype(F32))
    gain_grad[...] += jnp.sum(total * unit, axis=0, keepdims=True)
    shift_grad[...] += jnp.sum(total, axis=0, keepdims=True)
    back = normalize_back(unit, scale, total, vectors[FIRST_GAIN : FIRST_GAIN + 1])
    full[...] = (d_middle[...].astype(F32) + back).reshape(slabs, ROWS, width)
    scatter_quarters(step == last, full, staged, tokens_out, step * slabs, slabs)


def first_back(before, steps, meta, rows_dev, rows_in, d_middle, vectors, grads, pieces):
    slots, _, width = rows_in.shape
    parts = WROWS // rows_dev
    slabs = group(slots)
    wide4 = QUAD * HD
    block = pl.BlockSpec((slabs, ROWS, width), lambda i, *_: (i + before, 0, 0))
    flat = pl.BlockSpec((slabs * ROWS, width), lambda i, *_: (i + before, 0))
    narrow = pl.BlockSpec((slabs, ROWS, wide4), lambda i, *_: (i + before, 0, 0))
    rows = steps * slabs * ROWS
    quarter = (parts, rows_dev, steps * slabs, width)
    return call(
        functools.partial(first_kernel, slabs),
        "first_back",
        steps,
        (meta,),
        [(rows_in, block), (d_middle, flat), (vectors, whole(*vectors.shape))]
        + [(item, narrow) for item in grads]
        + [(item, ANY) for item in pieces],
        [(like(quarter, BF16), whole(*quarter))] + [(like((1, width), F32), whole(1, width))] * 2,
        [
            pltpu.VMEM((slabs, ROWS, width), F32),
            pltpu.VMEM((parts * width // LANES, rows_dev * steps * slabs, LANES), F32),
            pltpu.VMEM((width, 3 * width), BF16),
            pltpu.SemaphoreType.DMA((10,)),
        ],
        (6 * rows * width * width, rows * width * 14, 0),
    )


def join_halves(meta, items, staged):
    upper = meta[1] > 0
    for number, both in enumerate(staged):
        mine, other = items[2 * number], items[2 * number + 1]
        half = mine.shape[0]

        @pl.when(upper)
        def _():
            both[:half] = other[...]
            both[half:] = mine[...]

        @pl.when(jnp.logical_not(upper))
        def _():
            both[:half] = mine[...]
            both[half:] = other[...]


def finish_feed_kernel(unit, pairs, meta, *refs):
    items, (expand_out, shrink_out, output_out), staged = (
        refs[: 2 * pairs], refs[2 * pairs : 2 * pairs + 3], refs[2 * pairs + 3 :]
    )
    join_halves(meta, items, staged)
    output_out[...] = staged[-1][2 * unit :, :].astype(F32)
    shard, width = expand_out.shape[0], shrink_out.shape[1]
    third = shard // 3
    parts = width // shard
    for number, both in enumerate(staged):
        here = number * unit
        shrink_out[here : here + unit, :] = both[:unit, :].astype(F32)
        for block in range(parts - 1):
            start = block * width + here
            expand_out[:, start : start + unit] = both[
                unit : unit + shard, block * unit : (block + 1) * unit
            ].astype(F32)
        start = (parts - 1) * width + here
        for piece in range(3):
            expand_out[piece * third : (piece + 1) * third, start : start + unit] = both[
                unit + shard : 2 * unit, piece * unit : (piece + 1) * unit
            ].astype(F32)


def finish_rest_kernel(pairs, meta, *refs):
    items, small, refs = refs[: 2 * pairs], refs[2 * pairs], refs[2 * pairs + 1 :]
    triple_out, refs = refs[0], refs[1:]
    vectors, tables, staged = refs[:8], refs[8:10], refs[10:]
    join_halves(meta, items, staged)
    shard, width = triple_out.shape[0], small.shape[1]
    wide4 = QUAD * HD
    quads = [both[n : n + shard, :] for both in staged for n in range(0, both.shape[0], shard)]
    for quad, values in enumerate(quads):
        for part in range(3):
            start = part * width + quad * wide4
            triple_out[:, start : start + wide4] = values[
                :, part * wide4 : (part + 1) * wide4
            ].astype(F32)
    row = 0
    for item in vectors:
        for start in range(0, item.shape[0], width):
            item[pl.ds(start, width)] = small[row : row + 1, :].reshape(width)
            row += 1
    for which, item in enumerate(tables):
        for piece in range(3):
            start = piece * LANES + which * HD
            item[9 * piece : 9 * piece + 9, :] = small[TABLES : TABLES + 9, start : start + HD]


def finish(kernel, name, meta, shares, others, outs):
    items = [item for pair in shares for item in pair]
    return call(
        kernel,
        name,
        1,
        (meta,),
        [(item, whole(*item.shape)) for item in (*items, *others)],
        [(like(item.shape, F32), whole(*item.shape)) for item in outs],
        [pltpu.VMEM((2 * mine.shape[0], mine.shape[1]), BF16) for mine, _ in shares],
        (0, sum(6 * item.size for item in items), 0),
    )


def swap(values, axis, bits):
    count = lax.axis_size(axis)
    return lax.ppermute(values, axis, [(n, n ^ bits) for n in range(count)])


def swap_diagonal(values):
    across = lax.axis_size("seq")
    count = lax.axis_size("dp") * across
    perm = [(n, (n // across ^ 1) * across + (n % across ^ 1)) for n in range(count)]
    return lax.ppermute(values, ("dp", "seq"), perm)


def spread(far):
    return far, swap(far, "dp", 1), swap(far, "seq", 1), swap_diagonal(far)


def exchange_windows(values):
    return lax.all_to_all(values, "tensor", split_axis=0, concat_axis=0, tiled=True)


def after(values, *others):
    return lax.optimization_barrier((values, *others))[0]


def far_quarter(packed):
    which = 2 * (lax.axis_index("dp") & 1) + (lax.axis_index("seq") & 1)
    return lax.dynamic_index_in_dim(packed, which, axis=0, keepdims=False)


def add(*items):
    total = items[0].astype(F32)
    for item in items[1:]:
        total = total + item.astype(F32)
    return total.astype(BF16)


def halves(axis):
    out, bit = [], 1
    while bit < lax.axis_size(axis):
        out.append(bit)
        bit *= 2
    return out


def reduce_stages(payloads, plan, hook=None):
    bits_of = {"c": 1, "y": 2}
    totals = []
    while True:
        keep, send, more = payloads.pop(0)
        (far,) = yield [(send, "tensor", bits_of[plan[0]])]
        totals.append(add(keep, far))
        if not more:
            break
    total = totals[0] if len(totals) == 1 else jnp.concatenate(totals, axis=1)
    spot = lax.axis_index("dp")
    place = lax.axis_index("seq")

    def split(values, upper):
        size = values.shape[-2] // 2
        low, high = values[..., :size, :], values[..., size:, :]
        return jnp.where(upper, high, low), jnp.where(upper, low, high)

    def join(mine, far, upper):
        return jnp.concatenate([jnp.where(upper, far, mine), jnp.where(upper, mine, far)], axis=0)

    for letter in plan[1:]:
        if letter == "w":
            total = hook(total)
        elif letter in bits_of:
            (far,) = yield [(total[1], "tensor", bits_of[letter])]
            total = add(total[0], far)
        elif letter == "x":
            for bit in halves("dp"):
                near, far = split(total, (spot & bit) > 0)
                (far,) = yield [(far, "dp", bit)]
                total = add(near, far)
        else:
            if letter == "s":
                near, far = split(total, (place & 1) > 0)
                (far,) = yield [(far, "seq", 1)]
                total = add(near, far)
            for bit in halves("seq"):
                if letter == "s" and bit == 1:
                    continue
                (far,) = yield [(total, "seq", bit)]
                total = add(total, far)
            if letter == "s":
                (far,) = yield [(total, "seq", 1)]
                total = join(total, far, (place & 1) > 0)
    for bit in reversed(halves("dp")):
        (far,) = yield [(total, "dp", bit)]
        if bit > 1:
            total = join(total, far, (spot & bit) > 0)
    return total, far


def sum_stages(values):
    steps = [(axis, bit) for axis in ("tensor", "dp", "seq") for bit in halves(axis)]
    steps = [("tensor", 2)] + [item for item in steps if item != ("tensor", 2)]
    for axis, bit in steps:
        (far,) = yield [(values, axis, bit)]
        values = values + far
    return (values,)


class Exchanges:
    def __init__(self):
        self.running = []
        self.done = {}

    def begin(self, name, stages):
        self.running.append([name, stages, None])

    def step(self, names, token, meta, *extra):
        asked, ended = [], []
        chosen = [entry for entry in self.running if names is None or entry[0] in names]
        arrived = [item for entry in chosen for item in (entry[2] or ())]
        if token is not None and arrived:
            token, *arrived = lax.optimization_barrier((token, *arrived))
        arrived = iter(arrived)
        for entry in chosen:
            name, stages, waiting = entry
            mine = None if waiting is None else [next(arrived) for _ in waiting]
            try:
                asked.append((entry, stages.send(mine)))
            except StopIteration as stop:
                ended.append((name, stop.value))
                self.running.remove(entry)
        values = [item[0] for _, wanted in asked for item in wanted]
        finished = [item for _, pair in ended for item in pair]
        if meta is not None:
            count = len(values)
            meta, *rest = lax.optimization_barrier((meta, *values, *finished, *extra))
            values = rest[:count]
            finished = rest[count : count + len(finished)]
            extra = rest[count + len(finished) :]
        values, finished = iter(values), iter(finished)
        for entry, wanted in asked:
            entry[2] = [swap(next(values), axis, bits) for _, axis, bits in wanted]
        for name, pair in ended:
            self.done[name] = tuple(next(finished) for _ in pair)
        return (token, meta, *extra)

    def finish(self, names):
        while any(entry[0] in names for entry in self.running):
            self.step(names, None, None)


def local(
    tokens,
    out_grad,
    slot_window,
    first_gain,
    first_shift,
    triple_weight,
    triple_bias,
    height_table,
    width_table,
    output_weight,
    output_bias,
    second_gain,
    second_shift,
    expand_weight,
    expand_bias,
    shrink_weight,
    shrink_bias,
):
    micros, images, slots, rows_dev, width = tokens.shape
    parts = lax.axis_size("tensor")
    mine = lax.axis_index("tensor")
    shard = width // parts
    chunks = 3
    unit = width // chunks
    bit = lax.axis_index("dp") & 1
    quarter = 2 * bit + (lax.axis_index("seq") & 1)
    meta = jnp.where(
        jnp.arange(3) == 0, mine, jnp.where(jnp.arange(3) == 1, bit, quarter)
    ).astype(jnp.int32)

    by_image = lambda values: jnp.swapaxes(values, 2, 3).reshape(parts, rows_dev, slots, width)
    to_image = lambda values: jnp.swapaxes(
        values.reshape(micros, images, rows_dev, slots, width), 2, 3
    )
    windows = slot_window.reshape(parts, slots)

    far = jnp.concatenate(
        [
            far_quarter(triple_weight.reshape(4, shard // 4, -1)),
            far_quarter(output_weight.reshape(4, shard // 4, -1)),
        ],
        axis=1,
    )
    far = swap(far, "tensor", 2)
    near_triple = swap(triple_weight, "tensor", 1)
    near_output = swap(output_weight, "tensor", 1)
    vectors, packed_rest = prepare(
        chunks,
        (
            first_gain, first_shift, output_bias, second_gain, second_shift, shrink_bias,
            triple_bias, expand_bias,
        ),
        (expand_weight, shrink_weight),
    )
    sums = np.zeros((QUAD * HD, LANES), np.float32)
    for head in range(QUAD):
        sums[head * HD : (head + 1) * HD, 2 * head : 2 * head + 2] = 1.0
    sums = jnp.asarray(sums, BF16)
    ahead = (height_table, width_table, table_places(False), head_blocks(False))
    behind = (height_table, width_table, table_places(True), head_blocks(True))
    first_rest = far_quarter(packed_rest)
    far, vectors, packed_rest, first_rest, meta, own_tokens, near_triple, near_output = (
        lax.optimization_barrier(
            (
                far, vectors, packed_rest, first_rest, meta, by_image(tokens), near_triple,
                near_output,
            )
        )
    )
    rows_in = exchange_windows(own_tokens)
    fetched = jnp.stack(spread(far))
    crossed = swap(fetched, "tensor", 1)

    packed, first_rest, rows_in, fetched, crossed = lax.optimization_barrier(
        (packed_rest, first_rest, rows_in, fetched, crossed)
    )
    triple_pieces = (triple_weight, near_triple, fetched, crossed)
    output_pieces = (output_weight, near_output, fetched, crossed)
    far = swap(first_rest, "tensor", 2)
    near = swap(packed, "tensor", 1)
    steps = slots // group(slots)
    early = max(1, steps // 4)
    selectors = key_selectors(False)
    kept = attend(
        0, early, meta, windows, rows_in, vectors, ahead, selectors, triple_pieces, None
    )
    kept = list(kept)
    kept[4], far, own_grads = lax.optimization_barrier((kept[4], far, by_image(out_grad)))
    meta, far, near, own_grads = lax.optimization_barrier((meta, far, near, own_grads))
    grads_in = exchange_windows(own_grads)
    fetched = spread(far)
    crossed = (swap(far, "tensor", 1),)
    if early < steps:
        kept = attend(
            early, steps - early, meta, windows, rows_in, vectors, ahead, selectors,
            triple_pieces, kept,
        )
    full_rows, normed, triple, probs, attended = kept
    attended, *others = lax.optimization_barrier((attended, *fetched[1:]))
    meta, *others = lax.optimization_barrier((meta, *others))
    crossed += tuple(swap(item, "tensor", 1) for item in others)
    middle_stage = project(
        meta, windows, attended, full_rows, grads_in, vectors, output_pieces
    )
    shrink_bias_grad = middle_stage[3]
    rest_pieces = (packed, near, far, *others, *crossed)
    middle, normed2, branch = middle_stage[:3]
    exchanges = Exchanges()
    kept = None
    expand_bias_grads = []
    for number in range(chunks):
        *kept, keep, send, bias_grad = feed(
            number, chunks, meta, normed2, branch, vectors, rest_pieces, kept
        )
        plan = ("cyxz", "cyxz", "cxys")[number]
        payloads = [(keep, send, number == chunks - 1)]
        exchanges.begin(("feed", number), reduce_stages(payloads, plan))
        bias_grad, meta = exchanges.step(None, bias_grad, meta)
        expand_bias_grads.append(bias_grad)

    result, d_middle, d_attended, keep, send, output_bias_grad, gain2_grad, shift2_grad = (
        middle_back(
            meta, windows, rows_dev, middle, *kept, branch, attended, vectors, output_pieces
        )
    )
    payloads.append((keep, send, False))
    output_bias_grad, meta = exchanges.step(None, output_bias_grad, meta)
    result = exchange_windows(result)

    quad_grads, triple_bias_grads, table_grads = [], [], []
    for quad in range(HEADS // QUAD):
        dq, dk, dv, keep, send, bias_grad, table_grad = attend_back(
            quad, 1, meta, normed, triple, probs, d_attended, attended, behind, key_selectors(True), sums
        )
        if quad == 0:
            payloads = [(keep, send, True)]
            exchanges.begin(("rest", 0), reduce_stages(payloads, "cyxs"))
        elif quad == 1:
            payloads.append((keep, send, False))
        else:
            hook = lambda total: after(total, *feed_gradients)
            exchanges.begin(("rest", 1), reduce_stages([(keep, send, False)], "cyxz", hook))
        if quad == 1:
            bias_grad, meta, result = exchanges.step(None, bias_grad, meta, result)
        else:
            bias_grad, meta = exchanges.step(None, bias_grad, meta)
        quad_grads.append((dq, dk, dv))
        triple_bias_grads.append(bias_grad)
        table_grads.append(table_grad)
    wide4 = QUAD * HD
    grads9 = [quad_grads[quad][part] for part in range(3) for quad in range(HEADS // QUAD)]
    token_grad, gain1_grad, shift1_grad = first_back(
        0, steps, meta, rows_dev, full_rows, d_middle, vectors, grads9, triple_pieces
    )
    result = to_image(result)
    gain1_grad, _ = exchanges.step(None, gain1_grad, None)
    small = collect(
        (gain1_grad, shift1_grad, output_bias_grad, gain2_grad, shift2_grad, shrink_bias_grad),
        triple_bias_grads,
        expand_bias_grads,
        table_grads,
    )
    exchanges.begin("small", sum_stages(small))
    exchanges.step(["small"], None, None)
    first_far = exchanges.running[-1][2][0]
    tokens_gradient = to_image(exchange_windows(after(token_grad, first_far)))
    names = [("feed", number) for number in range(chunks)]
    exchanges.finish(names)
    shares = [exchanges.done[name] for name in names]
    feed_gradients = finish(
        functools.partial(finish_feed_kernel, unit, chunks),
        "finish_feed",
        meta,
        shares,
        (),
        (expand_weight, shrink_weight, output_weight),
    )
    expand_gradient, shrink_gradient, output_gradient = feed_gradients
    exchanges.finish([("rest", number) for number in range(2)] + ["small"])
    shares = [exchanges.done["rest", number] for number in range(2)]
    triple_gradient, *outs, high, wide = finish(
        functools.partial(finish_rest_kernel, len(shares)),
        "finish_rest",
        meta,
        shares,
        exchanges.done["small"],
        (
            triple_weight, first_gain, first_shift, output_bias, second_gain, second_shift,
            shrink_bias, triple_bias, expand_bias, height_table, width_table,
        ),
    )
    return (
        result,
        tokens_gradient,
        outs[0],
        outs[1],
        triple_gradient,
        outs[6],
        high,
        wide,
        output_gradient,
        outs[2],
        outs[3],
        outs[4],
        expand_gradient,
        outs[7],
        shrink_gradient,
        outs[5],
    )


def solution(mesh):
    split = P(None, "dp", "seq", "tensor", None)
    rows = P("tensor", None)
    return jax.shard_map(
        local,
        mesh=mesh,
        in_specs=(
            split, split, P(None, "dp", "seq"), P(), P(), rows, P(), P(), P(), rows, P(), P(), P(),
            rows, P(), rows, P(),
        ),
        out_specs=(
            split, split, P(), P(), rows, P(), P(), P(), rows, P(), P(), P(), rows, P(), rows, P(),
        ),
        check_vma=False,
    )
```

```python
import functools

import jax
import jax.numpy as jnp
import numpy as np
from jax import lax
from jax.experimental import pallas as pl
from jax.experimental.pallas import tpu as pltpu
from jax.sharding import PartitionSpec as P

HEADS = 12
HD = 64
WIN = 14
GRID = 64
WGRID = 5
WROWS = WIN * WIN
ROWS = 200
QUAD = 4
LANES = 128
REL = 2 * WIN - 1
SEG = 32
EPSILON = 1e-06
PENALTY = -1e9

F32 = jnp.float32
BF16 = jnp.bfloat16
FIRST_GAIN, FIRST_SHIFT, OUTPUT_BIAS, SECOND_GAIN, SECOND_SHIFT, SHRINK_BIAS = range(6)
TRIPLE_BIAS, EXPAND_BIAS, TABLES = 6, 9, 13
VMEM_LIMIT = 58 * 1024 * 1024


def dot(left, right):
    return lax.dot_general(left, right, (((1,), (0,)), ((), ())), preferred_element_type=F32)


def dot_t(left, right):
    return lax.dot_general(left, right, (((1,), (1,)), ((), ())), preferred_element_type=F32)


def dot_rows(left, right):
    return lax.dot_general(left, right, (((0,), (0,)), ((), ())), preferred_element_type=F32)


def key_selectors(mirrored):
    out = np.zeros((QUAD, ROWS, LANES), np.float32)
    for head in range(QUAD):
        for key in range(WROWS):
            high, wide = key // WIN, key % WIN
            if mirrored:
                high, wide = WIN - 1 - high, WIN - 1 - wide
            out[head, key, SEG * head + high] = 1.0
            out[head, key, SEG * head + 16 + wide] = 1.0
    return jnp.asarray(out, BF16)


def table_places(mirrored):
    out = np.zeros((2, REL, 2 * LANES), np.float32)
    for head in range(QUAD):
        for row in range(REL):
            if mirrored:
                out[0, row, SEG * head + row] = 1.0
                out[1, row, LANES + (SEG * head + 16 + row) % LANES] = 1.0
            else:
                out[0, REL - 1 - row, (SEG * head + row - 13) % LANES] = 1.0
                out[1, REL - 1 - row, LANES + (SEG * head + row + 3) % LANES] = 1.0
    return jnp.asarray(out, BF16)


def head_blocks(mirrored):
    out = np.zeros((QUAD * HD, 2 * LANES), np.float32)
    for head in range(QUAD):
        rows = slice(head * HD, (head + 1) * HD)
        for row in range(REL):
            if mirrored:
                out[rows, SEG * head + row] = 1.0
                out[rows, LANES + (SEG * head + 16 + row) % LANES] = 1.0
            else:
                out[rows, (SEG * head + row - 13) % LANES] = 1.0
                out[rows, LANES + (SEG * head + row + 3) % LANES] = 1.0
    return jnp.asarray(out, BF16)


def valid_rows(window):
    high_place = (window * 13) >> 6
    wide_place = window - high_place * WGRID
    inside = window < WGRID * WGRID
    row = lax.broadcasted_iota(jnp.int32, (ROWS, 1), 0)
    high = (row * 4682) >> 16
    wide = row - high * WIN
    high_limit = jnp.where(inside, GRID - high_place * WIN, 0)
    return (high < high_limit) & (wide < GRID - wide_place * WIN) & (row < WROWS)


def build_tables(height, width, places, blocks):
    both = dot_rows(height[...].astype(BF16), places[0]) + dot_rows(
        width[...].astype(BF16), places[1]
    )
    both = both.astype(BF16)
    return jnp.concatenate([both] * QUAD, axis=0) * blocks[...]


def roll_rows(values, by_width):
    sub = lax.broadcasted_iota(jnp.int32, (8, LANES), 0)
    pieces = []
    for start in range(0, ROWS, 8):
        piece = values[start : start + 8]
        first = start // WIN
        crossing = (first + 1) * WIN - start
        shifts = (first, first + 1)
        if by_width:
            one = pltpu.roll(piece, start - first * WIN, 1, stride=1, stride_axis=0)
        else:
            one = pltpu.roll(piece, first, 1) if first else piece
        if crossing < 8:
            if by_width:
                two = pltpu.roll(piece, LANES - crossing, 1)
                two = pltpu.roll(two, 0, 1, stride=1, stride_axis=0)
            else:
                two = pltpu.roll(piece, shifts[1], 1)
            one = jnp.where(sub < crossing, one, two)
        pieces.append(one)
    return jnp.concatenate(pieces, axis=0)


def normalize(values):
    centre = jnp.mean(values, axis=-1, keepdims=True)
    spread = values - centre
    variance = jnp.mean(spread * spread, axis=-1, keepdims=True)
    scale = lax.rsqrt(variance + EPSILON)
    return spread * scale, scale


def normalize_back(unit, scale, grad, gain):
    scaled = grad * gain
    mean_grad = jnp.mean(scaled, axis=-1, keepdims=True)
    mean_both = jnp.mean(scaled * unit, axis=-1, keepdims=True)
    return (scaled - mean_grad - unit * mean_both) * scale


def quarter_places(meta):
    mine, quarter = meta[0], meta[2]
    return [
        [4 * (mine ^ who) + (quarter ^ flip) for flip in (0, 2, 1, 3)] for who in (2, 3)
    ]


def start_copies(pairs, sems):
    copies = []
    for number, (source, target) in enumerate(pairs):
        copies.append(pltpu.make_async_copy(source, target, sems.at[number]))
    for copy in copies:
        copy.start()
    return copies


def wait_all(copies):
    for copy in copies:
        copy.wait()


def load_rows(meta, pieces, target, sems, first=0):
    own, near, *far = pieces
    columns = target.shape[1]
    quarter = target.shape[0] // 16
    pairs = []
    for source, who in ((own, 0), (near, 1)):
        start = pl.multiple_of(4 * (meta[0] ^ who) * quarter, 16)
        pairs.append((source, target.at[pl.ds(start, 4 * quarter), :]))
    for sources, places in zip(far, quarter_places(meta)):
        for index, place in enumerate(places):
            start = pl.multiple_of(place * quarter, 16)
            pairs.append(
                (sources.at[index, :, pl.ds(first, columns)], target.at[pl.ds(start, quarter), :])
            )
    return start_copies(pairs, sems)


def gather_quarters(first, block, staged, target, base, slabs):
    parts, rows, slots, width = block.shape
    lanes = width // LANES

    @pl.when(first)
    def _():
        for part in range(parts):
            values = block[part].astype(F32).reshape(rows * slots, width)
            for piece in range(lanes):
                staged[part * lanes + piece] = values[:, piece * LANES : (piece + 1) * LANES]
        target[:, parts * rows :, :] = jnp.zeros((slabs, ROWS - parts * rows, width), F32)

    for slab in range(slabs):
        for part in range(parts):
            for piece in range(lanes):
                target[
                    slab, part * rows : (part + 1) * rows, piece * LANES : (piece + 1) * LANES
                ] = staged[part * lanes + piece, pl.ds(base + slab, rows, stride=slots), :]


def scatter_quarters(last, full, staged, block, base, slabs):
    parts, rows, slots, width = block.shape
    lanes = width // LANES
    for slab in range(slabs):
        for part in range(parts):
            for piece in range(lanes):
                staged[part * lanes + piece, pl.ds(base + slab, rows, stride=slots), :] = full[
                    slab, part * rows : (part + 1) * rows, piece * LANES : (piece + 1) * LANES
                ]

    @pl.when(last)
    def _():
        for part in range(parts):
            for piece in range(lanes):
                values = staged[part * lanes + piece].reshape(rows, slots, LANES)
                block[part, :, :, piece * LANES : (piece + 1) * LANES] = values.astype(BF16)


def write_owned(source, meta, keep, send, across):
    height = keep.shape[1]
    for index in range(4):
        start = pl.multiple_of((meta[0] ^ index) * height, 16)
        target = send if index & across else keep
        target[index >> 1 if across == 1 else index & 1] = source[
            pl.ds(start, height), :
        ].astype(BF16)


ANY = pl.BlockSpec(memory_space=pl.ANY)


def whole(*shape):
    return pl.BlockSpec(shape, lambda *_: (0,) * len(shape))


def like(shape, dtype):
    return jax.ShapeDtypeStruct(shape, dtype)


def call(kernel, name, steps, scalars, ins, outs, scratch, cost, aliases=None):
    flops, moved, transcendentals = cost
    return pl.pallas_call(
        kernel,
        out_shape=tuple(item for item, _ in outs),
        grid_spec=pltpu.PrefetchScalarGridSpec(
            num_scalar_prefetch=len(scalars),
            grid=(steps,),
            in_specs=[spec for _, spec in ins],
            out_specs=tuple(spec for _, spec in outs),
            scratch_shapes=scratch,
        ),
        input_output_aliases={len(scalars) + k: v for k, v in (aliases or {}).items()},
        compiler_params=pltpu.CompilerParams(vmem_limit_bytes=VMEM_LIMIT),
        cost_estimate=pl.CostEstimate(
            flops=int(flops), bytes_accessed=int(moved), transcendentals=int(transcendentals)
        ),
        name=name,
    )(*scalars, *[item for item, _ in ins])


def group(count):
    return 2 if count % 2 == 0 else 1


def prepare_kernel(chunks, *refs):
    items, (expand, shrink), (vectors, packed) = refs[:8], refs[8:10], refs[10:]
    width = vectors.shape[1]
    row = 0
    for item in items:
        for start in range(0, item.shape[0], width):
            vectors[row : row + 1, :] = item[pl.ds(start, width)].reshape(1, width)
            row += 1
    quarter = expand.shape[0] // 4
    blocks = expand.shape[1] // width
    tall = shrink.shape[0] // (4 * chunks)
    for index in range(4):
        rows = slice(index * quarter, (index + 1) * quarter)
        for block in range(blocks):
            start = block * quarter
            packed[index, start : start + quarter, :] = expand[
                rows, block * width : (block + 1) * width
            ]
        for number in range(chunks):
            start = blocks * quarter + number * tall
            source = (4 * number + index) * tall
            packed[index, start : start + tall, :] = shrink[source : source + tall, :]


def prepare(chunks, items, weights):
    width = weights[1].shape[1]
    count = sum(item.shape[0] for item in items) // width
    total = sum(item.shape[0] * item.shape[1] for item in weights) // (4 * width)
    return call(
        functools.partial(prepare_kernel, chunks),
        "prepare",
        1,
        (),
        [(item, whole(*item.shape)) for item in (*items, *weights)],
        [
            (like((count, width), F32), whole(count, width)),
            (like((4, total, width), BF16), whole(4, total, width)),
        ],
        [],
        (0, 8 * total * width, 0),
    )


def collect_kernel(*refs):
    out = refs[-1]
    width = out.shape[1]
    singles, triples, expands, tables = refs[:6], refs[6:9], refs[9:12], refs[12:-1]
    out[...] = jnp.zeros_like(out)
    for row, item in enumerate(singles):
        out[row : row + 1, :] = item[...]
    size = width // 3
    for number, item in enumerate(triples):
        for part in range(3):
            row = TRIPLE_BIAS + part
            out[row : row + 1, number * size : (number + 1) * size] = item[
                :, part * size : (part + 1) * size
            ]
    for number, item in enumerate(expands):
        for part in range(item.shape[1] // size):
            row = EXPAND_BIAS + part
            out[row : row + 1, number * size : (number + 1) * size] = item[
                :, part * size : (part + 1) * size
            ]
    total = tables[0][...]
    for item in tables[1:]:
        total = total + item[...]
    for piece in range(3):
        out[TABLES : TABLES + 9, piece * LANES : (piece + 1) * LANES] = total[
            9 * piece : 9 * piece + 9, :
        ]


def collect(singles, triples, expands, tables):
    width = singles[0].shape[1]
    items = (*singles, *triples, *expands, *tables)
    return call(
        collect_kernel,
        "collect",
        1,
        (),
        [(item, whole(*item.shape)) for item in items],
        [(like((24, width), F32), whole(24, width))],
        [],
        (0, 16 * 24 * width, 0),
    )[0]


def attend_kernel(
    slabs, before, meta, windows, tokens, vectors, height, width_table, places, blocks, selectors,
    *rest,
):
    (
        rows_out, normed_out, triple_out, probs_out, attended_out,
        full, staged, weight, tables, masked_keys, sems,
    ) = rest[-11:]
    pieces = rest[:4]
    step = pl.program_id(0)
    base_slab = (step + before) * slabs
    width = full.shape[2]

    @pl.when(step == 0)
    def _():
        copies = load_rows(meta, pieces, weight, sems)
        tables[...] = build_tables(height, width_table, places, blocks)
        wait_all(copies)

    gather_quarters(step == 0, tokens, staged, full, base_slab, slabs)
    rows = full[...].reshape(slabs * ROWS, width)
    unit, _ = normalize(rows)
    normed = unit * vectors[FIRST_GAIN : FIRST_GAIN + 1] + vectors[FIRST_SHIFT : FIRST_SHIFT + 1]
    normed = normed.astype(BF16)
    rows_out[...] = rows.astype(BF16).reshape(slabs, ROWS, width)
    normed_out[...] = normed.reshape(slabs, ROWS, width)
    for part in range(3):
        columns = slice(part * width, (part + 1) * width)
        bias = vectors[TRIPLE_BIAS + part : TRIPLE_BIAS + part + 1]
        triple = dot(normed, weight[:, columns]) + bias
        triple_out[:, :, columns] = triple.astype(BF16).reshape(slabs, ROWS, width)

    lane = lax.broadcasted_iota(jnp.int32, (ROWS, LANES), 1)
    within = lane & (SEG - 1)
    upper = lane >= HD
    quads = HEADS // QUAD
    for slab in range(slabs):
        allowed = valid_rows(windows[meta[0], base_slab + slab])
        penalty = jnp.where((lane == WIN) & jnp.logical_not(allowed), PENALTY, 0.0).astype(BF16)
        for head in range(QUAD):
            masked_keys[slab, head] = selectors[head] + penalty

    sides = (jnp.logical_not(upper), upper)
    zero = jnp.zeros((ROWS, LANES), BF16)
    halves_of = lambda values, head: jnp.where(
        sides[head & 1], values[:, (head >> 1) * LANES : ((head >> 1) + 1) * LANES], zero
    )
    every = [(slab, head) for slab in range(slabs) for head in range(QUAD)]
    constant = jnp.where(lane == WIN, 1.0, 0.0)

    def one_quad(quad, carry):
        base = pl.multiple_of(quad * QUAD * HD, LANES)
        near = pl.multiple_of(base + width, LANES)
        far = pl.multiple_of(base + 2 * width, LANES)
        queries = [triple_out[slab, :, pl.ds(base, QUAD * HD)] for slab in range(slabs)]
        keys = [triple_out[slab, :, pl.ds(near, QUAD * HD)] for slab in range(slabs)]
        values = [triple_out[slab, :, pl.ds(far, QUAD * HD)] for slab in range(slabs)]
        terms = [dot(item, tables[...]) for item in queries]
        lefts = []
        for slab in range(slabs):
            high = roll_rows(terms[slab][:, :LANES], False)
            wide = roll_rows(terms[slab][:, LANES:], True)
            relative = jnp.where(
                within < WIN, high, jnp.where((within >= 16) & (within < 16 + WIN), wide, constant)
            ).astype(BF16)
            scaled = queries[slab] * jnp.asarray(HD**-0.5, BF16)
            lefts.append(
                [
                    jnp.concatenate([scaled[:, pair * LANES : (pair + 1) * LANES], relative], axis=1)
                    for pair in range(QUAD // 2)
                ]
            )
        scores = [
            dot_t(
                lefts[slab][head >> 1],
                jnp.concatenate([halves_of(keys[slab], head), masked_keys[slab, head]], axis=1),
            )
            for slab, head in every
        ]
        probs = []
        for (slab, head), score in zip(every, scores):
            maxima = jnp.max(score, axis=-1, keepdims=True)
            exponent = jnp.exp(score - maxima)
            summed = jnp.sum(exponent, axis=-1, keepdims=True)
            probs.append((exponent * (1.0 / summed)).astype(BF16))
            probs_out[slab, quad * QUAD + head] = probs[-1]
        parts = [dot(prob, halves_of(values[slab], head)) for (slab, head), prob in zip(every, probs)]
        for slab in range(slabs):
            mine = parts[slab * QUAD : (slab + 1) * QUAD]
            mixed = jnp.concatenate(
                [mine[2 * pair] + mine[2 * pair + 1] for pair in range(QUAD // 2)], axis=1
            )
            allowed = valid_rows(windows[meta[0], base_slab + slab])
            mixed = jnp.where(allowed, mixed, 0.0)
            attended_out[slab, :, pl.ds(base, QUAD * HD)] = mixed.astype(BF16)
        return carry

    lax.fori_loop(0, quads, one_quad, 0, unroll=True)


def attend(before, steps, meta, windows, tokens, vectors, tables, selectors, pieces, kept):
    parts, rows_dev, slots, width = tokens.shape
    slabs = group(slots)
    block3 = lambda columns: pl.BlockSpec((slabs, ROWS, columns), lambda i, *_: (i + before, 0, 0))
    rows = steps * slabs * ROWS
    ins = [(item, whole(*item.shape)) for item in (tokens, vectors, *tables, selectors)]
    ins += [(item, ANY) for item in pieces]
    aliases = {}
    if kept is not None:
        aliases = {len(ins) + n: n for n in range(len(kept))}
        ins += [(item, ANY) for item in kept]
    return call(
        functools.partial(attend_kernel, slabs, before),
        "attend",
        steps,
        (meta, windows),
        ins,
        [
            (like((slots, ROWS, width), BF16), block3(width)),
            (like((slots, ROWS, width), BF16), block3(width)),
            (like((slots, ROWS, 3 * width), BF16), block3(3 * width)),
            (
                like((slots, HEADS, ROWS, ROWS), BF16),
                pl.BlockSpec((slabs, HEADS, ROWS, ROWS), lambda i, *_: (i + before, 0, 0, 0)),
            ),
            (like((slots, ROWS, width), BF16), block3(width)),
        ],
        [
            pltpu.VMEM((slabs, ROWS, width), F32),
            pltpu.VMEM((parts * width // LANES, rows_dev * slots, LANES), F32),
            pltpu.VMEM((width, 3 * width), BF16),
            pltpu.VMEM((2 * LANES, 2 * LANES), BF16),
            pltpu.VMEM((slabs, QUAD, ROWS, LANES), BF16),
            pltpu.SemaphoreType.DMA((10,)),
        ],
        (
            6 * rows * width * width + steps * slabs * HEADS * 4 * ROWS * ROWS * 256,
            rows * (width * 16 + HEADS * 512) + width * width * 6,
            steps * slabs * HEADS * ROWS * ROWS,
        ),
        aliases,
    )


def project_kernel(
    slabs, first, meta, windows, attended, rows_in, grads, vectors, *rest,
):
    pieces = rest[:4]
    middle_out, normed_out, branch_out, shrink_bias_out, full, staged, weight, sems = rest[4:]
    step = pl.program_id(0)

    @pl.when(step == 0)
    def _():
        wait_all(load_rows(meta, pieces, weight, sems, first))
        shrink_bias_out[...] = jnp.zeros_like(shrink_bias_out)

    width = full.shape[2]
    count = slabs * ROWS
    middle = (
        rows_in[...].reshape(count, width).astype(F32)
        + dot(attended[...].reshape(count, width), weight[...])
        + vectors[OUTPUT_BIAS : OUTPUT_BIAS + 1]
    )
    unit, _ = normalize(middle)
    middle_out[...] = middle
    normed = unit * vectors[SECOND_GAIN : SECOND_GAIN + 1] + vectors[SECOND_SHIFT : SECOND_SHIFT + 1]
    normed_out[...] = normed.astype(BF16)
    gather_quarters(step == 0, grads, staged, full, step * slabs, slabs)
    for slab in range(slabs):
        allowed = valid_rows(windows[meta[0], step * slabs + slab])
        branch = jnp.where(allowed, full[slab], 0.0)
        branch_out[slab * ROWS : (slab + 1) * ROWS, :] = branch.astype(BF16)
        shrink_bias_out[...] += jnp.sum(branch, axis=0, keepdims=True)


def project(meta, windows, attended, rows_in, grads, vectors, pieces):
    parts, rows_dev, slots, width = grads.shape
    slabs = group(slots)
    block = pl.BlockSpec((slabs, ROWS, width), lambda i, *_: (i, 0, 0))
    flat = pl.BlockSpec((slabs * ROWS, width), lambda i, *_: (i, 0))
    rows = slots * ROWS
    return call(
        functools.partial(project_kernel, slabs, 3 * width),
        "project",
        slots // slabs,
        (meta, windows),
        [(attended, block), (rows_in, block)]
        + [(item, whole(*item.shape)) for item in (grads, vectors)]
        + [(item, ANY) for item in pieces],
        [
            (like((rows, width), F32), flat),
            (like((rows, width), BF16), flat),
            (like((rows, width), BF16), flat),
            (like((1, width), F32), whole(1, width)),
        ],
        [
            pltpu.VMEM((slabs, ROWS, width), F32),
            pltpu.VMEM((parts * width // LANES, rows_dev * slots, LANES), F32),
            pltpu.VMEM((width, width), BF16),
            pltpu.SemaphoreType.DMA((10,)),
        ],
        (2 * rows * width * width, rows * width * 14, 0),
    )


def gate_both(hidden):
    half = 0.5 * (1.0 + lax.erf(hidden * 0.7071067811865476))
    density = jnp.exp(hidden * hidden * -0.5) * 0.3989422804014327
    return hidden * half, half + hidden * density


def feed_kernel(number, first, unit, meta, normed, branch, vectors, *rest):
    pieces, rest = rest[:10], rest[10:]
    if not first:
        out_in, grad_in = rest[:2]
    out_acc, grad_acc, keep, send, bias_grad, expand, shrink, acc_e, acc_s, sems = rest[-10:]
    step = pl.program_id(0)
    last = pl.num_programs(0) - 1
    width, chunk = acc_e.shape
    blocks = chunk // unit

    @pl.when(step == 0)
    def _():
        pairs = []
        quarter, tall = expand.shape[1], shrink.shape[1]
        here = blocks * quarter + number * tall
        columns = pl.ds(number * unit, unit)
        for source, who in zip(pieces[:2], (0, 1)):
            places = pl.ds(4 * (meta[0] ^ who), 4)
            for block in range(blocks):
                pairs.append(
                    (
                        source.at[:, pl.ds(block * quarter, quarter), columns],
                        expand.at[places, :, pl.ds(block * unit, unit)],
                    )
                )
            pairs.append((source.at[:, pl.ds(here, tall), :], shrink.at[places]))
        for fetched, places in zip((pieces[2:6], pieces[6:10]), quarter_places(meta)):
            for source, place in zip(fetched, places):
                for block in range(blocks):
                    pairs.append(
                        (
                            source.at[pl.ds(block * quarter, quarter), columns],
                            expand.at[place, :, pl.ds(block * unit, unit)],
                        )
                    )
                pairs.append((source.at[pl.ds(here, tall), :], shrink.at[place]))
        copies = start_copies(pairs, sems)
        acc_e[...] = jnp.zeros_like(acc_e)
        acc_s[...] = jnp.zeros_like(acc_s)
        bias_grad[...] = jnp.zeros_like(bias_grad)
        wait_all(copies)

    rows = normed[...]
    grads = branch[...]
    bias = jnp.concatenate(
        [
            vectors[
                EXPAND_BIAS + block : EXPAND_BIAS + block + 1, number * unit : (number + 1) * unit
            ]
            for block in range(blocks)
        ],
        axis=1,
    )
    whole_expand = expand[...].reshape(width, chunk)
    whole_shrink = shrink[...].reshape(chunk, width)
    hidden = dot(rows, whole_expand) + bias
    d_active = dot_t(grads, whole_shrink)
    active, slope = gate_both(hidden)
    active = active.astype(BF16)
    back = (d_active * slope).astype(BF16)
    bias_grad[...] += jnp.sum(back.astype(F32), axis=0, keepdims=True)
    acc_s[...] += dot_rows(active, grads)
    acc_e[...] += dot_rows(rows, back)
    total_out = dot(active, whole_shrink)
    total_grad = dot_t(back, whole_expand)
    if first:
        out_acc[...] = total_out.astype(BF16)
        grad_acc[...] = total_grad.astype(BF16)
    else:
        out_acc[...] = (out_in[...].astype(F32) + total_out).astype(BF16)
        grad_acc[...] = (grad_in[...].astype(F32) + total_grad).astype(BF16)

    @pl.when(step == last)
    def _():
        height = width // 4
        third = height // 3
        for index in range(4):
            target = (send if index & 1 else keep).at[index >> 1]
            start = pl.multiple_of((meta[0] ^ index) * unit, 16)
            target[:unit, :] = acc_s[pl.ds(start, unit), :].astype(BF16)
            start = pl.multiple_of((meta[0] ^ index) * height, 16)
            target[unit : unit + height, :] = acc_e[pl.ds(start, height), :width].astype(BF16)
            for piece in range(3):
                here = pl.multiple_of(start + piece * third, 16)
                target[unit + height :, piece * unit : (piece + 1) * unit] = acc_e[
                    pl.ds(here, third), width:
                ].astype(BF16)


def feed(number, count, meta, normed, branch, vectors, pieces, kept):
    rows, width = normed.shape
    chunk = 4 * width // count
    unit = chunk // 4
    block_rows = 2 * ROWS
    block = pl.BlockSpec((block_rows, width), lambda i, *_: (i, 0))
    ins = [(normed, block), (branch, block), (vectors, whole(*vectors.shape))]
    ins += [(item, ANY) for item in pieces]
    aliases = {}
    if kept is not None:
        aliases = {len(ins) + n: n for n in range(2)}
        ins += [(item, block) for item in kept]
    payload = (2, unit + unit, width)
    return call(
        functools.partial(feed_kernel, number, kept is None, unit),
        "feed",
        rows // block_rows,
        (meta,),
        ins,
        [
            (like((rows, width), BF16), block),
            (like((rows, width), BF16), block),
            (like(payload, BF16), whole(*payload)),
            (like(payload, BF16), whole(*payload)),
            (like((1, chunk), F32), whole(1, chunk)),
        ],
        [
            pltpu.VMEM((16, width // 16, chunk), BF16),
            pltpu.VMEM((16, chunk // 16, width), BF16),
            pltpu.VMEM((width, chunk), F32),
            pltpu.VMEM((chunk, width), F32),
            pltpu.SemaphoreType.DMA((64,)),
        ],
        (12 * rows * width * chunk, rows * width * 12 + width * chunk * 8, 2 * rows * chunk),
        aliases,
    )


def middle_kernel(
    slabs, first, meta, windows, middle, out_acc, grad_acc, branch, attended, vectors,
    *rest,
):
    pieces = rest[:4]
    (
        result_out, d_middle_out, d_attended_out, keep, send, output_bias_grad, gain_grad,
        shift_grad, full, staged, weight, acc, sems,
    ) = rest[4:]
    step = pl.program_id(0)
    last = pl.num_programs(0) - 1

    @pl.when(step == 0)
    def _():
        copies = load_rows(meta, pieces, weight, sems, first)
        acc[...] = jnp.zeros_like(acc)
        output_bias_grad[...] = jnp.zeros_like(output_bias_grad)
        gain_grad[...] = jnp.zeros_like(gain_grad)
        shift_grad[...] = jnp.zeros_like(shift_grad)
        wait_all(copies)

    width = full.shape[2]
    count = slabs * ROWS
    rows = middle[...]
    result = rows + out_acc[...].astype(F32) + vectors[SHRINK_BIAS : SHRINK_BIAS + 1]
    full[...] = result.reshape(slabs, ROWS, width)
    scatter_quarters(step == last, full, staged, result_out, step * slabs, slabs)
    unit, scale = normalize(rows)
    grad = grad_acc[...].astype(F32)
    gain_grad[...] += jnp.sum(grad * unit, axis=0, keepdims=True)
    shift_grad[...] += jnp.sum(grad, axis=0, keepdims=True)
    d_middle = branch[...].astype(F32) + normalize_back(
        unit, scale, grad, vectors[SECOND_GAIN : SECOND_GAIN + 1]
    )
    d_output = d_middle.astype(BF16)
    d_middle_out[...] = d_output
    output_bias_grad[...] += jnp.sum(d_output.astype(F32), axis=0, keepdims=True)
    acc[...] += dot_rows(attended[...].reshape(count, width), d_output)
    d_attended = dot_t(d_output, weight[...]).reshape(slabs, ROWS, width)
    for slab in range(slabs):
        allowed = valid_rows(windows[meta[0], step * slabs + slab])
        d_attended_out[slab] = jnp.where(allowed, d_attended[slab], 0.0).astype(BF16)

    @pl.when(step == last)
    def _():
        write_owned(acc, meta, keep, send, 1)


def middle_back(meta, windows, rows_dev, middle, out_acc, grad_acc, branch, attended, vectors, pieces):
    slots, _, width = attended.shape
    parts = WROWS // rows_dev
    slabs = group(slots)
    block = pl.BlockSpec((slabs, ROWS, width), lambda i, *_: (i, 0, 0))
    flat = pl.BlockSpec((slabs * ROWS, width), lambda i, *_: (i, 0))
    rows = slots * ROWS
    vec = (like((1, width), F32), whole(1, width))
    payload = (2, width // 4, width)
    quarter = (parts, rows_dev, slots, width)
    return call(
        functools.partial(middle_kernel, slabs, 3 * width),
        "middle",
        slots // slabs,
        (meta, windows),
        [
            (middle, flat), (out_acc, flat), (grad_acc, flat), (branch, flat), (attended, block),
            (vectors, whole(*vectors.shape)),
        ]
        + [(item, ANY) for item in pieces],
        [
            (like(quarter, BF16), whole(*quarter)),
            (like((rows, width), BF16), flat),
            (like((slots, ROWS, width), BF16), block),
            (like(payload, BF16), whole(*payload)),
            (like(payload, BF16), whole(*payload)),
            vec,
            vec,
            vec,
        ],
        [
            pltpu.VMEM((slabs, ROWS, width), F32),
            pltpu.VMEM((parts * width // LANES, rows_dev * slots, LANES), F32),
            pltpu.VMEM((width, width), BF16),
            pltpu.VMEM((width, width), F32),
            pltpu.SemaphoreType.DMA((10,)),
        ],
        (4 * rows * width * width, rows * width * 18, 0),
    )


def attend_back_kernel(
    slabs, across, meta, normed, queries_in, keys_in, values_in, probs_in, d_mixed_in, mixed_in,
    height, width_table, places, blocks, selectors, sums,
    d_queries, d_keys, d_values, keep, send, bias_grad, table_out, grads, acc, tables, table_grad,
):
    step = pl.program_id(0)
    last = pl.num_programs(0) - 1
    wide4 = QUAD * HD

    @pl.when(step == 0)
    def _():
        acc[...] = jnp.zeros_like(acc)
        bias_grad[...] = jnp.zeros_like(bias_grad)
        table_grad[...] = jnp.zeros_like(table_grad)
        tables[...] = build_tables(height, width_table, places, blocks)

    lane = lax.broadcasted_iota(jnp.int32, (ROWS, LANES), 1)
    within = lane & (SEG - 1)
    upper = lane >= HD
    zero = jnp.zeros((ROWS, LANES), BF16)

    sides = (jnp.logical_not(upper), upper)
    halves_of = lambda items, head: jnp.where(
        sides[head & 1], items[:, (head >> 1) * LANES : ((head >> 1) + 1) * LANES], zero
    )
    minus = [
        jnp.where((lane == 2 * head) | (lane == 2 * head + 1), -1.0, 0.0).astype(BF16)
        for head in range(QUAD)
    ]
    every = [(slab, head) for slab in range(slabs) for head in range(QUAD)]
    lefts = []
    for slab in range(slabs):
        d_mixed = d_mixed_in[slab]
        product = d_mixed.astype(F32) * mixed_in[slab].astype(F32)
        product_high = product.astype(BF16)
        product_low = (product - product_high.astype(F32)).astype(BF16)
        inner = dot(product_high, sums[...]) + dot(product_low, sums[...])
        inner_high = inner.astype(BF16)
        inner_low = (inner - inner_high.astype(F32)).astype(BF16)
        inner = jnp.where((lane & 1) == 0, inner_high, inner_low)
        lefts.append(
            [
                jnp.concatenate([d_mixed[:, pair * LANES : (pair + 1) * LANES], inner], axis=1)
                for pair in range(QUAD // 2)
            ]
        )
    d_probs = [
        dot_t(
            lefts[slab][head >> 1],
            jnp.concatenate([halves_of(values_in[slab], head), minus[head]], axis=1),
        )
        for slab, head in every
    ]
    parts_v = [
        dot_rows(probs_in[slab, head], halves_of(d_mixed_in[slab], head)) for slab, head in every
    ]
    d_scores = [
        (probs_in[slab, head].astype(F32) * item).astype(BF16)
        for (slab, head), item in zip(every, d_probs)
    ]
    backs = [
        dot(
            item,
            jnp.concatenate([halves_of(keys_in[slab], head), selectors[head]], axis=1),
        )
        for (slab, head), item in zip(every, d_scores)
    ]
    parts_k = [
        dot_rows(item, halves_of(queries_in[slab], head))
        for (slab, head), item in zip(every, d_scores)
    ]
    scale = HD**-0.5
    joined = lambda items: jnp.concatenate(
        [items[2 * pair] + items[2 * pair + 1] for pair in range(QUAD // 2)], axis=1
    )
    for slab in range(slabs):
        mine = slice(slab * QUAD, (slab + 1) * QUAD)
        d_relative = backs[slab * QUAD][:, LANES:]
        for head in range(1, QUAD):
            d_relative = d_relative + backs[slab * QUAD + head][:, LANES:]
        high = roll_rows(jnp.where(within < WIN, d_relative, 0.0), False)
        wide = roll_rows(jnp.where((within >= 16) & (within < 16 + WIN), d_relative, 0.0), True)
        d_terms = jnp.concatenate([high, wide], axis=1).astype(BF16)
        dq = joined([item[:, :LANES] for item in backs[mine]]) * scale
        dq = (dq + dot_t(d_terms, tables[...])).astype(BF16)
        table_grad[...] += dot_rows(queries_in[slab], d_terms)
        dk = (joined(parts_k[mine]) * scale).astype(BF16)
        dv = joined(parts_v[mine]).astype(BF16)
        d_queries[slab] = dq
        d_keys[slab] = dk
        d_values[slab] = dv
        grads[slab] = jnp.concatenate([dq, dk, dv], axis=1)

    width = normed.shape[2]
    both = grads[...].reshape(slabs * ROWS, 3 * wide4)
    bias_grad[...] += jnp.sum(both.astype(F32), axis=0, keepdims=True)
    acc[...] += dot_rows(normed[...].reshape(slabs * ROWS, width), both)

    @pl.when(step == last)
    def _():
        write_owned(acc, meta, keep, send, across)
        masked = table_grad[...] * blocks[...].astype(F32)
        folded = masked[:HD]
        for head in range(1, QUAD):
            folded = folded + masked[head * HD : (head + 1) * HD]
        high = folded.astype(BF16)
        low = (folded - high.astype(F32)).astype(BF16)
        for which in range(2):
            table_out[:, which * HD : (which + 1) * HD] = dot_t(places[which], high) + dot_t(
                places[which], low
            )


def attend_back(quad, across, meta, normed, triple, probs, d_mixed, mixed, tables, selectors, sums):
    slots, _, width = normed.shape
    slabs = group(slots)
    wide4 = QUAD * HD
    quads = HEADS // QUAD
    column = lambda where: pl.BlockSpec((slabs, ROWS, wide4), lambda i, *_: (i, 0, where))
    narrow = (
        like((slots, ROWS, wide4), BF16),
        pl.BlockSpec((slabs, ROWS, wide4), lambda i, *_: (i, 0, 0)),
    )
    rows = slots * ROWS
    payload = (2, width // 4, 3 * wide4)
    return call(
        functools.partial(attend_back_kernel, slabs, across),
        "attend_back",
        slots // slabs,
        (meta,),
        [
            (normed, pl.BlockSpec((slabs, ROWS, width), lambda i, *_: (i, 0, 0))),
            (triple, column(quad)),
            (triple, column(quads + quad)),
            (triple, column(2 * quads + quad)),
            (probs, pl.BlockSpec((slabs, QUAD, ROWS, ROWS), lambda i, *_: (i, quad, 0, 0))),
            (d_mixed, column(quad)),
            (mixed, column(quad)),
        ]
        + [(item, whole(*item.shape)) for item in (*tables, selectors, sums)],
        [
            narrow,
            narrow,
            narrow,
            (like(payload, BF16), whole(*payload)),
            (like(payload, BF16), whole(*payload)),
            (like((1, 3 * wide4), F32), whole(1, 3 * wide4)),
            (like((REL, 2 * HD), F32), whole(REL, 2 * HD)),
        ],
        [
            pltpu.VMEM((slabs, ROWS, 3 * wide4), BF16),
            pltpu.VMEM((width, 3 * wide4), F32),
            pltpu.VMEM((2 * LANES, 2 * LANES), BF16),
            pltpu.VMEM((2 * LANES, 2 * LANES), F32),
        ],
        (
            2 * rows * width * 3 * wide4 + slots * QUAD * 8 * ROWS * ROWS * 256,
            rows * (width * 2 + wide4 * 16 + QUAD * 512),
            0,
        ),
    )


def first_kernel(slabs, meta, rows_in, d_middle, vectors, *rest):
    grads, pieces = rest[:9], rest[9:13]
    tokens_out, gain_grad, shift_grad, full, staged, weight, sems = rest[13:]
    step = pl.program_id(0)
    last = pl.num_programs(0) - 1

    @pl.when(step == 0)
    def _():
        copies = load_rows(meta, pieces, weight, sems)
        gain_grad[...] = jnp.zeros_like(gain_grad)
        shift_grad[...] = jnp.zeros_like(shift_grad)
        wait_all(copies)

    width = full.shape[2]
    count = slabs * ROWS
    wide4 = QUAD * HD
    both = jnp.concatenate([grad[...].reshape(count, wide4) for grad in grads], axis=1)
    total = dot_t(both, weight[...])
    unit, scale = normalize(rows_in[...].reshape(count, width).astype(F32))
    gain_grad[...] += jnp.sum(total * unit, axis=0, keepdims=True)
    shift_grad[...] += jnp.sum(total, axis=0, keepdims=True)
    back = normalize_back(unit, scale, total, vectors[FIRST_GAIN : FIRST_GAIN + 1])
    full[...] = (d_middle[...].astype(F32) + back).reshape(slabs, ROWS, width)
    scatter_quarters(step == last, full, staged, tokens_out, step * slabs, slabs)


def first_back(before, steps, meta, rows_dev, rows_in, d_middle, vectors, grads, pieces):
    slots, _, width = rows_in.shape
    parts = WROWS // rows_dev
    slabs = group(slots)
    wide4 = QUAD * HD
    block = pl.BlockSpec((slabs, ROWS, width), lambda i, *_: (i + before, 0, 0))
    flat = pl.BlockSpec((slabs * ROWS, width), lambda i, *_: (i + before, 0))
    narrow = pl.BlockSpec((slabs, ROWS, wide4), lambda i, *_: (i + before, 0, 0))
    rows = steps * slabs * ROWS
    quarter = (parts, rows_dev, steps * slabs, width)
    return call(
        functools.partial(first_kernel, slabs),
        "first_back",
        steps,
        (meta,),
        [(rows_in, block), (d_middle, flat), (vectors, whole(*vectors.shape))]
        + [(item, narrow) for item in grads]
        + [(item, ANY) for item in pieces],
        [(like(quarter, BF16), whole(*quarter))] + [(like((1, width), F32), whole(1, width))] * 2,
        [
            pltpu.VMEM((slabs, ROWS, width), F32),
            pltpu.VMEM((parts * width // LANES, rows_dev * steps * slabs, LANES), F32),
            pltpu.VMEM((width, 3 * width), BF16),
            pltpu.SemaphoreType.DMA((10,)),
        ],
        (6 * rows * width * width, rows * width * 14, 0),
    )


def join_halves(meta, items, staged):
    upper = meta[1] > 0
    for number, both in enumerate(staged):
        mine, other = items[2 * number], items[2 * number + 1]
        half = mine.shape[0]

        @pl.when(upper)
        def _():
            both[:half] = other[...]
            both[half:] = mine[...]

        @pl.when(jnp.logical_not(upper))
        def _():
            both[:half] = mine[...]
            both[half:] = other[...]


def finish_feed_kernel(unit, pairs, meta, *refs):
    items, (expand_out, shrink_out, output_out), staged = (
        refs[: 2 * pairs], refs[2 * pairs : 2 * pairs + 3], refs[2 * pairs + 3 :]
    )
    join_halves(meta, items, staged)
    output_out[...] = staged[-1][2 * unit :, :].astype(F32)
    shard, width = expand_out.shape[0], shrink_out.shape[1]
    third = shard // 3
    parts = width // shard
    for number, both in enumerate(staged):
        here = number * unit
        shrink_out[here : here + unit, :] = both[:unit, :].astype(F32)
        for block in range(parts - 1):
            start = block * width + here
            expand_out[:, start : start + unit] = both[
                unit : unit + shard, block * unit : (block + 1) * unit
            ].astype(F32)
        start = (parts - 1) * width + here
        for piece in range(3):
            expand_out[piece * third : (piece + 1) * third, start : start + unit] = both[
                unit + shard : 2 * unit, piece * unit : (piece + 1) * unit
            ].astype(F32)


def finish_rest_kernel(pairs, meta, *refs):
    items, small, refs = refs[: 2 * pairs], refs[2 * pairs], refs[2 * pairs + 1 :]
    triple_out, refs = refs[0], refs[1:]
    vectors, tables, staged = refs[:8], refs[8:10], refs[10:]
    join_halves(meta, items, staged)
    shard, width = triple_out.shape[0], small.shape[1]
    wide4 = QUAD * HD
    quads = [both[n : n + shard, :] for both in staged for n in range(0, both.shape[0], shard)]
    for quad, values in enumerate(quads):
        for part in range(3):
            start = part * width + quad * wide4
            triple_out[:, start : start + wide4] = values[
                :, part * wide4 : (part + 1) * wide4
            ].astype(F32)
    row = 0
    for item in vectors:
        for start in range(0, item.shape[0], width):
            item[pl.ds(start, width)] = small[row : row + 1, :].reshape(width)
            row += 1
    for which, item in enumerate(tables):
        for piece in range(3):
            start = piece * LANES + which * HD
            item[9 * piece : 9 * piece + 9, :] = small[TABLES : TABLES + 9, start : start + HD]


def finish(kernel, name, meta, shares, others, outs):
    items = [item for pair in shares for item in pair]
    return call(
        kernel,
        name,
        1,
        (meta,),
        [(item, whole(*item.shape)) for item in (*items, *others)],
        [(like(item.shape, F32), whole(*item.shape)) for item in outs],
        [pltpu.VMEM((2 * mine.shape[0], mine.shape[1]), BF16) for mine, _ in shares],
        (0, sum(6 * item.size for item in items), 0),
    )


def swap(values, axis, bits):
    count = lax.axis_size(axis)
    return lax.ppermute(values, axis, [(n, n ^ bits) for n in range(count)])


def swap_diagonal(values):
    across = lax.axis_size("seq")
    count = lax.axis_size("dp") * across
    perm = [(n, (n // across ^ 1) * across + (n % across ^ 1)) for n in range(count)]
    return lax.ppermute(values, ("dp", "seq"), perm)


def spread(far):
    return far, swap(far, "dp", 1), swap(far, "seq", 1), swap_diagonal(far)


def exchange_windows(values):
    return lax.all_to_all(values, "tensor", split_axis=0, concat_axis=0, tiled=True)


def after(values, *others):
    return lax.optimization_barrier((values, *others))[0]


def far_quarter(packed):
    which = 2 * (lax.axis_index("dp") & 1) + (lax.axis_index("seq") & 1)
    return lax.dynamic_index_in_dim(packed, which, axis=0, keepdims=False)


def add(*items):
    total = items[0].astype(F32)
    for item in items[1:]:
        total = total + item.astype(F32)
    return total.astype(BF16)


def halves(axis):
    out, bit = [], 1
    while bit < lax.axis_size(axis):
        out.append(bit)
        bit *= 2
    return out


def reduce_stages(payloads, plan, hook=None):
    bits_of = {"c": 1, "y": 2}
    totals = []
    while True:
        keep, send, more = payloads.pop(0)
        (far,) = yield [(send, "tensor", bits_of[plan[0]])]
        totals.append(add(keep, far))
        if not more:
            break
    total = totals[0] if len(totals) == 1 else jnp.concatenate(totals, axis=1)
    spot = lax.axis_index("dp")
    place = lax.axis_index("seq")

    def split(values, upper):
        size = values.shape[-2] // 2
        low, high = values[..., :size, :], values[..., size:, :]
        return jnp.where(upper, high, low), jnp.where(upper, low, high)

    def join(mine, far, upper):
        return jnp.concatenate([jnp.where(upper, far, mine), jnp.where(upper, mine, far)], axis=0)

    for letter in plan[1:]:
        if letter == "w":
            total = hook(total)
        elif letter in bits_of:
            (far,) = yield [(total[1], "tensor", bits_of[letter])]
            total = add(total[0], far)
        elif letter == "x":
            for bit in halves("dp"):
                near, far = split(total, (spot & bit) > 0)
                (far,) = yield [(far, "dp", bit)]
                total = add(near, far)
        else:
            if letter == "s":
                near, far = split(total, (place & 1) > 0)
                (far,) = yield [(far, "seq", 1)]
                total = add(near, far)
            for bit in halves("seq"):
                if letter == "s" and bit == 1:
                    continue
                (far,) = yield [(total, "seq", bit)]
                total = add(total, far)
            if letter == "s":
                (far,) = yield [(total, "seq", 1)]
                total = join(total, far, (place & 1) > 0)
    for bit in reversed(halves("dp")):
        (far,) = yield [(total, "dp", bit)]
        if bit > 1:
            total = join(total, far, (spot & bit) > 0)
    return total, far


def sum_stages(values, hook):
    steps = [(axis, bit) for axis in ("tensor", "dp", "seq") for bit in halves(axis)]
    steps = [("tensor", 2)] + [item for item in steps if item != ("tensor", 2)]
    for number, (axis, bit) in enumerate(steps):
        (far,) = yield [(values, axis, bit)]
        if number == len(steps) - 1:
            far = hook(far)
        values = values + far
    return (values,)


class Exchanges:
    def __init__(self):
        self.running = []
        self.done = {}

    def begin(self, name, stages):
        self.running.append([name, stages, None])

    def step(self, names, token, meta, *extra):
        asked, ended = [], []
        chosen = [entry for entry in self.running if names is None or entry[0] in names]
        arrived = [item for entry in chosen for item in (entry[2] or ())]
        if token is not None and arrived:
            token, *arrived = lax.optimization_barrier((token, *arrived))
        arrived = iter(arrived)
        for entry in chosen:
            name, stages, waiting = entry
            mine = None if waiting is None else [next(arrived) for _ in waiting]
            try:
                asked.append((entry, stages.send(mine)))
            except StopIteration as stop:
                ended.append((name, stop.value))
                self.running.remove(entry)
        values = [item[0] for _, wanted in asked for item in wanted]
        finished = [item for _, pair in ended for item in pair]
        if meta is not None:
            count = len(values)
            meta, *rest = lax.optimization_barrier((meta, *values, *finished, *extra))
            values = rest[:count]
            finished = rest[count : count + len(finished)]
            extra = rest[count + len(finished) :]
        values, finished = iter(values), iter(finished)
        for entry, wanted in asked:
            entry[2] = [swap(next(values), axis, bits) for _, axis, bits in wanted]
        for name, pair in ended:
            self.done[name] = tuple(next(finished) for _ in pair)
        return (token, meta, *extra)

    def finish(self, names):
        while any(entry[0] in names for entry in self.running):
            self.step(names, None, None)


def local(
    tokens,
    out_grad,
    slot_window,
    first_gain,
    first_shift,
    triple_weight,
    triple_bias,
    height_table,
    width_table,
    output_weight,
    output_bias,
    second_gain,
    second_shift,
    expand_weight,
    expand_bias,
    shrink_weight,
    shrink_bias,
):
    micros, images, slots, rows_dev, width = tokens.shape
    parts = lax.axis_size("tensor")
    mine = lax.axis_index("tensor")
    shard = width // parts
    chunks = 3
    unit = width // chunks
    bit = lax.axis_index("dp") & 1
    quarter = 2 * bit + (lax.axis_index("seq") & 1)
    meta = jnp.where(
        jnp.arange(3) == 0, mine, jnp.where(jnp.arange(3) == 1, bit, quarter)
    ).astype(jnp.int32)

    by_image = lambda values: jnp.swapaxes(values, 2, 3).reshape(parts, rows_dev, slots, width)
    to_image = lambda values: jnp.swapaxes(
        values.reshape(micros, images, rows_dev, slots, width), 2, 3
    )
    windows = slot_window.reshape(parts, slots)

    far = jnp.concatenate(
        [
            far_quarter(triple_weight.reshape(4, shard // 4, -1)),
            far_quarter(output_weight.reshape(4, shard // 4, -1)),
        ],
        axis=1,
    )
    far = swap(far, "tensor", 2)
    near_triple = swap(triple_weight, "tensor", 1)
    near_output = swap(output_weight, "tensor", 1)
    vectors, packed_rest = prepare(
        chunks,
        (
            first_gain, first_shift, output_bias, second_gain, second_shift, shrink_bias,
            triple_bias, expand_bias,
        ),
        (expand_weight, shrink_weight),
    )
    sums = np.zeros((QUAD * HD, LANES), np.float32)
    for head in range(QUAD):
        sums[head * HD : (head + 1) * HD, 2 * head : 2 * head + 2] = 1.0
    sums = jnp.asarray(sums, BF16)
    ahead = (height_table, width_table, table_places(False), head_blocks(False))
    behind = (height_table, width_table, table_places(True), head_blocks(True))
    first_rest = far_quarter(packed_rest)
    far, vectors, packed_rest, first_rest, meta, own_tokens, near_triple, near_output = (
        lax.optimization_barrier(
            (
                far, vectors, packed_rest, first_rest, meta, by_image(tokens), near_triple,
                near_output,
            )
        )
    )
    rows_in = exchange_windows(own_tokens)
    fetched = jnp.stack(spread(far))
    crossed = swap(fetched, "tensor", 1)

    packed, first_rest, rows_in, fetched, crossed = lax.optimization_barrier(
        (packed_rest, first_rest, rows_in, fetched, crossed)
    )
    triple_pieces = (triple_weight, near_triple, fetched, crossed)
    output_pieces = (output_weight, near_output, fetched, crossed)
    far = swap(first_rest, "tensor", 2)
    near = swap(packed, "tensor", 1)
    steps = slots // group(slots)
    early = max(1, steps // 4)
    selectors = key_selectors(False)
    kept = attend(
        0, early, meta, windows, rows_in, vectors, ahead, selectors, triple_pieces, None
    )
    kept = list(kept)
    kept[4], far, own_grads = lax.optimization_barrier((kept[4], far, by_image(out_grad)))
    meta, far, near, own_grads = lax.optimization_barrier((meta, far, near, own_grads))
    grads_in = exchange_windows(own_grads)
    fetched = spread(far)
    crossed = (swap(far, "tensor", 1),)
    if early < steps:
        kept = attend(
            early, steps - early, meta, windows, rows_in, vectors, ahead, selectors,
            triple_pieces, kept,
        )
    full_rows, normed, triple, probs, attended = kept
    attended, *others = lax.optimization_barrier((attended, *fetched[1:]))
    meta, *others = lax.optimization_barrier((meta, *others))
    crossed += tuple(swap(item, "tensor", 1) for item in others)
    middle_stage = project(
        meta, windows, attended, full_rows, grads_in, vectors, output_pieces
    )
    shrink_bias_grad = middle_stage[3]
    rest_pieces = (packed, near, far, *others, *crossed)
    middle, normed2, branch = middle_stage[:3]
    exchanges = Exchanges()
    kept = None
    expand_bias_grads = []
    for number in range(chunks):
        *kept, keep, send, bias_grad = feed(
            number, chunks, meta, normed2, branch, vectors, rest_pieces, kept
        )
        plan = ("cyxz", "cyxz", "cxys")[number]
        payloads = [(keep, send, number == chunks - 1)]
        exchanges.begin(("feed", number), reduce_stages(payloads, plan))
        bias_grad, meta = exchanges.step(None, bias_grad, meta)
        expand_bias_grads.append(bias_grad)

    result, d_middle, d_attended, keep, send, output_bias_grad, gain2_grad, shift2_grad = (
        middle_back(
            meta, windows, rows_dev, middle, *kept, branch, attended, vectors, output_pieces
        )
    )
    payloads.append((keep, send, False))
    output_bias_grad, meta = exchanges.step(None, output_bias_grad, meta)
    result = exchange_windows(result)

    quad_grads, triple_bias_grads, table_grads = [], [], []
    for quad in range(HEADS // QUAD):
        dq, dk, dv, keep, send, bias_grad, table_grad = attend_back(
            quad, 1, meta, normed, triple, probs, d_attended, attended, behind, key_selectors(True), sums
        )
        if quad == 0:
            payloads = [(keep, send, True)]
            exchanges.begin(("rest", 0), reduce_stages(payloads, "cyxs"))
        elif quad == 1:
            payloads.append((keep, send, False))
        else:
            hook = lambda total: after(total, *feed_gradients)
            exchanges.begin(("rest", 1), reduce_stages([(keep, send, False)], "cyxz", hook))
        if quad == 1:
            bias_grad, meta, result = exchanges.step(None, bias_grad, meta, result)
        else:
            bias_grad, meta = exchanges.step(None, bias_grad, meta)
        quad_grads.append((dq, dk, dv))
        triple_bias_grads.append(bias_grad)
        table_grads.append(table_grad)
    wide4 = QUAD * HD
    grads9 = [quad_grads[quad][part] for part in range(3) for quad in range(HEADS // QUAD)]
    token_grad, gain1_grad, shift1_grad = first_back(
        0, steps, meta, rows_dev, full_rows, d_middle, vectors, grads9, triple_pieces
    )
    result = to_image(result)
    gain1_grad, _ = exchanges.step(None, gain1_grad, None)
    small = collect(
        (gain1_grad, shift1_grad, output_bias_grad, gain2_grad, shift2_grad, shrink_bias_grad),
        triple_bias_grads,
        expand_bias_grads,
        table_grads,
    )
    hook = lambda far: after(far, *feed_gradients)
    exchanges.begin("small", sum_stages(small, hook))
    exchanges.step(["small"], None, None)
    first_far = exchanges.running[-1][2][0]
    tokens_gradient = to_image(exchange_windows(after(token_grad, first_far)))
    names = [("feed", number) for number in range(chunks)]
    exchanges.finish(names)
    shares = [exchanges.done[name] for name in names]
    feed_gradients = finish(
        functools.partial(finish_feed_kernel, unit, chunks),
        "finish_feed",
        meta,
        shares,
        (),
        (expand_weight, shrink_weight, output_weight),
    )
    expand_gradient, shrink_gradient, output_gradient = feed_gradients
    exchanges.finish([("rest", number) for number in range(2)] + ["small"])
    shares = [exchanges.done["rest", number] for number in range(2)]
    triple_gradient, *outs, high, wide = finish(
        functools.partial(finish_rest_kernel, len(shares)),
        "finish_rest",
        meta,
        shares,
        exchanges.done["small"],
        (
            triple_weight, first_gain, first_shift, output_bias, second_gain, second_shift,
            shrink_bias, triple_bias, expand_bias, height_table, width_table,
        ),
    )
    return (
        result,
        tokens_gradient,
        outs[0],
        outs[1],
        triple_gradient,
        outs[6],
        high,
        wide,
        output_gradient,
        outs[2],
        outs[3],
        outs[4],
        expand_gradient,
        outs[7],
        shrink_gradient,
        outs[5],
    )


def solution(mesh):
    split = P(None, "dp", "seq", "tensor", None)
    rows = P("tensor", None)
    return jax.shard_map(
        local,
        mesh=mesh,
        in_specs=(
            split, split, P(None, "dp", "seq"), P(), P(), rows, P(), P(), P(), rows, P(), P(), P(),
            rows, P(), rows, P(),
        ),
        out_specs=(
            split, split, P(), P(), rows, P(), P(), P(), rows, P(), P(), P(), rows, P(), rows, P(),
        ),
        check_vma=False,
    )
```

```python
import functools

import jax
import jax.numpy as jnp
import numpy as np
from jax import lax
from jax.experimental import pallas as pl
from jax.experimental.pallas import tpu as pltpu
from jax.sharding import PartitionSpec as P

HEADS = 12
HD = 64
WIN = 14
GRID = 64
WGRID = 5
WROWS = WIN * WIN
ROWS = 200
QUAD = 4
LANES = 128
REL = 2 * WIN - 1
SEG = 32
EPSILON = 1e-06
PENALTY = -1e9

F32 = jnp.float32
BF16 = jnp.bfloat16
FIRST_GAIN, FIRST_SHIFT, OUTPUT_BIAS, SECOND_GAIN, SECOND_SHIFT, SHRINK_BIAS = range(6)
TRIPLE_BIAS, EXPAND_BIAS, TABLES = 6, 9, 13
VMEM_LIMIT = 58 * 1024 * 1024


def dot(left, right):
    return lax.dot_general(left, right, (((1,), (0,)), ((), ())), preferred_element_type=F32)


def dot_t(left, right):
    return lax.dot_general(left, right, (((1,), (1,)), ((), ())), preferred_element_type=F32)


def dot_rows(left, right):
    return lax.dot_general(left, right, (((0,), (0,)), ((), ())), preferred_element_type=F32)


def key_selectors(mirrored):
    out = np.zeros((QUAD, ROWS, LANES), np.float32)
    for head in range(QUAD):
        for key in range(WROWS):
            high, wide = key // WIN, key % WIN
            if mirrored:
                high, wide = WIN - 1 - high, WIN - 1 - wide
            out[head, key, SEG * head + high] = 1.0
            out[head, key, SEG * head + 16 + wide] = 1.0
    return jnp.asarray(out, BF16)


def table_places(mirrored):
    out = np.zeros((2, REL, 2 * LANES), np.float32)
    for head in range(QUAD):
        for row in range(REL):
            if mirrored:
                out[0, row, SEG * head + row] = 1.0
                out[1, row, LANES + (SEG * head + 16 + row) % LANES] = 1.0
            else:
                out[0, REL - 1 - row, (SEG * head + row - 13) % LANES] = 1.0
                out[1, REL - 1 - row, LANES + (SEG * head + row + 3) % LANES] = 1.0
    return jnp.asarray(out, BF16)


def head_blocks(mirrored):
    out = np.zeros((QUAD * HD, 2 * LANES), np.float32)
    for head in range(QUAD):
        rows = slice(head * HD, (head + 1) * HD)
        for row in range(REL):
            if mirrored:
                out[rows, SEG * head + row] = 1.0
                out[rows, LANES + (SEG * head + 16 + row) % LANES] = 1.0
            else:
                out[rows, (SEG * head + row - 13) % LANES] = 1.0
                out[rows, LANES + (SEG * head + row + 3) % LANES] = 1.0
    return jnp.asarray(out, BF16)


def valid_rows(window):
    high_place = (window * 13) >> 6
    wide_place = window - high_place * WGRID
    inside = window < WGRID * WGRID
    row = lax.broadcasted_iota(jnp.int32, (ROWS, 1), 0)
    high = (row * 4682) >> 16
    wide = row - high * WIN
    high_limit = jnp.where(inside, GRID - high_place * WIN, 0)
    return (high < high_limit) & (wide < GRID - wide_place * WIN) & (row < WROWS)


def build_tables(height, width, places, blocks):
    both = dot_rows(height[...].astype(BF16), places[0]) + dot_rows(
        width[...].astype(BF16), places[1]
    )
    both = both.astype(BF16)
    return jnp.concatenate([both] * QUAD, axis=0) * blocks[...]


def roll_rows(values, by_width):
    sub = lax.broadcasted_iota(jnp.int32, (8, LANES), 0)
    pieces = []
    for start in range(0, ROWS, 8):
        piece = values[start : start + 8]
        first = start // WIN
        crossing = (first + 1) * WIN - start
        shifts = (first, first + 1)
        if by_width:
            one = pltpu.roll(piece, start - first * WIN, 1, stride=1, stride_axis=0)
        else:
            one = pltpu.roll(piece, first, 1) if first else piece
        if crossing < 8:
            if by_width:
                two = pltpu.roll(piece, LANES - crossing, 1)
                two = pltpu.roll(two, 0, 1, stride=1, stride_axis=0)
            else:
                two = pltpu.roll(piece, shifts[1], 1)
            one = jnp.where(sub < crossing, one, two)
        pieces.append(one)
    return jnp.concatenate(pieces, axis=0)


def normalize(values):
    centre = jnp.mean(values, axis=-1, keepdims=True)
    spread = values - centre
    variance = jnp.mean(spread * spread, axis=-1, keepdims=True)
    scale = lax.rsqrt(variance + EPSILON)
    return spread * scale, scale


def normalize_back(unit, scale, grad, gain):
    scaled = grad * gain
    mean_grad = jnp.mean(scaled, axis=-1, keepdims=True)
    mean_both = jnp.mean(scaled * unit, axis=-1, keepdims=True)
    return (scaled - mean_grad - unit * mean_both) * scale


def quarter_places(meta):
    mine, quarter = meta[0], meta[2]
    return [
        [4 * (mine ^ who) + (quarter ^ flip) for flip in (0, 2, 1, 3)] for who in (2, 3)
    ]


def start_copies(pairs, sems):
    copies = []
    for number, (source, target) in enumerate(pairs):
        copies.append(pltpu.make_async_copy(source, target, sems.at[number]))
    for copy in copies:
        copy.start()
    return copies


def wait_all(copies):
    for copy in copies:
        copy.wait()


def load_rows(meta, pieces, target, sems, first=0):
    own, near, *far = pieces
    columns = target.shape[1]
    quarter = target.shape[0] // 16
    pairs = []
    for source, who in ((own, 0), (near, 1)):
        start = pl.multiple_of(4 * (meta[0] ^ who) * quarter, 16)
        pairs.append((source, target.at[pl.ds(start, 4 * quarter), :]))
    for sources, places in zip(far, quarter_places(meta)):
        for index, place in enumerate(places):
            start = pl.multiple_of(place * quarter, 16)
            pairs.append(
                (sources.at[index, :, pl.ds(first, columns)], target.at[pl.ds(start, quarter), :])
            )
    return start_copies(pairs, sems)


def gather_quarters(first, block, staged, target, base, slabs):
    parts, rows, slots, width = block.shape
    lanes = width // LANES

    @pl.when(first)
    def _():
        for part in range(parts):
            values = block[part].astype(F32).reshape(rows * slots, width)
            for piece in range(lanes):
                staged[part * lanes + piece] = values[:, piece * LANES : (piece + 1) * LANES]
        target[:, parts * rows :, :] = jnp.zeros((slabs, ROWS - parts * rows, width), F32)

    for slab in range(slabs):
        for part in range(parts):
            for piece in range(lanes):
                target[
                    slab, part * rows : (part + 1) * rows, piece * LANES : (piece + 1) * LANES
                ] = staged[part * lanes + piece, pl.ds(base + slab, rows, stride=slots), :]


def scatter_quarters(last, full, staged, block, base, slabs):
    parts, rows, slots, width = block.shape
    lanes = width // LANES
    for slab in range(slabs):
        for part in range(parts):
            for piece in range(lanes):
                staged[part * lanes + piece, pl.ds(base + slab, rows, stride=slots), :] = full[
                    slab, part * rows : (part + 1) * rows, piece * LANES : (piece + 1) * LANES
                ]

    @pl.when(last)
    def _():
        for part in range(parts):
            for piece in range(lanes):
                values = staged[part * lanes + piece].reshape(rows, slots, LANES)
                block[part, :, :, piece * LANES : (piece + 1) * LANES] = values.astype(BF16)


def write_owned(source, meta, keep, send, across):
    height = keep.shape[1]
    for index in range(4):
        start = pl.multiple_of((meta[0] ^ index) * height, 16)
        target = send if index & across else keep
        target[index >> 1 if across == 1 else index & 1] = source[
            pl.ds(start, height), :
        ].astype(BF16)


ANY = pl.BlockSpec(memory_space=pl.ANY)


def whole(*shape):
    return pl.BlockSpec(shape, lambda *_: (0,) * len(shape))


def like(shape, dtype):
    return jax.ShapeDtypeStruct(shape, dtype)


def call(kernel, name, steps, scalars, ins, outs, scratch, cost, aliases=None):
    flops, moved, transcendentals = cost
    return pl.pallas_call(
        kernel,
        out_shape=tuple(item for item, _ in outs),
        grid_spec=pltpu.PrefetchScalarGridSpec(
            num_scalar_prefetch=len(scalars),
            grid=(steps,),
            in_specs=[spec for _, spec in ins],
            out_specs=tuple(spec for _, spec in outs),
            scratch_shapes=scratch,
        ),
        input_output_aliases={len(scalars) + k: v for k, v in (aliases or {}).items()},
        compiler_params=pltpu.CompilerParams(vmem_limit_bytes=VMEM_LIMIT),
        cost_estimate=pl.CostEstimate(
            flops=int(flops), bytes_accessed=int(moved), transcendentals=int(transcendentals)
        ),
        name=name,
    )(*scalars, *[item for item, _ in ins])


def group(count):
    return 2 if count % 2 == 0 else 1


def prepare_kernel(chunks, *refs):
    items, (expand, shrink), (vectors, packed) = refs[:8], refs[8:10], refs[10:]
    width = vectors.shape[1]
    row = 0
    for item in items:
        for start in range(0, item.shape[0], width):
            vectors[row : row + 1, :] = item[pl.ds(start, width)].reshape(1, width)
            row += 1
    quarter = expand.shape[0] // 4
    blocks = expand.shape[1] // width
    tall = shrink.shape[0] // (4 * chunks)
    for index in range(4):
        rows = slice(index * quarter, (index + 1) * quarter)
        for block in range(blocks):
            start = block * quarter
            packed[index, start : start + quarter, :] = expand[
                rows, block * width : (block + 1) * width
            ]
        for number in range(chunks):
            start = blocks * quarter + number * tall
            source = (4 * number + index) * tall
            packed[index, start : start + tall, :] = shrink[source : source + tall, :]


def prepare(chunks, items, weights):
    width = weights[1].shape[1]
    count = sum(item.shape[0] for item in items) // width
    total = sum(item.shape[0] * item.shape[1] for item in weights) // (4 * width)
    return call(
        functools.partial(prepare_kernel, chunks),
        "prepare",
        1,
        (),
        [(item, whole(*item.shape)) for item in (*items, *weights)],
        [
            (like((count, width), F32), whole(count, width)),
            (like((4, total, width), BF16), whole(4, total, width)),
        ],
        [],
        (0, 8 * total * width, 0),
    )


def collect_kernel(*refs):
    out = refs[-1]
    width = out.shape[1]
    singles, triples, expands, tables = refs[:6], refs[6:9], refs[9:12], refs[12:-1]
    out[...] = jnp.zeros_like(out)
    for row, item in enumerate(singles):
        out[row : row + 1, :] = item[...]
    size = width // 3
    for number, item in enumerate(triples):
        for part in range(3):
            row = TRIPLE_BIAS + part
            out[row : row + 1, number * size : (number + 1) * size] = item[
                :, part * size : (part + 1) * size
            ]
    for number, item in enumerate(expands):
        for part in range(item.shape[1] // size):
            row = EXPAND_BIAS + part
            out[row : row + 1, number * size : (number + 1) * size] = item[
                :, part * size : (part + 1) * size
            ]
    total = tables[0][...]
    for item in tables[1:]:
        total = total + item[...]
    for piece in range(3):
        out[TABLES : TABLES + 9, piece * LANES : (piece + 1) * LANES] = total[
            9 * piece : 9 * piece + 9, :
        ]


def collect(singles, triples, expands, tables):
    width = singles[0].shape[1]
    items = (*singles, *triples, *expands, *tables)
    return call(
        collect_kernel,
        "collect",
        1,
        (),
        [(item, whole(*item.shape)) for item in items],
        [(like((24, width), F32), whole(24, width))],
        [],
        (0, 16 * 24 * width, 0),
    )[0]


def attend_kernel(
    slabs, before, meta, windows, tokens, vectors, height, width_table, places, blocks, selectors,
    *rest,
):
    (
        rows_out, normed_out, triple_out, probs_out, attended_out,
        full, staged, weight, tables, masked_keys, sems,
    ) = rest[-11:]
    pieces = rest[:4]
    step = pl.program_id(0)
    base_slab = (step + before) * slabs
    width = full.shape[2]

    @pl.when(step == 0)
    def _():
        copies = load_rows(meta, pieces, weight, sems)
        tables[...] = build_tables(height, width_table, places, blocks)
        wait_all(copies)

    gather_quarters(step == 0, tokens, staged, full, base_slab, slabs)
    rows = full[...].reshape(slabs * ROWS, width)
    unit, _ = normalize(rows)
    normed = unit * vectors[FIRST_GAIN : FIRST_GAIN + 1] + vectors[FIRST_SHIFT : FIRST_SHIFT + 1]
    normed = normed.astype(BF16)
    rows_out[...] = rows.astype(BF16).reshape(slabs, ROWS, width)
    normed_out[...] = normed.reshape(slabs, ROWS, width)
    for part in range(3):
        columns = slice(part * width, (part + 1) * width)
        bias = vectors[TRIPLE_BIAS + part : TRIPLE_BIAS + part + 1]
        triple = dot(normed, weight[:, columns]) + bias
        triple_out[:, :, columns] = triple.astype(BF16).reshape(slabs, ROWS, width)

    lane = lax.broadcasted_iota(jnp.int32, (ROWS, LANES), 1)
    within = lane & (SEG - 1)
    upper = lane >= HD
    quads = HEADS // QUAD
    for slab in range(slabs):
        allowed = valid_rows(windows[meta[0], base_slab + slab])
        penalty = jnp.where((lane == WIN) & jnp.logical_not(allowed), PENALTY, 0.0).astype(BF16)
        for head in range(QUAD):
            masked_keys[slab, head] = selectors[head] + penalty

    sides = (jnp.logical_not(upper), upper)
    zero = jnp.zeros((ROWS, LANES), BF16)
    halves_of = lambda values, head: jnp.where(
        sides[head & 1], values[:, (head >> 1) * LANES : ((head >> 1) + 1) * LANES], zero
    )
    every = [(slab, head) for slab in range(slabs) for head in range(QUAD)]
    constant = jnp.where(lane == WIN, 1.0, 0.0)

    def one_quad(quad, carry):
        base = pl.multiple_of(quad * QUAD * HD, LANES)
        near = pl.multiple_of(base + width, LANES)
        far = pl.multiple_of(base + 2 * width, LANES)
        queries = [triple_out[slab, :, pl.ds(base, QUAD * HD)] for slab in range(slabs)]
        keys = [triple_out[slab, :, pl.ds(near, QUAD * HD)] for slab in range(slabs)]
        values = [triple_out[slab, :, pl.ds(far, QUAD * HD)] for slab in range(slabs)]
        terms = [dot(item, tables[...]) for item in queries]
        lefts = []
        for slab in range(slabs):
            high = roll_rows(terms[slab][:, :LANES], False)
            wide = roll_rows(terms[slab][:, LANES:], True)
            relative = jnp.where(
                within < WIN, high, jnp.where((within >= 16) & (within < 16 + WIN), wide, constant)
            ).astype(BF16)
            scaled = queries[slab] * jnp.asarray(HD**-0.5, BF16)
            lefts.append(
                [
                    jnp.concatenate([scaled[:, pair * LANES : (pair + 1) * LANES], relative], axis=1)
                    for pair in range(QUAD // 2)
                ]
            )
        scores = [
            dot_t(
                lefts[slab][head >> 1],
                jnp.concatenate([halves_of(keys[slab], head), masked_keys[slab, head]], axis=1),
            )
            for slab, head in every
        ]
        probs = []
        for (slab, head), score in zip(every, scores):
            maxima = jnp.max(score, axis=-1, keepdims=True)
            exponent = jnp.exp(score - maxima)
            summed = jnp.sum(exponent, axis=-1, keepdims=True)
            probs.append((exponent * (1.0 / summed)).astype(BF16))
            probs_out[slab, quad * QUAD + head] = probs[-1]
        parts = [dot(prob, halves_of(values[slab], head)) for (slab, head), prob in zip(every, probs)]
        for slab in range(slabs):
            mine = parts[slab * QUAD : (slab + 1) * QUAD]
            mixed = jnp.concatenate(
                [mine[2 * pair] + mine[2 * pair + 1] for pair in range(QUAD // 2)], axis=1
            )
            allowed = valid_rows(windows[meta[0], base_slab + slab])
            mixed = jnp.where(allowed, mixed, 0.0)
            attended_out[slab, :, pl.ds(base, QUAD * HD)] = mixed.astype(BF16)
        return carry

    lax.fori_loop(0, quads, one_quad, 0, unroll=True)


def attend(before, steps, meta, windows, tokens, vectors, tables, selectors, pieces, kept):
    parts, rows_dev, slots, width = tokens.shape
    slabs = group(slots)
    block3 = lambda columns: pl.BlockSpec((slabs, ROWS, columns), lambda i, *_: (i + before, 0, 0))
    rows = steps * slabs * ROWS
    ins = [(item, whole(*item.shape)) for item in (tokens, vectors, *tables, selectors)]
    ins += [(item, ANY) for item in pieces]
    aliases = {}
    if kept is not None:
        aliases = {len(ins) + n: n for n in range(len(kept))}
        ins += [(item, ANY) for item in kept]
    return call(
        functools.partial(attend_kernel, slabs, before),
        "attend",
        steps,
        (meta, windows),
        ins,
        [
            (like((slots, ROWS, width), BF16), block3(width)),
            (like((slots, ROWS, width), BF16), block3(width)),
            (like((slots, ROWS, 3 * width), BF16), block3(3 * width)),
            (
                like((slots, HEADS, ROWS, ROWS), BF16),
                pl.BlockSpec((slabs, HEADS, ROWS, ROWS), lambda i, *_: (i + before, 0, 0, 0)),
            ),
            (like((slots, ROWS, width), BF16), block3(width)),
        ],
        [
            pltpu.VMEM((slabs, ROWS, width), F32),
            pltpu.VMEM((parts * width // LANES, rows_dev * slots, LANES), F32),
            pltpu.VMEM((width, 3 * width), BF16),
            pltpu.VMEM((2 * LANES, 2 * LANES), BF16),
            pltpu.VMEM((slabs, QUAD, ROWS, LANES), BF16),
            pltpu.SemaphoreType.DMA((10,)),
        ],
        (
            6 * rows * width * width + steps * slabs * HEADS * 4 * ROWS * ROWS * 256,
            rows * (width * 16 + HEADS * 512) + width * width * 6,
            steps * slabs * HEADS * ROWS * ROWS,
        ),
        aliases,
    )


def project_kernel(
    slabs, first, meta, windows, attended, rows_in, grads, vectors, *rest,
):
    pieces = rest[:4]
    middle_out, normed_out, branch_out, shrink_bias_out, full, staged, weight, sems = rest[4:]
    step = pl.program_id(0)

    @pl.when(step == 0)
    def _():
        wait_all(load_rows(meta, pieces, weight, sems, first))
        shrink_bias_out[...] = jnp.zeros_like(shrink_bias_out)

    width = full.shape[2]
    count = slabs * ROWS
    middle = (
        rows_in[...].reshape(count, width).astype(F32)
        + dot(attended[...].reshape(count, width), weight[...])
        + vectors[OUTPUT_BIAS : OUTPUT_BIAS + 1]
    )
    unit, _ = normalize(middle)
    middle_out[...] = middle.astype(BF16)
    normed = unit * vectors[SECOND_GAIN : SECOND_GAIN + 1] + vectors[SECOND_SHIFT : SECOND_SHIFT + 1]
    normed_out[...] = normed.astype(BF16)
    gather_quarters(step == 0, grads, staged, full, step * slabs, slabs)
    for slab in range(slabs):
        allowed = valid_rows(windows[meta[0], step * slabs + slab])
        branch = jnp.where(allowed, full[slab], 0.0)
        branch_out[slab * ROWS : (slab + 1) * ROWS, :] = branch.astype(BF16)
        shrink_bias_out[...] += jnp.sum(branch, axis=0, keepdims=True)


def project(meta, windows, attended, rows_in, grads, vectors, pieces):
    parts, rows_dev, slots, width = grads.shape
    slabs = group(slots)
    block = pl.BlockSpec((slabs, ROWS, width), lambda i, *_: (i, 0, 0))
    flat = pl.BlockSpec((slabs * ROWS, width), lambda i, *_: (i, 0))
    rows = slots * ROWS
    return call(
        functools.partial(project_kernel, slabs, 3 * width),
        "project",
        slots // slabs,
        (meta, windows),
        [(attended, block), (rows_in, block)]
        + [(item, whole(*item.shape)) for item in (grads, vectors)]
        + [(item, ANY) for item in pieces],
        [
            (like((rows, width), BF16), flat),
            (like((rows, width), BF16), flat),
            (like((rows, width), BF16), flat),
            (like((1, width), F32), whole(1, width)),
        ],
        [
            pltpu.VMEM((slabs, ROWS, width), F32),
            pltpu.VMEM((parts * width // LANES, rows_dev * slots, LANES), F32),
            pltpu.VMEM((width, width), BF16),
            pltpu.SemaphoreType.DMA((10,)),
        ],
        (2 * rows * width * width, rows * width * 14, 0),
    )


def gate_both(hidden):
    half = 0.5 * (1.0 + lax.erf(hidden * 0.7071067811865476))
    density = jnp.exp(hidden * hidden * -0.5) * 0.3989422804014327
    return hidden * half, half + hidden * density


def feed_kernel(number, first, unit, meta, normed, branch, vectors, *rest):
    pieces, rest = rest[:10], rest[10:]
    if not first:
        out_in, grad_in = rest[:2]
    out_acc, grad_acc, keep, send, bias_grad, expand, shrink, acc_e, acc_s, sems = rest[-10:]
    step = pl.program_id(0)
    last = pl.num_programs(0) - 1
    width, chunk = acc_e.shape
    blocks = chunk // unit

    @pl.when(step == 0)
    def _():
        pairs = []
        quarter, tall = expand.shape[1], shrink.shape[1]
        here = blocks * quarter + number * tall
        columns = pl.ds(number * unit, unit)
        for source, who in zip(pieces[:2], (0, 1)):
            places = pl.ds(4 * (meta[0] ^ who), 4)
            for block in range(blocks):
                pairs.append(
                    (
                        source.at[:, pl.ds(block * quarter, quarter), columns],
                        expand.at[places, :, pl.ds(block * unit, unit)],
                    )
                )
            pairs.append((source.at[:, pl.ds(here, tall), :], shrink.at[places]))
        for fetched, places in zip((pieces[2:6], pieces[6:10]), quarter_places(meta)):
            for source, place in zip(fetched, places):
                for block in range(blocks):
                    pairs.append(
                        (
                            source.at[pl.ds(block * quarter, quarter), columns],
                            expand.at[place, :, pl.ds(block * unit, unit)],
                        )
                    )
                pairs.append((source.at[pl.ds(here, tall), :], shrink.at[place]))
        copies = start_copies(pairs, sems)
        acc_e[...] = jnp.zeros_like(acc_e)
        acc_s[...] = jnp.zeros_like(acc_s)
        bias_grad[...] = jnp.zeros_like(bias_grad)
        wait_all(copies)

    rows = normed[...]
    grads = branch[...]
    bias = jnp.concatenate(
        [
            vectors[
                EXPAND_BIAS + block : EXPAND_BIAS + block + 1, number * unit : (number + 1) * unit
            ]
            for block in range(blocks)
        ],
        axis=1,
    )
    whole_expand = expand[...].reshape(width, chunk)
    whole_shrink = shrink[...].reshape(chunk, width)
    hidden = dot(rows, whole_expand) + bias
    d_active = dot_t(grads, whole_shrink)
    active, slope = gate_both(hidden)
    active = active.astype(BF16)
    back = (d_active * slope).astype(BF16)
    bias_grad[...] += jnp.sum(back.astype(F32), axis=0, keepdims=True)
    acc_s[...] += dot_rows(active, grads)
    acc_e[...] += dot_rows(rows, back)
    total_out = dot(active, whole_shrink)
    total_grad = dot_t(back, whole_expand)
    if first:
        out_acc[...] = total_out.astype(BF16)
        grad_acc[...] = total_grad.astype(BF16)
    else:
        out_acc[...] = (out_in[...].astype(F32) + total_out).astype(BF16)
        grad_acc[...] = (grad_in[...].astype(F32) + total_grad).astype(BF16)

    @pl.when(step == last)
    def _():
        height = width // 4
        third = height // 3
        for index in range(4):
            target = (send if index & 1 else keep).at[index >> 1]
            start = pl.multiple_of((meta[0] ^ index) * unit, 16)
            target[:unit, :] = acc_s[pl.ds(start, unit), :].astype(BF16)
            start = pl.multiple_of((meta[0] ^ index) * height, 16)
            target[unit : unit + height, :] = acc_e[pl.ds(start, height), :width].astype(BF16)
            for piece in range(3):
                here = pl.multiple_of(start + piece * third, 16)
                target[unit + height :, piece * unit : (piece + 1) * unit] = acc_e[
                    pl.ds(here, third), width:
                ].astype(BF16)


def feed(number, count, meta, normed, branch, vectors, pieces, kept):
    rows, width = normed.shape
    chunk = 4 * width // count
    unit = chunk // 4
    block_rows = 2 * ROWS
    block = pl.BlockSpec((block_rows, width), lambda i, *_: (i, 0))
    ins = [(normed, block), (branch, block), (vectors, whole(*vectors.shape))]
    ins += [(item, ANY) for item in pieces]
    aliases = {}
    if kept is not None:
        aliases = {len(ins) + n: n for n in range(2)}
        ins += [(item, block) for item in kept]
    payload = (2, unit + unit, width)
    return call(
        functools.partial(feed_kernel, number, kept is None, unit),
        "feed",
        rows // block_rows,
        (meta,),
        ins,
        [
            (like((rows, width), BF16), block),
            (like((rows, width), BF16), block),
            (like(payload, BF16), whole(*payload)),
            (like(payload, BF16), whole(*payload)),
            (like((1, chunk), F32), whole(1, chunk)),
        ],
        [
            pltpu.VMEM((16, width // 16, chunk), BF16),
            pltpu.VMEM((16, chunk // 16, width), BF16),
            pltpu.VMEM((width, chunk), F32),
            pltpu.VMEM((chunk, width), F32),
            pltpu.SemaphoreType.DMA((64,)),
        ],
        (12 * rows * width * chunk, rows * width * 12 + width * chunk * 8, 2 * rows * chunk),
        aliases,
    )


def middle_kernel(
    slabs, first, meta, windows, middle, out_acc, grad_acc, branch, attended, vectors,
    *rest,
):
    pieces = rest[:4]
    (
        result_out, d_middle_out, d_attended_out, keep, send, output_bias_grad, gain_grad,
        shift_grad, full, staged, weight, acc, sems,
    ) = rest[4:]
    step = pl.program_id(0)
    last = pl.num_programs(0) - 1

    @pl.when(step == 0)
    def _():
        copies = load_rows(meta, pieces, weight, sems, first)
        acc[...] = jnp.zeros_like(acc)
        output_bias_grad[...] = jnp.zeros_like(output_bias_grad)
        gain_grad[...] = jnp.zeros_like(gain_grad)
        shift_grad[...] = jnp.zeros_like(shift_grad)
        wait_all(copies)

    width = full.shape[2]
    count = slabs * ROWS
    rows = middle[...].astype(F32)
    result = rows + out_acc[...].astype(F32) + vectors[SHRINK_BIAS : SHRINK_BIAS + 1]
    full[...] = result.reshape(slabs, ROWS, width)
    scatter_quarters(step == last, full, staged, result_out, step * slabs, slabs)
    unit, scale = normalize(rows)
    grad = grad_acc[...].astype(F32)
    gain_grad[...] += jnp.sum(grad * unit, axis=0, keepdims=True)
    shift_grad[...] += jnp.sum(grad, axis=0, keepdims=True)
    d_middle = branch[...].astype(F32) + normalize_back(
        unit, scale, grad, vectors[SECOND_GAIN : SECOND_GAIN + 1]
    )
    d_output = d_middle.astype(BF16)
    d_middle_out[...] = d_output
    output_bias_grad[...] += jnp.sum(d_output.astype(F32), axis=0, keepdims=True)
    acc[...] += dot_rows(attended[...].reshape(count, width), d_output)
    d_attended = dot_t(d_output, weight[...]).reshape(slabs, ROWS, width)
    for slab in range(slabs):
        allowed = valid_rows(windows[meta[0], step * slabs + slab])
        d_attended_out[slab] = jnp.where(allowed, d_attended[slab], 0.0).astype(BF16)

    @pl.when(step == last)
    def _():
        write_owned(acc, meta, keep, send, 1)


def middle_back(meta, windows, rows_dev, middle, out_acc, grad_acc, branch, attended, vectors, pieces):
    slots, _, width = attended.shape
    parts = WROWS // rows_dev
    slabs = group(slots)
    block = pl.BlockSpec((slabs, ROWS, width), lambda i, *_: (i, 0, 0))
    flat = pl.BlockSpec((slabs * ROWS, width), lambda i, *_: (i, 0))
    rows = slots * ROWS
    vec = (like((1, width), F32), whole(1, width))
    payload = (2, width // 4, width)
    quarter = (parts, rows_dev, slots, width)
    return call(
        functools.partial(middle_kernel, slabs, 3 * width),
        "middle",
        slots // slabs,
        (meta, windows),
        [
            (middle, flat), (out_acc, flat), (grad_acc, flat), (branch, flat), (attended, block),
            (vectors, whole(*vectors.shape)),
        ]
        + [(item, ANY) for item in pieces],
        [
            (like(quarter, BF16), whole(*quarter)),
            (like((rows, width), BF16), flat),
            (like((slots, ROWS, width), BF16), block),
            (like(payload, BF16), whole(*payload)),
            (like(payload, BF16), whole(*payload)),
            vec,
            vec,
            vec,
        ],
        [
            pltpu.VMEM((slabs, ROWS, width), F32),
            pltpu.VMEM((parts * width // LANES, rows_dev * slots, LANES), F32),
            pltpu.VMEM((width, width), BF16),
            pltpu.VMEM((width, width), F32),
            pltpu.SemaphoreType.DMA((10,)),
        ],
        (4 * rows * width * width, rows * width * 18, 0),
    )


def attend_back_kernel(
    slabs, across, meta, normed, queries_in, keys_in, values_in, probs_in, d_mixed_in, mixed_in,
    height, width_table, places, blocks, selectors, sums,
    d_queries, d_keys, d_values, keep, send, bias_grad, table_out, grads, acc, tables, table_grad,
):
    step = pl.program_id(0)
    last = pl.num_programs(0) - 1
    wide4 = QUAD * HD

    @pl.when(step == 0)
    def _():
        acc[...] = jnp.zeros_like(acc)
        bias_grad[...] = jnp.zeros_like(bias_grad)
        table_grad[...] = jnp.zeros_like(table_grad)
        tables[...] = build_tables(height, width_table, places, blocks)

    lane = lax.broadcasted_iota(jnp.int32, (ROWS, LANES), 1)
    within = lane & (SEG - 1)
    upper = lane >= HD
    zero = jnp.zeros((ROWS, LANES), BF16)

    sides = (jnp.logical_not(upper), upper)
    halves_of = lambda items, head: jnp.where(
        sides[head & 1], items[:, (head >> 1) * LANES : ((head >> 1) + 1) * LANES], zero
    )
    minus = [
        jnp.where((lane == 2 * head) | (lane == 2 * head + 1), -1.0, 0.0).astype(BF16)
        for head in range(QUAD)
    ]
    every = [(slab, head) for slab in range(slabs) for head in range(QUAD)]
    lefts = []
    for slab in range(slabs):
        d_mixed = d_mixed_in[slab]
        product = d_mixed.astype(F32) * mixed_in[slab].astype(F32)
        product_high = product.astype(BF16)
        product_low = (product - product_high.astype(F32)).astype(BF16)
        inner = dot(product_high, sums[...]) + dot(product_low, sums[...])
        inner_high = inner.astype(BF16)
        inner_low = (inner - inner_high.astype(F32)).astype(BF16)
        inner = jnp.where((lane & 1) == 0, inner_high, inner_low)
        lefts.append(
            [
                jnp.concatenate([d_mixed[:, pair * LANES : (pair + 1) * LANES], inner], axis=1)
                for pair in range(QUAD // 2)
            ]
        )
    d_probs = [
        dot_t(
            lefts[slab][head >> 1],
            jnp.concatenate([halves_of(values_in[slab], head), minus[head]], axis=1),
        )
        for slab, head in every
    ]
    parts_v = [
        dot_rows(probs_in[slab, head], halves_of(d_mixed_in[slab], head)) for slab, head in every
    ]
    d_scores = [
        (probs_in[slab, head].astype(F32) * item).astype(BF16)
        for (slab, head), item in zip(every, d_probs)
    ]
    backs = [
        dot(
            item,
            jnp.concatenate([halves_of(keys_in[slab], head), selectors[head]], axis=1),
        )
        for (slab, head), item in zip(every, d_scores)
    ]
    parts_k = [
        dot_rows(item, halves_of(queries_in[slab], head))
        for (slab, head), item in zip(every, d_scores)
    ]
    scale = HD**-0.5
    joined = lambda items: jnp.concatenate(
        [items[2 * pair] + items[2 * pair + 1] for pair in range(QUAD // 2)], axis=1
    )
    for slab in range(slabs):
        mine = slice(slab * QUAD, (slab + 1) * QUAD)
        d_relative = backs[slab * QUAD][:, LANES:]
        for head in range(1, QUAD):
            d_relative = d_relative + backs[slab * QUAD + head][:, LANES:]
        high = roll_rows(jnp.where(within < WIN, d_relative, 0.0), False)
        wide = roll_rows(jnp.where((within >= 16) & (within < 16 + WIN), d_relative, 0.0), True)
        d_terms = jnp.concatenate([high, wide], axis=1).astype(BF16)
        dq = joined([item[:, :LANES] for item in backs[mine]]) * scale
        dq = (dq + dot_t(d_terms, tables[...])).astype(BF16)
        table_grad[...] += dot_rows(queries_in[slab], d_terms)
        dk = (joined(parts_k[mine]) * scale).astype(BF16)
        dv = joined(parts_v[mine]).astype(BF16)
        d_queries[slab] = dq
        d_keys[slab] = dk
        d_values[slab] = dv
        grads[slab] = jnp.concatenate([dq, dk, dv], axis=1)

    width = normed.shape[2]
    both = grads[...].reshape(slabs * ROWS, 3 * wide4)
    bias_grad[...] += jnp.sum(both.astype(F32), axis=0, keepdims=True)
    acc[...] += dot_rows(normed[...].reshape(slabs * ROWS, width), both)

    @pl.when(step == last)
    def _():
        write_owned(acc, meta, keep, send, across)
        masked = table_grad[...] * blocks[...].astype(F32)
        folded = masked[:HD]
        for head in range(1, QUAD):
            folded = folded + masked[head * HD : (head + 1) * HD]
        high = folded.astype(BF16)
        low = (folded - high.astype(F32)).astype(BF16)
        for which in range(2):
            table_out[:, which * HD : (which + 1) * HD] = dot_t(places[which], high) + dot_t(
                places[which], low
            )


def attend_back(quad, across, meta, normed, triple, probs, d_mixed, mixed, tables, selectors, sums):
    slots, _, width = normed.shape
    slabs = group(slots)
    wide4 = QUAD * HD
    quads = HEADS // QUAD
    column = lambda where: pl.BlockSpec((slabs, ROWS, wide4), lambda i, *_: (i, 0, where))
    narrow = (
        like((slots, ROWS, wide4), BF16),
        pl.BlockSpec((slabs, ROWS, wide4), lambda i, *_: (i, 0, 0)),
    )
    rows = slots * ROWS
    payload = (2, width // 4, 3 * wide4)
    return call(
        functools.partial(attend_back_kernel, slabs, across),
        "attend_back",
        slots // slabs,
        (meta,),
        [
            (normed, pl.BlockSpec((slabs, ROWS, width), lambda i, *_: (i, 0, 0))),
            (triple, column(quad)),
            (triple, column(quads + quad)),
            (triple, column(2 * quads + quad)),
            (probs, pl.BlockSpec((slabs, QUAD, ROWS, ROWS), lambda i, *_: (i, quad, 0, 0))),
            (d_mixed, column(quad)),
            (mixed, column(quad)),
        ]
        + [(item, whole(*item.shape)) for item in (*tables, selectors, sums)],
        [
            narrow,
            narrow,
            narrow,
            (like(payload, BF16), whole(*payload)),
            (like(payload, BF16), whole(*payload)),
            (like((1, 3 * wide4), F32), whole(1, 3 * wide4)),
            (like((REL, 2 * HD), F32), whole(REL, 2 * HD)),
        ],
        [
            pltpu.VMEM((slabs, ROWS, 3 * wide4), BF16),
            pltpu.VMEM((width, 3 * wide4), F32),
            pltpu.VMEM((2 * LANES, 2 * LANES), BF16),
            pltpu.VMEM((2 * LANES, 2 * LANES), F32),
        ],
        (
            2 * rows * width * 3 * wide4 + slots * QUAD * 8 * ROWS * ROWS * 256,
            rows * (width * 2 + wide4 * 16 + QUAD * 512),
            0,
        ),
    )


def first_kernel(slabs, meta, rows_in, d_middle, vectors, *rest):
    grads, pieces = rest[:9], rest[9:13]
    tokens_out, gain_grad, shift_grad, full, staged, weight, sems = rest[13:]
    step = pl.program_id(0)
    last = pl.num_programs(0) - 1

    @pl.when(step == 0)
    def _():
        copies = load_rows(meta, pieces, weight, sems)
        gain_grad[...] = jnp.zeros_like(gain_grad)
        shift_grad[...] = jnp.zeros_like(shift_grad)
        wait_all(copies)

    width = full.shape[2]
    count = slabs * ROWS
    wide4 = QUAD * HD
    both = jnp.concatenate([grad[...].reshape(count, wide4) for grad in grads], axis=1)
    total = dot_t(both, weight[...])
    unit, scale = normalize(rows_in[...].reshape(count, width).astype(F32))
    gain_grad[...] += jnp.sum(total * unit, axis=0, keepdims=True)
    shift_grad[...] += jnp.sum(total, axis=0, keepdims=True)
    back = normalize_back(unit, scale, total, vectors[FIRST_GAIN : FIRST_GAIN + 1])
    full[...] = (d_middle[...].astype(F32) + back).reshape(slabs, ROWS, width)
    scatter_quarters(step == last, full, staged, tokens_out, step * slabs, slabs)


def first_back(before, steps, meta, rows_dev, rows_in, d_middle, vectors, grads, pieces):
    slots, _, width = rows_in.shape
    parts = WROWS // rows_dev
    slabs = group(slots)
    wide4 = QUAD * HD
    block = pl.BlockSpec((slabs, ROWS, width), lambda i, *_: (i + before, 0, 0))
    flat = pl.BlockSpec((slabs * ROWS, width), lambda i, *_: (i + before, 0))
    narrow = pl.BlockSpec((slabs, ROWS, wide4), lambda i, *_: (i + before, 0, 0))
    rows = steps * slabs * ROWS
    quarter = (parts, rows_dev, steps * slabs, width)
    return call(
        functools.partial(first_kernel, slabs),
        "first_back",
        steps,
        (meta,),
        [(rows_in, block), (d_middle, flat), (vectors, whole(*vectors.shape))]
        + [(item, narrow) for item in grads]
        + [(item, ANY) for item in pieces],
        [(like(quarter, BF16), whole(*quarter))] + [(like((1, width), F32), whole(1, width))] * 2,
        [
            pltpu.VMEM((slabs, ROWS, width), F32),
            pltpu.VMEM((parts * width // LANES, rows_dev * steps * slabs, LANES), F32),
            pltpu.VMEM((width, 3 * width), BF16),
            pltpu.SemaphoreType.DMA((10,)),
        ],
        (6 * rows * width * width, rows * width * 14, 0),
    )


def join_halves(meta, items, staged):
    upper = meta[1] > 0
    for number, both in enumerate(staged):
        mine, other = items[2 * number], items[2 * number + 1]
        half = mine.shape[0]

        @pl.when(upper)
        def _():
            both[:half] = other[...]
            both[half:] = mine[...]

        @pl.when(jnp.logical_not(upper))
        def _():
            both[:half] = mine[...]
            both[half:] = other[...]


def finish_feed_kernel(unit, pairs, meta, *refs):
    items, (expand_out, shrink_out, output_out), staged = (
        refs[: 2 * pairs], refs[2 * pairs : 2 * pairs + 3], refs[2 * pairs + 3 :]
    )
    join_halves(meta, items, staged)
    output_out[...] = staged[-1][2 * unit :, :].astype(F32)
    shard, width = expand_out.shape[0], shrink_out.shape[1]
    third = shard // 3
    parts = width // shard
    for number, both in enumerate(staged):
        here = number * unit
        shrink_out[here : here + unit, :] = both[:unit, :].astype(F32)
        for block in range(parts - 1):
            start = block * width + here
            expand_out[:, start : start + unit] = both[
                unit : unit + shard, block * unit : (block + 1) * unit
            ].astype(F32)
        start = (parts - 1) * width + here
        for piece in range(3):
            expand_out[piece * third : (piece + 1) * third, start : start + unit] = both[
                unit + shard : 2 * unit, piece * unit : (piece + 1) * unit
            ].astype(F32)


def finish_rest_kernel(pairs, meta, *refs):
    items, small, refs = refs[: 2 * pairs], refs[2 * pairs], refs[2 * pairs + 1 :]
    triple_out, refs = refs[0], refs[1:]
    vectors, tables, staged = refs[:8], refs[8:10], refs[10:]
    join_halves(meta, items, staged)
    shard, width = triple_out.shape[0], small.shape[1]
    wide4 = QUAD * HD
    quads = [both[n : n + shard, :] for both in staged for n in range(0, both.shape[0], shard)]
    for quad, values in enumerate(quads):
        for part in range(3):
            start = part * width + quad * wide4
            triple_out[:, start : start + wide4] = values[
                :, part * wide4 : (part + 1) * wide4
            ].astype(F32)
    row = 0
    for item in vectors:
        for start in range(0, item.shape[0], width):
            item[pl.ds(start, width)] = small[row : row + 1, :].reshape(width)
            row += 1
    for which, item in enumerate(tables):
        for piece in range(3):
            start = piece * LANES + which * HD
            item[9 * piece : 9 * piece + 9, :] = small[TABLES : TABLES + 9, start : start + HD]


def finish(kernel, name, meta, shares, others, outs):
    items = [item for pair in shares for item in pair]
    return call(
        kernel,
        name,
        1,
        (meta,),
        [(item, whole(*item.shape)) for item in (*items, *others)],
        [(like(item.shape, F32), whole(*item.shape)) for item in outs],
        [pltpu.VMEM((2 * mine.shape[0], mine.shape[1]), BF16) for mine, _ in shares],
        (0, sum(6 * item.size for item in items), 0),
    )


def swap(values, axis, bits):
    count = lax.axis_size(axis)
    return lax.ppermute(values, axis, [(n, n ^ bits) for n in range(count)])


def swap_diagonal(values):
    across = lax.axis_size("seq")
    count = lax.axis_size("dp") * across
    perm = [(n, (n // across ^ 1) * across + (n % across ^ 1)) for n in range(count)]
    return lax.ppermute(values, ("dp", "seq"), perm)


def spread(far):
    return far, swap(far, "dp", 1), swap(far, "seq", 1), swap_diagonal(far)


def exchange_windows(values):
    return lax.all_to_all(values, "tensor", split_axis=0, concat_axis=0, tiled=True)


def after(values, *others):
    return lax.optimization_barrier((values, *others))[0]


def far_quarter(packed):
    which = 2 * (lax.axis_index("dp") & 1) + (lax.axis_index("seq") & 1)
    return lax.dynamic_index_in_dim(packed, which, axis=0, keepdims=False)


def add(*items):
    total = items[0].astype(F32)
    for item in items[1:]:
        total = total + item.astype(F32)
    return total.astype(BF16)


def halves(axis):
    out, bit = [], 1
    while bit < lax.axis_size(axis):
        out.append(bit)
        bit *= 2
    return out


def reduce_stages(payloads, plan, hook=None):
    bits_of = {"c": 1, "y": 2}
    totals = []
    while True:
        keep, send, more = payloads.pop(0)
        (far,) = yield [(send, "tensor", bits_of[plan[0]])]
        totals.append(add(keep, far))
        if not more:
            break
    total = totals[0] if len(totals) == 1 else jnp.concatenate(totals, axis=1)
    spot = lax.axis_index("dp")
    place = lax.axis_index("seq")

    def split(values, upper):
        size = values.shape[-2] // 2
        low, high = values[..., :size, :], values[..., size:, :]
        return jnp.where(upper, high, low), jnp.where(upper, low, high)

    def join(mine, far, upper):
        return jnp.concatenate([jnp.where(upper, far, mine), jnp.where(upper, mine, far)], axis=0)

    for letter in plan[1:]:
        if letter == "w":
            total = hook(total)
        elif letter in bits_of:
            (far,) = yield [(total[1], "tensor", bits_of[letter])]
            total = add(total[0], far)
        elif letter == "x":
            for bit in halves("dp"):
                near, far = split(total, (spot & bit) > 0)
                (far,) = yield [(far, "dp", bit)]
                total = add(near, far)
        else:
            if letter == "s":
                near, far = split(total, (place & 1) > 0)
                (far,) = yield [(far, "seq", 1)]
                total = add(near, far)
            for bit in halves("seq"):
                if letter == "s" and bit == 1:
                    continue
                (far,) = yield [(total, "seq", bit)]
                total = add(total, far)
            if letter == "s":
                (far,) = yield [(total, "seq", 1)]
                total = join(total, far, (place & 1) > 0)
    for bit in reversed(halves("dp")):
        (far,) = yield [(total, "dp", bit)]
        if bit > 1:
            total = join(total, far, (spot & bit) > 0)
    return total, far


def sum_stages(values, hook):
    steps = [(axis, bit) for axis in ("tensor", "dp", "seq") for bit in halves(axis)]
    steps = [("tensor", 2)] + [item for item in steps if item != ("tensor", 2)]
    for number, (axis, bit) in enumerate(steps):
        (far,) = yield [(values, axis, bit)]
        if number == len(steps) - 1:
            far = hook(far)
        values = values + far
    return (values,)


class Exchanges:
    def __init__(self):
        self.running = []
        self.done = {}

    def begin(self, name, stages):
        self.running.append([name, stages, None])

    def step(self, names, token, meta, *extra):
        asked, ended = [], []
        chosen = [entry for entry in self.running if names is None or entry[0] in names]
        arrived = [item for entry in chosen for item in (entry[2] or ())]
        if token is not None and arrived:
            token, *arrived = lax.optimization_barrier((token, *arrived))
        arrived = iter(arrived)
        for entry in chosen:
            name, stages, waiting = entry
            mine = None if waiting is None else [next(arrived) for _ in waiting]
            try:
                asked.append((entry, stages.send(mine)))
            except StopIteration as stop:
                ended.append((name, stop.value))
                self.running.remove(entry)
        values = [item[0] for _, wanted in asked for item in wanted]
        finished = [item for _, pair in ended for item in pair]
        if meta is not None:
            count = len(values)
            meta, *rest = lax.optimization_barrier((meta, *values, *finished, *extra))
            values = rest[:count]
            finished = rest[count : count + len(finished)]
            extra = rest[count + len(finished) :]
        values, finished = iter(values), iter(finished)
        for entry, wanted in asked:
            entry[2] = [swap(next(values), axis, bits) for _, axis, bits in wanted]
        for name, pair in ended:
            self.done[name] = tuple(next(finished) for _ in pair)
        return (token, meta, *extra)

    def finish(self, names):
        while any(entry[0] in names for entry in self.running):
            self.step(names, None, None)


def local(
    tokens,
    out_grad,
    slot_window,
    first_gain,
    first_shift,
    triple_weight,
    triple_bias,
    height_table,
    width_table,
    output_weight,
    output_bias,
    second_gain,
    second_shift,
    expand_weight,
    expand_bias,
    shrink_weight,
    shrink_bias,
):
    micros, images, slots, rows_dev, width = tokens.shape
    parts = lax.axis_size("tensor")
    mine = lax.axis_index("tensor")
    shard = width // parts
    chunks = 3
    unit = width // chunks
    bit = lax.axis_index("dp") & 1
    quarter = 2 * bit + (lax.axis_index("seq") & 1)
    meta = jnp.where(
        jnp.arange(3) == 0, mine, jnp.where(jnp.arange(3) == 1, bit, quarter)
    ).astype(jnp.int32)

    by_image = lambda values: jnp.swapaxes(values, 2, 3).reshape(parts, rows_dev, slots, width)
    to_image = lambda values: jnp.swapaxes(
        values.reshape(micros, images, rows_dev, slots, width), 2, 3
    )
    windows = slot_window.reshape(parts, slots)

    far = jnp.concatenate(
        [
            far_quarter(triple_weight.reshape(4, shard // 4, -1)),
            far_quarter(output_weight.reshape(4, shard // 4, -1)),
        ],
        axis=1,
    )
    far = swap(far, "tensor", 2)
    near_triple = swap(triple_weight, "tensor", 1)
    near_output = swap(output_weight, "tensor", 1)
    vectors, packed_rest = prepare(
        chunks,
        (
            first_gain, first_shift, output_bias, second_gain, second_shift, shrink_bias,
            triple_bias, expand_bias,
        ),
        (expand_weight, shrink_weight),
    )
    sums = np.zeros((QUAD * HD, LANES), np.float32)
    for head in range(QUAD):
        sums[head * HD : (head + 1) * HD, 2 * head : 2 * head + 2] = 1.0
    sums = jnp.asarray(sums, BF16)
    ahead = (height_table, width_table, table_places(False), head_blocks(False))
    behind = (height_table, width_table, table_places(True), head_blocks(True))
    first_rest = far_quarter(packed_rest)
    far, vectors, packed_rest, first_rest, meta, own_tokens, near_triple, near_output = (
        lax.optimization_barrier(
            (
                far, vectors, packed_rest, first_rest, meta, by_image(tokens), near_triple,
                near_output,
            )
        )
    )
    rows_in = exchange_windows(own_tokens)
    fetched = jnp.stack(spread(far))
    crossed = swap(fetched, "tensor", 1)

    packed, first_rest, rows_in, fetched, crossed = lax.optimization_barrier(
        (packed_rest, first_rest, rows_in, fetched, crossed)
    )
    triple_pieces = (triple_weight, near_triple, fetched, crossed)
    output_pieces = (output_weight, near_output, fetched, crossed)
    far = swap(first_rest, "tensor", 2)
    near = swap(packed, "tensor", 1)
    steps = slots // group(slots)
    early = max(1, steps // 4)
    selectors = key_selectors(False)
    kept = attend(
        0, early, meta, windows, rows_in, vectors, ahead, selectors, triple_pieces, None
    )
    kept = list(kept)
    kept[4], far, own_grads = lax.optimization_barrier((kept[4], far, by_image(out_grad)))
    meta, far, near, own_grads = lax.optimization_barrier((meta, far, near, own_grads))
    grads_in = exchange_windows(own_grads)
    fetched = spread(far)
    crossed = (swap(far, "tensor", 1),)
    if early < steps:
        kept = attend(
            early, steps - early, meta, windows, rows_in, vectors, ahead, selectors,
            triple_pieces, kept,
        )
    full_rows, normed, triple, probs, attended = kept
    attended, *others = lax.optimization_barrier((attended, *fetched[1:]))
    meta, *others = lax.optimization_barrier((meta, *others))
    crossed += tuple(swap(item, "tensor", 1) for item in others)
    middle_stage = project(
        meta, windows, attended, full_rows, grads_in, vectors, output_pieces
    )
    shrink_bias_grad = middle_stage[3]
    rest_pieces = (packed, near, far, *others, *crossed)
    middle, normed2, branch = middle_stage[:3]
    exchanges = Exchanges()
    kept = None
    expand_bias_grads = []
    for number in range(chunks):
        *kept, keep, send, bias_grad = feed(
            number, chunks, meta, normed2, branch, vectors, rest_pieces, kept
        )
        plan = ("cyxz", "cyxz", "cxys")[number]
        payloads = [(keep, send, number == chunks - 1)]
        exchanges.begin(("feed", number), reduce_stages(payloads, plan))
        bias_grad, meta = exchanges.step(None, bias_grad, meta)
        expand_bias_grads.append(bias_grad)

    result, d_middle, d_attended, keep, send, output_bias_grad, gain2_grad, shift2_grad = (
        middle_back(
            meta, windows, rows_dev, middle, *kept, branch, attended, vectors, output_pieces
        )
    )
    payloads.append((keep, send, False))
    output_bias_grad, meta = exchanges.step(None, output_bias_grad, meta)
    result = exchange_windows(result)

    quad_grads, triple_bias_grads, table_grads = [], [], []
    for quad in range(HEADS // QUAD):
        dq, dk, dv, keep, send, bias_grad, table_grad = attend_back(
            quad, 1, meta, normed, triple, probs, d_attended, attended, behind, key_selectors(True), sums
        )
        if quad == 0:
            payloads = [(keep, send, True)]
            exchanges.begin(("rest", 0), reduce_stages(payloads, "cyxs"))
        elif quad == 1:
            payloads.append((keep, send, False))
        else:
            hook = lambda total: after(total, *feed_gradients)
            exchanges.begin(("rest", 1), reduce_stages([(keep, send, False)], "cyxz", hook))
        if quad == 1:
            bias_grad, meta, result = exchanges.step(None, bias_grad, meta, result)
        else:
            bias_grad, meta = exchanges.step(None, bias_grad, meta)
        quad_grads.append((dq, dk, dv))
        triple_bias_grads.append(bias_grad)
        table_grads.append(table_grad)
    wide4 = QUAD * HD
    grads9 = [quad_grads[quad][part] for part in range(3) for quad in range(HEADS // QUAD)]
    token_grad, gain1_grad, shift1_grad = first_back(
        0, steps, meta, rows_dev, full_rows, d_middle, vectors, grads9, triple_pieces
    )
    result = to_image(result)
    gain1_grad, _ = exchanges.step(None, gain1_grad, None)
    small = collect(
        (gain1_grad, shift1_grad, output_bias_grad, gain2_grad, shift2_grad, shrink_bias_grad),
        triple_bias_grads,
        expand_bias_grads,
        table_grads,
    )
    hook = lambda far: after(far, *feed_gradients)
    exchanges.begin("small", sum_stages(small, hook))
    exchanges.step(["small"], None, None)
    first_far = exchanges.running[-1][2][0]
    tokens_gradient = to_image(exchange_windows(after(token_grad, first_far)))
    names = [("feed", number) for number in range(chunks)]
    exchanges.finish(names)
    shares = [exchanges.done[name] for name in names]
    feed_gradients = finish(
        functools.partial(finish_feed_kernel, unit, chunks),
        "finish_feed",
        meta,
        shares,
        (),
        (expand_weight, shrink_weight, output_weight),
    )
    expand_gradient, shrink_gradient, output_gradient = feed_gradients
    exchanges.finish([("rest", number) for number in range(2)] + ["small"])
    shares = [exchanges.done["rest", number] for number in range(2)]
    triple_gradient, *outs, high, wide = finish(
        functools.partial(finish_rest_kernel, len(shares)),
        "finish_rest",
        meta,
        shares,
        exchanges.done["small"],
        (
            triple_weight, first_gain, first_shift, output_bias, second_gain, second_shift,
            shrink_bias, triple_bias, expand_bias, height_table, width_table,
        ),
    )
    return (
        result,
        tokens_gradient,
        outs[0],
        outs[1],
        triple_gradient,
        outs[6],
        high,
        wide,
        output_gradient,
        outs[2],
        outs[3],
        outs[4],
        expand_gradient,
        outs[7],
        shrink_gradient,
        outs[5],
    )


def solution(mesh):
    split = P(None, "dp", "seq", "tensor", None)
    rows = P("tensor", None)
    return jax.shard_map(
        local,
        mesh=mesh,
        in_specs=(
            split, split, P(None, "dp", "seq"), P(), P(), rows, P(), P(), P(), rows, P(), P(), P(),
            rows, P(), rows, P(),
        ),
        out_specs=(
            split, split, P(), P(), rows, P(), P(), P(), rows, P(), P(), P(), rows, P(), rows, P(),
        ),
        check_vma=False,
    )
```
